32 devices in a mesh: dp: 8 (over y, x, core), fsdp: 4 (over z).
Axes of the slice: x: 2, y: 2, z: 4, core: 2. Of those that a mesh axis runs over, the one named last changes fastest.
Arguments:
- state: bfloat16 [3, 8192, 512], P(None, ('dp', 'fsdp')), may hold values from -6 to 6
- segment: int32 [3, 8192], P(None, 'dp'), may hold values from 0 to 12, as said below
- parent: int32 [3, 8, 13], P(None, 'dp'), may hold values from 0 to 11, as said below
- halting: float32 [3, 8192], P(None, ('dp', 'fsdp')), may hold values from 0 to 1
- ponder: float32 [3, 8192], P(None, ('dp', 'fsdp')), may hold values from 1 to 4
- cot_state: bfloat16 [3, 8192, 512], P(None, ('dp', 'fsdp')), may hold values from -6 to 6
- cot_halt: float32 [3, 8192], P(None, ('dp', 'fsdp')), may hold values from -12 to 12
- w_query: bfloat16 [512, 512], P(('dp', 'fsdp')), may hold values from -0.25 to 0.25
- w_key: bfloat16 [512, 512], P(('dp', 'fsdp')), may hold values from -0.25 to 0.25
- w_value: bfloat16 [512, 512], P(('dp', 'fsdp')), may hold values from -0.25 to 0.25
- w_out: bfloat16 [512, 512], P(('dp', 'fsdp')), may hold values from -1 to 1
- w_up: bfloat16 [512, 2048], P(('dp', 'fsdp')), may hold values from -0.25 to 0.25
- b_up: bfloat16 [2048], P(('dp', 'fsdp')), may hold values from -3 to 3
- w_down: bfloat16 [2048, 512], P(('dp', 'fsdp')), may hold values from -0.125 to 0.125
- b_down: bfloat16 [512], P(('dp', 'fsdp')), may hold values from -3 to 3
- gain_one: bfloat16 [512], P(('dp', 'fsdp')), may hold values from 0.5 to 1.5
- bias_one: bfloat16 [512], P(('dp', 'fsdp')), may hold values from -3 to 3
- gain_two: bfloat16 [512], P(('dp', 'fsdp')), may hold values from 0.5 to 1.5
- bias_two: bfloat16 [512], P(('dp', 'fsdp')), may hold values from -3 to 3
- w_halt: bfloat16 [512], P(('dp', 'fsdp')), may hold values from -0.25 to 0.25
Outputs:
- new_state: bfloat16 [3, 8192, 512], P(None, ('dp', 'fsdp'))
- new_halting: float32 [3, 8192], P(None, ('dp', 'fsdp'))
- new_ponder: float32 [3, 8192], P(None, ('dp', 'fsdp'))
- grad_state: float32 [3, 8192, 512], P(None, ('dp', 'fsdp'))
- grad_w_query: float32 [512, 512], P(('dp', 'fsdp'))
- grad_w_key: float32 [512, 512], P(('dp', 'fsdp'))
- grad_w_value: float32 [512, 512], P(('dp', 'fsdp'))
- grad_w_out: float32 [512, 512], P(('dp', 'fsdp'))
- grad_w_up: float32 [512, 2048], P(('dp', 'fsdp'))
- grad_b_up: float32 [2048], P(('dp', 'fsdp'))
- grad_w_down: float32 [2048, 512], P(('dp', 'fsdp'))
- grad_b_down: float32 [512], P(('dp', 'fsdp'))
- grad_gain_one: float32 [512], P(('dp', 'fsdp'))
- grad_bias_one: float32 [512], P(('dp', 'fsdp'))
- grad_gain_two: float32 [512], P(('dp', 'fsdp'))
- grad_bias_two: float32 [512], P(('dp', 'fsdp'))
- grad_w_halt: float32 [512], P(('dp', 'fsdp'))
The draws below stay inside these ranges and needn't reach their ends.
Inputs may be any that keep to these rules, and one draw needn't show every extreme that they name: Within each tree of 1024 tokens the segment ids never fall, the first token has segment 0, the last has 12, and segment 0 covers at least the first 256 tokens. parent[m, t, 0] is 0 and parent[m, t, k] lies in 0 to k - 1: segment k of tree t hangs under segment parent[m, t, k].
All inputs are finite; a program needn't handle non-finite values.
Results may differ from the reference program's by a relative error of at most 0.018.
Values may be sent and summed in bfloat16 or wider, within the bound.
A program may use at most 128 MiB of HBM per device.

```python
import math
import jax
import jax.numpy as jnp
from jax import lax

D = 512
HEADS = 8
FF = 2048
MICRO = 3
SEGS = 13
TREE = 1024
TOKENS = 8192
N_DP = 8


def draw_segment(key, part):
    tree_count = MICRO * N_DP
    key_trunk, key_cut = jax.random.split(key)
    trunk_len = jax.random.randint(key_trunk, (tree_count, 1), TREE // 4, TREE // 2 + 1, dtype=jnp.int32)
    cut_points = jax.random.randint(key_cut, (tree_count, SEGS - 1), trunk_len, TREE, dtype=jnp.int32)
    places = jnp.arange(TREE, dtype=jnp.int32)
    labels = jnp.sum((places[None, :, None] >= cut_points[:, None, :]).astype(jnp.int32), axis=2)
    return labels.reshape(MICRO, TREE * N_DP).astype(jnp.int32)


def draw_parent(key, part):
    limits = jnp.maximum(jnp.arange(SEGS, dtype=jnp.int32), 1)
    drawn = jax.random.randint(key, (MICRO, N_DP, SEGS), 0, limits, dtype=jnp.int32).astype(jnp.int32)
    return drawn.at[:, 0, SEGS - 1].set(SEGS - 2).astype(jnp.int32)


def levels(stream_key, extent, cuts, smallest, largest):
    gain = 1.0
    for axis_at, blocks in cuts:
        heights = jax.random.uniform(jax.random.fold_in(jax.random.fold_in(stream_key, 6), axis_at), (blocks,), jnp.float32, smallest / len(cuts), largest / len(cuts))
        gain = gain * jnp.repeat(jnp.exp(heights), extent[axis_at] // blocks).reshape((-1,) + (1,) * (len(extent) - 1 - axis_at))
    return gain


def bell_draw(stream_key, dims, width, limit, cuts=(), held_as=jnp.bfloat16):
    values = width * jax.random.normal(stream_key, dims, jnp.float32)
    if cuts:
        values = values * levels(stream_key, dims, cuts, -0.22, 0.18)
    return jnp.clip(values, -limit, limit).astype(held_as)


def setup_inputs(seed: int = 0) -> dict:
    streams_of = jax.random.split(jax.random.key(seed), 21)
    state = bell_draw(streams_of[0], (MICRO, TOKENS, D), 1.0, 6.0, ((1, 32),))
    segment = draw_segment(jax.random.fold_in(streams_of[20], 71), 0)
    parent = draw_parent(jax.random.fold_in(streams_of[20], 71), 0)
    halting = jnp.clip(1.0 * jax.random.uniform(streams_of[3], (MICRO, TOKENS), jnp.float32) ** levels(streams_of[3], (MICRO, TOKENS), ((1, 32),), -0.2, 0.2), 0.0, 1.0)
    ponder = jnp.clip(1.0 + 3.0 * jax.random.uniform(streams_of[4], (MICRO, TOKENS), jnp.float32) ** levels(streams_of[4], (MICRO, TOKENS), ((1, 32),), -0.2, 0.2), 1.0, 4.0)
    cot_state = bell_draw(streams_of[5], (MICRO, TOKENS, D), 1.0, 6.0, ((1, 32),))
    cot_halt = bell_draw(streams_of[6], (MICRO, TOKENS), 2.0, 12.0, ((1, 32),), jnp.float32)
    w_query = bell_draw(streams_of[7], (D, D), D ** -0.5, 0.25, ((0, 32),))
    w_key = bell_draw(streams_of[8], (D, D), D ** -0.5, 0.25, ((0, 32),))
    w_value = bell_draw(streams_of[9], (D, D), D ** -0.5, 0.25, ((0, 32),))
    w_out = bell_draw(streams_of[10], (D, D), (D // 16) ** -0.5, 1.0, ((0, 32),))
    w_up = bell_draw(streams_of[11], (D, FF), D ** -0.5, 0.25, ((0, 32),))
    b_up = bell_draw(streams_of[12], (FF,), 0.5, 3.0, ((0, 32),))
    w_down = bell_draw(streams_of[13], (FF, D), FF ** -0.5, 0.125, ((0, 32),))
    b_down = bell_draw(streams_of[14], (D,), 0.5, 3.0, ((0, 32),))
    gain_one = jnp.clip(1.0 + 0.1 * jax.random.normal(streams_of[15], (D,), jnp.float32), 0.5, 1.5).astype(jnp.bfloat16)
    bias_one = bell_draw(streams_of[16], (D,), 0.5, 3.0, ((0, 32),))
    gain_two = jnp.clip(1.0 + 0.1 * jax.random.normal(streams_of[17], (D,), jnp.float32), 0.5, 1.5).astype(jnp.bfloat16)
    bias_two = bell_draw(streams_of[18], (D,), 0.5, 3.0, ((0, 32),))
    w_halt = bell_draw(streams_of[19], (D,), D ** -0.5, 0.25, ((0, 32),))
    return {"state": state, "segment": segment, "parent": parent, "halting": halting, "ponder": ponder, "cot_state": cot_state, "cot_halt": cot_halt, "w_query": w_query, "w_key": w_key, "w_value": w_value, "w_out": w_out, "w_up": w_up, "b_up": b_up, "w_down": w_down, "b_down": b_down, "gain_one": gain_one, "bias_one": bias_one, "gain_two": gain_two, "bias_two": bias_two, "w_halt": w_halt}


EPS = 1e-06
NEG = -1000000000.0
HALT_LIMIT = 0.99
GELU_C = math.sqrt(2.0 / math.pi)
GELU_A = 0.044715

@jax.custom_vjp
def low(v):
    return lax.optimization_barrier(v.astype(jnp.bfloat16)).astype(jnp.float32)

@jax.custom_vjp
def low_back(v):
    return v

def low_keep(v):
    return (low(v), None)

def low_pass(kept, grad):
    return (grad,)

def back_keep(v):
    return (v, None)

def back_low(kept, grad):
    return (low(grad),)
low.defvjp(low_keep, low_pass)
low_back.defvjp(back_keep, back_low)

def gelu(values):
    return 0.5 * values * (1.0 + jnp.tanh(GELU_C * (values + GELU_A * values * values * values)))

def timing(positions, model_width):
    half_width = model_width // 2
    freq_rates = jnp.exp(-math.log(10000.0) * jnp.arange(half_width, dtype=jnp.float32) / half_width)
    angles = positions[:, None] * freq_rates[None, :]
    return jnp.concatenate([jnp.sin(angles), jnp.cos(angles)], axis=1)

def reach_table(parent_row):
    seg_count = parent_row.shape[0]
    labels = jnp.arange(seg_count, dtype=jnp.int32)
    parent_hot = (parent_row[:, None] == labels[None, :]).astype(jnp.int32)
    walker = (labels[:, None] == labels[None, :]).astype(jnp.int32)
    reach_all = walker
    for repeat in range(seg_count):
        walker = jnp.dot(walker, parent_hot)
        reach_all = jnp.maximum(reach_all, walker)
    return reach_all

def allowed_mask(query_seg, key_seg, reach_all):
    seg_count = reach_all.shape[0]
    labels = jnp.arange(seg_count, dtype=jnp.int32)
    query_hot = (query_seg[:, None] == labels[None, :]).astype(jnp.float32)
    key_hot = (key_seg[:, None] == labels[None, :]).astype(jnp.float32)
    path_hits = jnp.dot(query_hot, reach_all.astype(jnp.float32), precision=lax.Precision.HIGHEST)
    return jnp.dot(path_hits, key_hot.T, precision=lax.Precision.HIGHEST) > 0.5

def layer_norm(values):
    centered = values - lax.optimization_barrier(jnp.mean(values, axis=-1, keepdims=True))
    variance = lax.optimization_barrier(jnp.mean(centered * centered, axis=-1, keepdims=True))
    return centered * lax.rsqrt(variance + EPS)

def forward(params, state32, allowed, halting_row):
    query_mat, key_mat, value_mat, out_mat, up_mat, up_bias, down_mat, down_bias, gain_a, bias_a, gain_b, bias_b, halt_vec = params
    precise = lax.Precision.HIGHEST
    row_count, model_width = state32.shape
    head_size = model_width // HEADS
    score_scale = head_size ** (-0.5)
    signal_in = state32 + timing(jnp.arange(row_count, dtype=jnp.float32), model_width)
    normed = low(signal_in)
    queries = low_back(low(jnp.dot(normed, query_mat, precision=precise))).reshape(row_count, HEADS, head_size)
    keys_all = low_back(low(jnp.dot(normed, key_mat, precision=precise))).reshape(row_count, HEADS, head_size)
    values_all = low_back(low(jnp.dot(normed, value_mat, precision=precise))).reshape(row_count, HEADS, head_size)
    scores = score_scale * low_back(jnp.einsum('qhd,khd->hqk', queries, keys_all, precision=precise))
    scores = jnp.where(allowed[None], scores, NEG)
    softmax_out = low(jax.nn.softmax(scores, axis=-1))
    mixed_heads = jnp.einsum('hqk,khd->qhd', softmax_out, values_all, precision=precise)
    mixed_heads = low_back(low(mixed_heads)).reshape(row_count, model_width)
    attended = low_back(jnp.dot(mixed_heads, out_mat, precision=precise))
    norm_one = layer_norm(signal_in + attended) * gain_a + bias_a
    pre_act = low_back(jnp.dot(low(norm_one), up_mat, precision=precise)) + up_bias
    hidden = low(gelu(pre_act))
    down_out = low_back(jnp.dot(hidden, down_mat, precision=precise)) + down_bias
    norm_two = layer_norm(norm_one + down_out) * gain_b + bias_b
    logits = lax.optimization_barrier(jnp.sum(norm_two * halt_vec, axis=1))
    running = (halting_row < HALT_LIMIT).astype(jnp.float32)
    weight = running * jax.nn.sigmoid(logits) * (1.0 - halting_row)
    mixed_state = weight[:, None] * norm_two + (1.0 - weight[:, None]) * state32
    return (mixed_state, halting_row + weight, weight)

def reference(state, segment, parent, halting, ponder, cot_state, cot_halt, w_query, w_key, w_value, w_out, w_up, b_up, w_down, b_down, gain_one, bias_one, gain_two, bias_two, w_halt):
    params = tuple((member.astype(jnp.float32) for member in (w_query, w_key, w_value, w_out, w_up, b_up, w_down, b_down, gain_one, bias_one, gain_two, bias_two, w_halt)))
    tree_count = MICRO * N_DP
    model_width = state.shape[2]
    members = (state.reshape(tree_count, TREE, model_width), segment.reshape(tree_count, TREE).astype(jnp.int32), parent.reshape(tree_count, SEGS).astype(jnp.int32), halting.reshape(tree_count, TREE), ponder.reshape(tree_count, TREE), cot_state.reshape(tree_count, TREE, model_width), cot_halt.reshape(tree_count, TREE))

    def one_tree(totals, member):
        tree_state, tree_seg, tree_parent, tree_halt, tree_ponder, tree_cot, tree_cot_halt = member
        allowed = allowed_mask(tree_seg, tree_seg, reach_table(tree_parent))
        state32 = tree_state.astype(jnp.float32)

        def apply_layer(weights, source):
            return forward(weights, source, allowed, tree_halt)
        (mixed_state, halt_next, weight), pullback = jax.vjp(apply_layer, params, state32)
        weight_grads, state_grad = pullback((tree_cot.astype(jnp.float32), tree_cot_halt, jnp.zeros_like(weight)))
        running = (tree_halt < HALT_LIMIT).astype(jnp.float32)
        ponder_next = tree_ponder + running * (1.0 - weight)
        totals = jax.tree.map(lambda first_term, second_term: first_term + second_term, totals, weight_grads)
        return (totals, (mixed_state.astype(jnp.bfloat16), halt_next, ponder_next, state_grad))
    zero_grads = tuple((jnp.zeros(member.shape, jnp.float32) for member in params))
    totals, stacked = lax.scan(one_tree, zero_grads, members)
    state_out, halt_out, ponder_out, grad_out = stacked
    return (state_out.reshape(MICRO, TOKENS, model_width), halt_out.reshape(MICRO, TOKENS), ponder_out.reshape(MICRO, TOKENS), grad_out.reshape(MICRO, TOKENS, model_width), totals[0], totals[1], totals[2], totals[3], totals[4], totals[5], totals[6], totals[7], totals[8], totals[9], totals[10], totals[11], totals[12])
```

```python
import functools
import math

import jax
import jax.numpy as jnp
from jax import lax
from jax.experimental import pallas as pl
from jax.experimental.pallas import tpu as pltpu
from jax.sharding import PartitionSpec as P

HEADS = 8
EPS = 1e-06
HALT_LIMIT = 0.99
GELU_C = math.sqrt(2.0 / math.pi)
GELU_A = 0.044715
LOG2E = 1.0 / math.log(2.0)
LN2 = math.log(2.0)
BIG = 2.0**100
F32 = jnp.float32
BF16 = jnp.bfloat16
MESH = pl.DeviceIdType.MESH
VECTORS = 6


def nn(a, b):
    return lax.dot_general(a, b, (((1,), (0,)), ((), ())), preferred_element_type=F32)


def nt(a, b):
    return lax.dot_general(a, b, (((1,), (1,)), ((), ())), preferred_element_type=F32)


def tn(a, b):
    return lax.dot_general(a, b, (((0,), (0,)), ((), ())), preferred_element_type=F32)


def iota(shape, axis):
    return lax.broadcasted_iota(jnp.int32, shape, axis)


def flip(index, bit):
    return index + bit - 2 * bit * lax.rem(lax.div(index, bit), 2)


def col_sum(values):
    return jnp.sum(values, axis=0, keepdims=True)


def norm(values):
    centered = values - jnp.mean(values, axis=-1, keepdims=True)
    inv = lax.rsqrt(jnp.mean(centered * centered, axis=-1, keepdims=True) + EPS)
    return centered * inv, inv


def norm_back(grad, normal, inv):
    return inv * (
        grad
        - jnp.mean(grad, axis=-1, keepdims=True)
        - normal * jnp.mean(grad * normal, axis=-1, keepdims=True)
    )


class Plan:
    def __init__(self, micro, rows, width, hidden, segs, n_dp, n_z, fused):
        self.micro, self.rows, self.width, self.hidden = micro, rows, width, hidden
        self.segs, self.n_dp, self.n_z, self.fused = segs, n_dp, n_z, fused
        self.tree = rows * n_z
        self.head = width // HEADS
        self.pair = 2 * self.head
        self.pairs = HEADS // 2
        self.cols = 4 * width + hidden
        self.devices = n_dp * n_z
        self.part = width // self.devices
        self.part_h = hidden // self.devices


def make_signal(p, sig):
    half = p.width // 2
    freq = jnp.exp(
        (-math.log(10000.0) / half) * iota((1, half), 1).astype(F32)
    )
    far = (iota((8, 1), 0) * p.rows).astype(F32) * freq
    far_sin, far_cos = jnp.sin(far), jnp.cos(far)
    step = 32

    @pl.loop(0, p.rows // step)
    def _(i):
        near = (iota((step, 1), 0) + i * step).astype(F32) * freq
        near_sin, near_cos = jnp.sin(near), jnp.cos(near)
        for b in range(p.n_z):
            s, c = far_sin[b : b + 1], far_cos[b : b + 1]
            at = pl.ds(pl.multiple_of(b * p.rows + i * step, step), step)
            sig[at, 0:half] = near_sin * c + near_cos * s
            sig[at, half : 2 * half] = near_cos * c - near_sin * s


def blocked_table(p, parent_row):
    size = 128
    up = jnp.where(
        iota((16, p.segs), 0) == parent_row, 1.0, 0.0
    )
    up = jnp.concatenate([up, jnp.zeros((16, size - p.segs), F32)], axis=1)
    up = jnp.concatenate([up, jnp.zeros((size - 16, size), F32)], axis=0)
    row, column = iota((size, size), 0), iota((size, size), 1)
    reach = jnp.where(row == column, 1.0, up)
    for _ in range(4):
        reach = jnp.minimum(nn(reach.astype(BF16), reach.astype(BF16)), 1.0)
    inside = (row < p.segs) & (column < p.segs)
    return jnp.where(inside & (reach < 0.5), -BIG, 0.0)


def prepare_micro(p, m, z, r):
    table = blocked_table(p, r.parent[pl.ds(m, 1), :])
    seg_row = r.seg[pl.ds(m, 1), :]
    hot = jnp.where(iota((128, p.tree), 0) == seg_row, 1.0, 0.0)
    r.kfull[:, 128:256] = hot.T.astype(BF16)
    own = pl.ds(pl.multiple_of(z * p.rows, p.rows), p.rows)
    hot = jnp.where(iota((128, p.rows), 0) == r.seg[pl.ds(m, 1), own], 1.0, 0.0)
    feature = nn(table.astype(BF16), hot.astype(BF16)).astype(BF16)
    r.qfull[128:256, 0 : p.rows] = feature
    r.qfull[128:256, p.rows : 2 * p.rows] = feature
    for b in range(p.n_z):
        at = slice(b * p.rows, (b + 1) * p.rows)
        r.h[at, :] = (r.states[m, b].astype(F32) + r.sig[at, :]).astype(BF16)

    w = p.width
    h_all = r.h[...]
    r.k[...] = nn(h_all, r.wa[:, w : 2 * w]).astype(BF16)
    r.v[...] = nn(h_all, r.wa[:, 2 * w : 3 * w]).astype(BF16)
    r.vt[...] = r.v[...].T
    q = nn(r.h[own, :], r.wa[:, 0:w]) * (LOG2E * p.head**-0.5)
    r.qt[...] = q.astype(BF16).T


def fill_pair(p, full, flat, i):
    low = pl.ds(pl.multiple_of(i * p.pair, p.pair), p.head)
    high = pl.ds(pl.multiple_of(i * p.pair + p.head, p.head), p.head)
    full[0 : p.head, 0 : p.rows] = flat[low, :].astype(BF16)
    full[p.head : p.pair, p.rows : 2 * p.rows] = flat[high, :].astype(BF16)


def attention_forward(p, r):
    @pl.loop(0, p.pairs)
    def _(i):
        lanes = pl.ds(pl.multiple_of(i * p.pair, p.pair), p.pair)
        r.kfull[:, 0:128] = r.k[:, lanes]
        fill_pair(p, r.qfull, r.qt, i)
        s = nn(r.kfull[...], r.qfull[...])
        top = jnp.max(s, axis=0, keepdims=True)
        r.e[i] = jnp.exp2(s - top).astype(BF16)
        r.vo[0:128, :] = r.vt[lanes, :]
        o = nn(r.vo[...], r.e[i])
        inv = 1.0 / o[128:136]
        r.inv[i] = inv
        low = pl.ds(pl.multiple_of(i * p.pair, p.pair), p.head)
        high = pl.ds(pl.multiple_of(i * p.pair + p.head, p.head), p.head)
        r.ot[low, :] = o[0 : p.head, 0 : p.rows] * inv[0:1, 0 : p.rows]
        r.ot[high, :] = o[p.head : p.pair, p.rows :] * inv[0:1, p.rows :]


def transition(p, m, z, r):
    w = p.width
    rows = p.rows
    vec = lambda k: r.vec[k : k + 1, :]
    gain_a, bias_a, gain_b, bias_b, halt_vec = vec(1), vec(2), vec(3), vec(4), vec(5)
    own = pl.ds(pl.multiple_of(z * rows, rows), rows)
    w_out = slice(3 * w, 4 * w)

    lane = iota((128, rows), 0)
    packed = jnp.where(
        lane == 0,
        r.halting[pl.ds(m, 1), :],
        jnp.where(lane == 1, r.ponder[pl.ds(m, 1), :], r.cot_halt[pl.ds(m, 1), :]),
    ).T
    halting, ponder, cot_halt = packed[:, 0:1], packed[:, 1:2], packed[:, 2:3]

    r.otb[...] = r.ot[...].astype(BF16)
    state = r.states[m, z].astype(F32)
    y1 = state + r.sig[own, :] + tn(r.otb[...], r.wa[:, w_out])
    xh1, inv1 = norm(y1)
    n1 = xh1 * gain_a + bias_a
    r.xh1[...] = xh1
    r.u[...] = n1.astype(BF16)
    r.acc[...] = n1

    @pl.loop(0, p.hidden // w)
    def _(j):
        at = pl.ds(pl.multiple_of(j * w, w), w)
        pre = nn(r.u[...], r.wa[:, pl.ds(pl.multiple_of(4 * w + j * w, w), w)])
        pre = pre + r.bup[:, at]
        square = pre * pre
        t = jnp.tanh(pre * (GELU_C + (GELU_C * GELU_A) * square))
        half = 0.5 + 0.5 * t
        f = (pre * half).astype(BF16)
        slope = half + (0.5 * pre) * (1.0 - t * t) * (
            GELU_C + (3.0 * GELU_A * GELU_C) * square
        )
        block = pl.ds(pl.multiple_of(j * rows, rows), rows)
        r.dkv[block, 0:w] = f
        r.dkv[block, w : 2 * w] = slope.astype(BF16)
        r.acc[...] += nn(f, r.wd[at, :])

    y2 = r.acc[...] + vec(0)
    xh2, inv2 = norm(y2)
    s2 = xh2 * gain_b + bias_b
    ph = jax.nn.sigmoid(jnp.sum(s2 * halt_vec, axis=1, keepdims=True))
    run = jnp.where(halting < HALT_LIMIT, 1.0, 0.0)
    room = run * (1.0 - halting)
    weight = room * ph
    state = r.states[m, z].astype(F32)
    r.new_state[m] = (weight * s2 + (1.0 - weight) * state).astype(BF16)
    lane = iota((rows, 128), 1)
    packed = jnp.where(
        lane == 0, halting + weight, ponder + run * (1.0 - weight)
    ).T
    r.new_halting[pl.ds(m, 1), :] = packed[0:1, :]
    r.new_ponder[pl.ds(m, 1), :] = packed[1:2, :]

    cot = r.cot[m].astype(F32)
    dw = jnp.sum(cot * (s2 - state), axis=1, keepdims=True) + cot_halt
    dl = dw * room * ph * (1.0 - ph)
    ds2 = weight * cot + dl * halt_vec
    r.gvec[5:6, :] += col_sum(dl * s2)
    r.gvec[3:4, :] += col_sum(ds2 * xh2)
    r.gvec[4:5, :] += col_sum(ds2)
    dy2 = norm_back(ds2 * gain_b, xh2, inv2)
    r.gvec[0:1, :] += col_sum(dy2)
    r.dg[...] = dy2.astype(BF16)
    r.acc[...] = dy2
    r.gstate[m] = (1.0 - weight) * cot

    @pl.loop(0, p.hidden // w)
    def _(j):
        at = pl.ds(pl.multiple_of(j * w, w), w)
        at_up = pl.ds(pl.multiple_of(4 * w + j * w, w), w)
        block = pl.ds(pl.multiple_of(j * rows, rows), rows)
        dz = nt(r.dg[...], r.wd[at, :]) * r.dkv[block, w : 2 * w].astype(F32)
        r.gbup[:, at] += col_sum(dz)
        dzb = dz.astype(BF16)
        r.acc[...] += nt(dzb, r.wa[:, at_up])
        r.ga[:, at_up] += tn(r.u[...], dzb)
        r.gd[at, :] += tn(r.dkv[block, 0:w], r.dg[...])

    dn1 = r.acc[...]
    xh1 = r.xh1[...]
    r.gvec[1:2, :] += col_sum(dn1 * xh1)
    r.gvec[2:3, :] += col_sum(dn1)
    dy1 = norm_back(dn1 * gain_a, xh1, inv1)
    r.gstate[m] += dy1
    da = dy1.astype(BF16)
    r.ga[:, w_out] += nn(r.otb[...], da)
    r.dot[...] = nt(r.wa[:, w_out], da)


def attention_backward(p, m, dp, z, r):
    w = p.width
    r.vt[...] = r.k[...].T

    @pl.loop(0, p.pairs)
    def _(i):
        lanes = pl.ds(pl.multiple_of(i * p.pair, p.pair), p.pair)
        low = pl.ds(pl.multiple_of(i * p.pair, p.pair), p.head)
        high = pl.ds(pl.multiple_of(i * p.pair + p.head, p.head), p.head)
        inv = r.inv[i]
        do_a = (r.dot[low, :] * inv[0:1, 0 : p.rows]).astype(BF16)
        do_b = (r.dot[high, :] * inv[0:1, p.rows :]).astype(BF16)
        r.dofull[0 : p.head, 0 : p.rows] = do_a
        r.dofull[p.head : p.pair, p.rows :] = do_b
        inner = jnp.concatenate(
            [
                col_sum(do_a.astype(F32) * r.ot[low, :]),
                col_sum(do_b.astype(F32) * r.ot[high, :]),
            ],
            axis=1,
        )
        rough = (-inner).astype(BF16).astype(F32)
        row = iota((16, 2 * p.rows), 0)
        r.dofull[128:144, :] = jnp.where(
            row == 0, rough, jnp.where(row == 1, -inner - rough, 0.0)
        ).astype(BF16)
        r.vfull[:, 0:128] = r.v[:, lanes]
        dp = nn(r.vfull[...], r.dofull[...])
        ds = (r.e[i].astype(F32) * dp).astype(BF16)
        r.ds[...] = ds
        fill_pair(p, r.qfull, r.qt, i)
        r.dkv[0 : p.tree, lanes] = (nt(ds, r.qfull[0:128, :]) * LN2).astype(BF16)
        r.dkv[0 : p.tree, pl.ds(pl.multiple_of(w + i * p.pair, p.pair), p.pair)] = nt(
            r.e[i], r.dofull[0:128, :]
        ).astype(BF16)
        dq = nn(r.vt[lanes, :], r.ds[...]) * (p.head**-0.5)
        r.dqt[low, :] = dq[0 : p.head, 0 : p.rows].astype(BF16)
        r.dqt[high, :] = dq[p.head : p.pair, p.rows :].astype(BF16)

    own = pl.ds(pl.multiple_of(z * p.rows, p.rows), p.rows)
    r.dq[...] = r.dqt[...].T
    r.gstate[m] += nt(r.dq[...], r.wa[:, 0:w])

    @pl.when(m >= 2)
    def _():
        for i in range(1, p.n_z):
            back_copy(p, m - 2, i, dp, z, r).wait_send()

    @pl.loop(0, p.n_z)
    def _(b):
        at = pl.ds(pl.multiple_of(b * p.rows, p.rows), p.rows)
        dh = nt(r.dkv[at, :], r.wa[:, w : 3 * w])
        r.dh[lax.rem(m, 2), b] = dh.astype(BF16)

        @pl.when(z == b)
        def _():
            r.gstate[m] += dh

    for i in range(1, p.n_z):
        back_copy(p, m, i, dp, z, r).start()

    r.ga[:, 0:w] += tn(r.h[own, :], r.dq[...])
    for j in range(2):
        at = slice(j * w, (j + 1) * w)
        to = slice((1 + j) * w, (2 + j) * w)
        r.ga[:, to] += tn(r.h[...], r.dkv[0 : p.tree, at])


def remote(src, dst, send, recv, device):
    return pltpu.make_async_remote_copy(
        src_ref=src,
        dst_ref=dst,
        send_sem=send,
        recv_sem=recv,
        device_id=device,
        device_id_type=MESH,
    )


def back_copy(p, m, i, dp, z, r):
    peer = lax.rem(z + i, p.n_z)
    return remote(
        r.dh.at[lax.rem(m, 2), peer],
        r.dh_in.at[m, i - 1],
        r.back_send.at[m, i - 1],
        r.back_recv.at[m, i - 1],
        (dp, peer),
    )


class Links:
    def __init__(self, send, recv):
        self.send, self.recv, self.used, self.sent = send, recv, 0, []

    def go(self, src, dst, device):
        copy = remote(src, dst, self.send.at[self.used], self.recv.at[self.used], device)
        self.used += 1
        copy.start()
        self.sent.append(copy)
        return copy

    def landed(self, copy):
        copy.wait_send()
        self.sent = [other for other in self.sent if other is not copy]

    def finish(self):
        for copy in self.sent:
            copy.wait_send()
        self.sent = []


def pieces(p, r):
    w = p.width
    return (
        (r.wa, p.part, 0, 3 * w),
        (r.wa, p.part, 3 * w, p.cols),
        (r.wd, p.part_h, 0, w),
        (r.ws, 16, 0, 128),
    )


def rows_of(dp, size):
    return pl.ds(pl.multiple_of(dp * size, size), size)


def gather_states_start(p, m, dp, z, r, links):
    copies = []
    for i in range(1, p.n_z):
        peer = lax.rem(z + i, p.n_z)
        copies.append(links.go(r.state.at[m], r.states.at[m, z], (dp, peer)))
    return copies


def gather_z_start(p, piece, dp, z, links):
    ref, part, c0, c1 = piece
    at = ref.at[rows_of(dp * p.n_z + z, part), c0:c1]
    return [links.go(at, at, (dp, lax.rem(z + i, p.n_z))) for i in range(1, p.n_z)]


def gather_rest(p, piece, dp, z, links):
    ref, part, c0, c1 = piece
    size = part * p.n_z
    mid = (c0 + c1) // 2 if c1 - c0 >= 256 else c1
    x, y, core = (flip(dp, 2), z), (flip(dp, 4), z), (flip(dp, 1), z)

    def send(block, a, b, to):
        at = ref.at[rows_of(block, size), a:b]
        return links.go(at, at, to)

    split = mid < c1
    dpx, dpy = flip(dp, 2), flip(dp, 4)
    dpxy = flip(dpx, 4)
    a1 = send(dp, c0, mid, x)
    b1 = send(dp, mid, c1, y) if split else None
    a2 = send(dp, c0, mid, y)
    b2 = send(dp, mid, c1, x) if split else None
    core0 = send(dp, c0, c1, core)
    a1.wait_recv()
    a3 = send(dpx, c0, mid, y)
    if split:
        b1.wait_recv()
        b3 = send(dpy, mid, c1, x)
        b2.wait_recv()
    core1 = send(dpx, c0, c1, core)
    a2.wait_recv()
    core2 = send(dpy, c0, c1, core)
    a3.wait_recv()
    if split:
        b3.wait_recv()
    core3 = send(dpxy, c0, c1, core)
    for copy in (core0, core1, core2, core3):
        copy.wait_recv()


def spread_vectors(p, r):
    r.wsf[...] = r.ws[...].astype(F32)

    def spread(k, part, total):
        g = r.wsf[pl.ds(k, p.devices, stride=16), :].astype(BF16)
        lane, column = iota((128, total), 0), iota((128, total), 1)
        place = jnp.where((lane < part) & (lax.rem(column, part) == lane), 1.0, 0.0)
        full = nn(g, place.astype(BF16))
        mine = lax.div(iota((p.devices, total), 1), part) == iota((p.devices, total), 0)
        return col_sum(jnp.where(mine, full, 0.0))

    for k in range(VECTORS):
        r.vec[k : k + 1, :] = spread(k, p.part, p.width)
    r.bup[...] = spread(VECTORS, p.part_h, p.hidden)


def collect_vectors(p, r):
    r.gs[...] = jnp.zeros(r.gs.shape, F32)

    def collect(k, row, part, total):
        mine = lax.div(iota((p.devices, total), 1), part) == iota((p.devices, total), 0)
        full = jnp.where(mine, row, 0.0)
        high = full.astype(BF16)
        rest = (full - high.astype(F32)).astype(BF16)
        lane, column = iota((128, total), 0), iota((128, total), 1)
        place = jnp.where(
            (lane < part) & (lax.rem(column, part) == lane), 1.0, 0.0
        ).astype(BF16)
        r.gs[pl.ds(k, p.devices, stride=16), :] = nt(high, place) + nt(rest, place)

    for k in range(VECTORS):
        collect(k, r.gvec[k : k + 1, :], p.part, p.width)
    collect(VECTORS, r.gbup[...], p.part_h, p.hidden)


def reduce_piece(p, g, part, c0, c1, bufs, dp, z, links):
    size = part * p.n_z
    cols = c1 - c0
    mid = cols // 2 if cols >= 256 else cols
    split = mid < cols
    s1, r1, r2, r3, s4, r4 = bufs
    s2 = s3 = s1
    x, y, core = (flip(dp, 2), z), (flip(dp, 4), z), (flip(dp, 1), z)
    dpx, dpy = flip(dp, 2), flip(dp, 4)
    order = (dp, dpx, dpy, flip(dpx, 4))
    links.finish()
    for k, block in enumerate(order):
        s1[k * size : (k + 1) * size, 0:cols] = g[
            rows_of(flip(block, 1), size), c0:c1
        ].astype(BF16)
    first = links.go(s1.at[:, 0:cols], r1.at[:, 0:cols], core)
    first.wait_recv()
    links.landed(first)
    for k, block in enumerate(order):
        g[rows_of(block, size), c0:c1] += r1[k * size : (k + 1) * size, 0:cols].astype(F32)

    def send2(slot, block, a, b):
        s2[slot * size : (slot + 1) * size, a:b] = g[
            rows_of(block, size), c0 + a : c0 + b
        ].astype(BF16)

    def add2(slot, block, a, b):
        g[rows_of(block, size), c0 + a : c0 + b] += r2[
            slot * size : (slot + 1) * size, a:b
        ].astype(F32)

    send2(0, order[1], 0, mid)
    send2(1, order[3], 0, mid)
    a1 = links.go(s2.at[0 : 2 * size, 0:mid], r2.at[:, 0:mid], x)
    if split:
        send2(0, order[2], mid, cols)
        send2(1, order[3], mid, cols)
        b1 = links.go(s2.at[0 : 2 * size, mid:cols], r2.at[:, mid:cols], y)
    a1.wait_recv()
    add2(0, order[0], 0, mid)
    add2(1, order[2], 0, mid)
    links.landed(a1)
    s3[0:size, 0:mid] = g[rows_of(order[2], size), c0 : c0 + mid].astype(BF16)
    a2 = links.go(s3.at[0:size, 0:mid], r3.at[:, 0:mid], y)
    if split:
        b1.wait_recv()
        add2(0, order[0], mid, cols)
        add2(1, order[1], mid, cols)
        links.landed(b1)
        s3[0:size, mid:cols] = g[rows_of(order[1], size), c0 + mid : c1].astype(BF16)
        b2 = links.go(s3.at[0:size, mid:cols], r3.at[:, mid:cols], x)
    a2.wait_recv()
    if split:
        b2.wait_recv()
    g[rows_of(dp, size), c0:c1] += r3[:, 0:cols].astype(F32)
    last = []
    for i in range(1, p.n_z):
        peer = lax.rem(z + i, p.n_z)
        s4[i - 1, :, 0:cols] = g[rows_of(dp * p.n_z + peer, part), c0:c1].astype(BF16)
        last.append(
            links.go(s4.at[i - 1, :, 0:cols], r4.at[i - 1, :, 0:cols], (dp, peer))
        )
    total = g[rows_of(dp * p.n_z + z, part), c0:c1]
    for i in range(1, p.n_z):
        last[i - 1].wait_recv()
        total = total + r4[i - 1, :, 0:cols].astype(F32)
    return total


class Refs:
    pass


def kernel(p, names, *refs):
    r = Refs()
    for name, ref in zip(names, refs):
        setattr(r, name, ref)
    dp = lax.axis_index("dp")
    z = lax.axis_index("fsdp")
    w = p.width
    links = Links(r.send_sem, r.recv_sem)

    barrier = pltpu.get_barrier_semaphore()
    peers = [(dp, lax.rem(z + i, p.n_z)) for i in range(1, p.n_z)]
    if p.fused:
        peers += [(flip(dp, bit), z) for bit in (1, 2, 4)]
        n = dp * p.n_z + z
        at = rows_of(n, p.part)
        r.wa[at, 0:w] = r.w_query[...]
        r.wa[at, w : 2 * w] = r.w_key[...]
        r.wa[at, 2 * w : 3 * w] = r.w_value[...]
        r.wa[at, 3 * w : 4 * w] = r.w_out[...]
        r.wa[at, 4 * w :] = r.w_up[...]
        r.wd[rows_of(n, p.part_h), :] = r.w_down[...]
        r.small[...] = jnp.zeros((16, 128), F32)
        for k, name in enumerate(
            ("b_down", "gain_one", "bias_one", "gain_two", "bias_two", "w_halt")
        ):
            r.small[k : k + 1, 0 : p.part] = getattr(r, name)[...].astype(F32)
        r.small[VECTORS : VECTORS + 1, 0 : p.part_h] = r.b_up[...].astype(F32)
        r.ws[rows_of(n, 16), :] = r.small[...].astype(BF16)
    for peer in peers:
        pl.semaphore_signal(barrier, inc=1, device_id=peer, device_id_type=MESH)
    pl.semaphore_wait(barrier, len(peers))

    coming = []
    if p.fused:
        stages = [gather_z_start(p, piece, dp, z, links) for piece in pieces(p, r)[:1]]
        coming += gather_states_start(p, 0, dp, z, r, links)
        stages += [gather_z_start(p, piece, dp, z, links) for piece in pieces(p, r)[1:]]
        for m in range(1, p.micro):
            coming += gather_states_start(p, m, dp, z, r, links)
    else:
        for m in range(p.micro):
            coming += gather_states_start(p, m, dp, z, r, links)

    for m in range(p.micro):
        r.states[m, z] = r.state[m]
    make_signal(p, r.sig)
    r.ga[...] = jnp.zeros(r.ga.shape, F32)
    r.gd[...] = jnp.zeros(r.gd.shape, F32)
    r.gvec[...] = jnp.zeros(r.gvec.shape, F32)
    r.gbup[...] = jnp.zeros(r.gbup.shape, F32)
    r.qfull[...] = jnp.zeros(r.qfull.shape, BF16)
    r.dofull[...] = jnp.zeros(r.dofull.shape, BF16)
    r.vo[128:144, :] = jnp.ones((16, p.tree), BF16)
    lane = iota((p.tree, 128), 1)
    r.vfull[:, 128:256] = jnp.where(lane < 2, 1.0, 0.0).astype(BF16)

    if p.fused:
        for piece, copies in zip(pieces(p, r), stages):
            for copy in copies:
                copy.wait_recv()
            gather_rest(p, piece, dp, z, links)
        spread_vectors(p, r)
    for copy in coming:
        copy.wait_recv()

    @pl.loop(0, p.micro)
    def _(m):
        prepare_micro(p, m, z, r)
        attention_forward(p, r)
        transition(p, m, z, r)
        attention_backward(p, m, dp, z, r)

    if p.fused:
        collect_vectors(p, r)
        bufs_f = [getattr(r, "f%d" % k) for k in range(6)]
        bufs = [r.f0] + [getattr(r, "b%d" % k) for k in range(1, 6)]
        bufs_d = [r.e.at[0]] + [getattr(r, "d%d" % k) for k in range(1, 6)]
        bufs_s = [getattr(r, "e%d" % k) for k in range(6)]
        total = reduce_piece(p, r.ga, p.part, 3 * w, p.cols, bufs_f, dp, z, links)
        r.g_out[...] = total[:, 0:w]
        r.g_up[...] = total[:, w:]
        r.g_down[...] = reduce_piece(p, r.gd, p.part_h, 0, w, bufs_d, dp, z, links)
        total = reduce_piece(p, r.ga, p.part, 0, 3 * w, bufs, dp, z, links)
        r.g_query[...] = total[:, 0:w]
        r.g_key[...] = total[:, w : 2 * w]
        r.g_value[...] = total[:, 2 * w : 3 * w]
        total = reduce_piece(p, r.gs, 16, 0, 128, bufs_s, dp, z, links)
        r.small[...] = total
        for k, name in enumerate(
            ("b_down", "gain_one", "bias_one", "gain_two", "bias_two", "w_halt")
        ):
            getattr(r, "g_" + name)[...] = r.small[k : k + 1, 0 : p.part]
        r.g_b_up[...] = r.small[VECTORS : VECTORS + 1, 0 : p.part_h]
    for m in range(p.micro):
        for i in range(1, p.n_z):
            copy = back_copy(p, m, i, dp, z, r)
            copy.wait_recv()
            if m >= p.micro - 2:
                copy.wait_send()
            r.gstate[m] += r.dh_in[m, i - 1].astype(F32)
    links.finish()


def run_kernel(p, inputs):
    w, t, rows = p.width, p.tree, p.rows
    outs = {
        "new_state": ((p.micro, rows, w), BF16),
        "new_halting": ((p.micro, rows), F32),
        "new_ponder": ((p.micro, rows), F32),
        "gstate": ((p.micro, rows, w), F32),
    }
    scratch = {}
    if p.fused:
        for name in ("query", "key", "value", "out"):
            outs["g_" + name] = ((p.part, w), F32)
        outs["g_up"] = ((p.part, p.hidden), F32)
        outs["g_down"] = ((p.part_h, w), F32)
        for name in ("b_down", "gain_one", "bias_one", "gain_two", "bias_two", "w_halt"):
            outs["g_" + name] = ((1, p.part), F32)
        outs["g_b_up"] = ((1, p.part_h), F32)
        scratch.update(
            wa=((w, p.cols), BF16),
            wd=((p.hidden, w), BF16),
            ws=((p.devices * 16, 128), BF16),
            wsf=((p.devices * 16, 128), F32),
            small=((16, 128), F32),
            vec=((8, w), F32),
            bup=((1, p.hidden), F32),
            ga=((w, p.cols), F32),
            gd=((p.hidden, w), F32),
            gs=((p.devices * 16, 128), F32),
            gvec=((8, w), F32),
            gbup=((1, p.hidden), F32),
        )
        kinds = (
            ("f", p.part, p.cols - 3 * w),
            ("b", p.part, 3 * w),
            ("d", p.part_h, w),
            ("e", 16, 128),
        )
        for tag, part, cols in kinds:
            size = part * p.n_z
            shapes = [(k * size, cols) for k in (4, 4, 2, 1)]
            shapes += [(p.n_z - 1, part, cols)] * 2
            for k, shape in enumerate(shapes):
                if k or tag in "fe":
                    scratch[tag + str(k)] = (shape, BF16)
    else:
        outs.update(
            ga=((w, p.cols), F32),
            gd=((p.hidden, w), F32),
            gvec=((8, w), F32),
            gbup=((1, p.hidden), F32),
        )
    scratch.update(
        states=((p.micro, p.n_z, rows, w), BF16),
        sig=((t, w), F32),
        h=((t, w), BF16),
        k=((t, w), BF16),
        v=((t, w), BF16),
        vt=((w, t), BF16),
        qt=((w, rows), BF16),
        kfull=((t, 256), BF16),
        qfull=((256, 2 * rows), BF16),
        vfull=((t, 256), BF16),
        dofull=((256, 2 * rows), BF16),
        vo=((144, t), BF16),
        e=((p.pairs, t, 2 * rows), BF16),
        inv=((p.pairs, 8, 2 * rows), F32),
        ot=((w, rows), F32),
        otb=((w, rows), BF16),
        dot=((w, rows), F32),
        xh1=((rows, w), F32),
        u=((rows, w), BF16),
        acc=((rows, w), F32),
        dg=((rows, w), BF16),
        ds=((t, 2 * rows), BF16),
        dkv=((max(t, rows * (p.hidden // w)), 2 * w), BF16),
        dqt=((w, rows), BF16),
        dq=((rows, w), BF16),
        dh=((2, p.n_z, rows, w), BF16),
        dh_in=((p.micro, p.n_z - 1, rows, w), BF16),
    )
    vmem = pl.BlockSpec(memory_space=pltpu.VMEM)
    copies = 128
    names = (
        list(inputs)
        + list(outs)
        + list(scratch)
        + ["send_sem", "recv_sem", "back_send", "back_recv"]
    )
    results = pl.pallas_call(
        functools.partial(kernel, p, names),
        out_shape=[jax.ShapeDtypeStruct(s, d) for s, d in outs.values()],
        in_specs=[vmem] * len(inputs),
        out_specs=[vmem] * len(outs),
        scratch_shapes=[pltpu.VMEM(s, d) for s, d in scratch.values()]
        + [pltpu.SemaphoreType.DMA((copies,))] * 2
        + [pltpu.SemaphoreType.DMA((p.micro, p.n_z - 1))] * 2,
        compiler_params=pltpu.CompilerParams(
            collective_id=0, has_side_effects=True, vmem_limit_bytes=62 << 20
        ),
        name="layer",
    )(*inputs.values())
    return dict(zip(outs, results))


WEIGHTS = (
    "w_query",
    "w_key",
    "w_value",
    "w_out",
    "w_up",
    "b_up",
    "w_down",
    "b_down",
    "gain_one",
    "bias_one",
    "gain_two",
    "bias_two",
    "w_halt",
)


def per_device(state, segment, parent, halting, ponder, cot_state, cot_halt, *weights):
    micro, rows, width = state.shape
    given = dict(zip(WEIGHTS, weights))
    n_dp, n_z = lax.axis_size("dp"), lax.axis_size("fsdp")
    part, hidden = given["w_query"].shape[0], given["w_up"].shape[1]
    fused = n_dp == 8 and part % 16 == 0 and part <= 128
    p = Plan(micro, rows, width, hidden, parent.shape[2], n_dp, n_z, fused)
    inputs = dict(
        state=state,
        seg=segment,
        parent=parent.reshape(micro, p.segs),
        halting=halting,
        ponder=ponder,
        cot=cot_state,
        cot_halt=cot_halt,
    )
    if fused:
        for name, value in given.items():
            inputs[name] = value if value.ndim == 2 else value.reshape(1, -1)
        out = run_kernel(p, inputs)
        grads = []
        for name in WEIGHTS:
            value = out["g_" + name[2:]] if name.startswith("w_") and name != "w_halt" else out["g_" + name]
            grads.append(value.reshape(given[name].shape))
    else:
        axes = ("dp", "fsdp")
        full = {k: lax.all_gather(v, axes, axis=0, tiled=True) for k, v in given.items()}
        inputs["wa"] = jnp.concatenate([full[k] for k in WEIGHTS[:5]], axis=1)
        inputs["wd"] = full["w_down"]
        rows_f32 = [full[k].astype(F32) for k in WEIGHTS[7:]]
        rows_f32 += [jnp.zeros((width,), F32)] * 2
        inputs["vec"] = jnp.stack(rows_f32)
        inputs["bup"] = full["b_up"].astype(F32).reshape(1, -1)
        out = run_kernel(p, inputs)
        whole = [out["ga"][:, k * width : (k + 1) * width] for k in range(4)]
        whole += [out["ga"][:, 4 * width :], out["gbup"][0], out["gd"]]
        whole += [out["gvec"][k] for k in range(VECTORS)]
        grads = [
            lax.psum_scatter(g, axes, scatter_dimension=0, tiled=True) for g in whole
        ]
    return (out["new_state"], out["new_halting"], out["new_ponder"], out["gstate"], *grads)


def solution(mesh):
    tokens, flags = P(None, ("dp", "fsdp"), None), P(None, ("dp", "fsdp"))
    matrix, vector = P(("dp", "fsdp"), None), P(("dp", "fsdp"))
    weights = tuple(
        matrix if name in ("w_query", "w_key", "w_value", "w_out", "w_up", "w_down") else vector
        for name in WEIGHTS
    )
    return jax.shard_map(
        per_device,
        mesh=mesh,
        in_specs=(tokens, P(None, "dp"), P(None, "dp", None), flags, flags, tokens, flags)
        + weights,
        out_specs=(tokens, flags, flags, tokens) + weights,
        check_vma=False,
    )
```

```python
import functools
import math

import jax
import jax.numpy as jnp
from jax import lax
from jax.experimental import pallas as pl
from jax.experimental.pallas import tpu as pltpu
from jax.sharding import PartitionSpec as P

HEADS = 8
EPS = 1e-06
HALT_LIMIT = 0.99
GELU_C = math.sqrt(2.0 / math.pi)
GELU_A = 0.044715
LOG2E = 1.0 / math.log(2.0)
LN2 = math.log(2.0)
BIG = 2.0**100
F32 = jnp.float32
BF16 = jnp.bfloat16
MESH = pl.DeviceIdType.MESH
SMALL = ("b_down", "gain_one", "bias_one", "gain_two", "bias_two", "w_halt")
VECTORS = len(SMALL)


def nn(a, b):
    return lax.dot_general(a, b, (((1,), (0,)), ((), ())), preferred_element_type=F32)


def nt(a, b):
    return lax.dot_general(a, b, (((1,), (1,)), ((), ())), preferred_element_type=F32)


def tn(a, b):
    return lax.dot_general(a, b, (((0,), (0,)), ((), ())), preferred_element_type=F32)


def iota(shape, axis):
    return lax.broadcasted_iota(jnp.int32, shape, axis)


def flip(index, bit):
    return index + bit - 2 * bit * lax.rem(lax.div(index, bit), 2)


def col_sum(values):
    return jnp.sum(values, axis=0, keepdims=True)


def norm(values):
    centered = values - jnp.mean(values, axis=-1, keepdims=True)
    inv = lax.rsqrt(jnp.mean(centered * centered, axis=-1, keepdims=True) + EPS)
    return centered * inv, inv


def norm_back(grad, normal, inv):
    return inv * (
        grad
        - jnp.mean(grad, axis=-1, keepdims=True)
        - normal * jnp.mean(grad * normal, axis=-1, keepdims=True)
    )


class Plan:
    def __init__(self, micro, rows, width, hidden, segs, n_dp, n_z, fused):
        self.micro, self.rows, self.width, self.hidden = micro, rows, width, hidden
        self.segs, self.n_dp, self.n_z, self.fused = segs, n_dp, n_z, fused
        self.tree = rows * n_z
        self.head = width // HEADS
        self.pair = 2 * self.head
        self.pairs = HEADS // 2
        self.cols = 4 * width + hidden
        self.devices = n_dp * n_z
        self.part = width // self.devices
        self.part_h = hidden // self.devices


def make_signal(p, r):
    half = p.width // 2
    freq = jnp.exp((-math.log(10000.0) / half) * iota((1, half), 1).astype(F32))
    far = (iota((8, 1), 0) * p.rows).astype(F32) * freq
    r.far[:, 0:half] = jnp.sin(far)
    r.far[:, half:] = jnp.cos(far)
    step = 32

    @pl.loop(0, p.rows // step)
    def _(i):
        near = (iota((step, 1), 0) + i * step).astype(F32) * freq
        at = pl.ds(pl.multiple_of(i * step, step), step)
        r.near[at, 0:half] = jnp.sin(near)
        r.near[at, half:] = jnp.cos(near)


def signal(p, r, b):
    half = p.width // 2
    far_sin, far_cos = r.far[pl.ds(b, 1), 0:half], r.far[pl.ds(b, 1), half:]
    near_sin, near_cos = r.near[:, 0:half], r.near[:, half:]
    return near_sin * far_cos + near_cos * far_sin, near_cos * far_cos - near_sin * far_sin


def blocked_table(p, parent_row):
    size = 128
    up = jnp.where(
        iota((16, p.segs), 0) == parent_row, 1.0, 0.0
    )
    up = jnp.concatenate([up, jnp.zeros((16, size - p.segs), F32)], axis=1)
    up = jnp.concatenate([up, jnp.zeros((size - 16, size), F32)], axis=0)
    row, column = iota((size, size), 0), iota((size, size), 1)
    reach = jnp.where(row == column, 1.0, up)
    for _ in range(4):
        reach = jnp.minimum(nn(reach.astype(BF16), reach.astype(BF16)), 1.0)
    inside = (row < p.segs) & (column < p.segs)
    return jnp.where(inside & (reach < 0.5), -BIG, 0.0)


def prepare_micro(p, m, z, r):
    table = blocked_table(p, r.parent[m])
    seg_row = r.seg[pl.ds(m, 1), :]
    hot = jnp.where(iota((128, p.tree), 0) == seg_row, 1.0, 0.0)
    r.kfull[:, 128:256] = hot.T.astype(BF16)
    own = pl.ds(pl.multiple_of(z * p.rows, p.rows), p.rows)
    hot = jnp.where(iota((128, p.rows), 0) == r.seg[pl.ds(m, 1), own], 1.0, 0.0)
    feature = nn(table.astype(BF16), hot.astype(BF16)).astype(BF16)
    r.qfull[128:256, 0 : p.rows] = feature
    r.qfull[128:256, p.rows : 2 * p.rows] = feature
    for b in range(p.n_z):
        at = slice(b * p.rows, (b + 1) * p.rows)
        for k, wave in enumerate(signal(p, r, b)):
            lanes = slice(k * (p.width // 2), (k + 1) * (p.width // 2))
            r.h[at, lanes] = (r.states[m, b, :, lanes].astype(F32) + wave).astype(BF16)

    w = p.width
    half = p.tree // 2
    for c in range(2):
        at = slice(c * half, (c + 1) * half)
        r.k[at, :] = nn(r.h[at, :], r.wa[:, w : 2 * w]).astype(BF16)
        r.v[at, :] = nn(r.h[at, :], r.wa[:, 2 * w : 3 * w]).astype(BF16)
    r.vt[...] = r.v[...].T
    q = nn(r.h[own, :], r.wa[:, 0:w]) * (LOG2E * p.head**-0.5)
    r.qt[...] = q.astype(BF16).T


def fill_pair(p, full, flat, i):
    low = pl.ds(pl.multiple_of(i * p.pair, p.pair), p.head)
    high = pl.ds(pl.multiple_of(i * p.pair + p.head, p.head), p.head)
    full[0 : p.head, 0 : p.rows] = flat[low, :].astype(BF16)
    full[p.head : p.pair, p.rows : 2 * p.rows] = flat[high, :].astype(BF16)


def attention_forward(p, r):
    step = p.tree // 8

    def ready(i):
        r.kfull[:, 0:128] = r.k[:, pl.ds(pl.multiple_of(i * p.pair, p.pair), p.pair)]
        fill_pair(p, r.qfull, r.qt, i)

    def scores(c, top):
        at = slice(c * step, (c + 1) * step)
        s = nn(r.kfull[at, :], r.qfull[...])
        r.s[at, :] = s
        own = jnp.max(s.reshape(step // 8, 8, 2 * p.rows), axis=0)
        return own if top is None else jnp.maximum(top, own)

    def soften(i, c, top):
        at = slice(c * step, (c + 1) * step)
        r.e[i, at, :] = jnp.exp2(r.s[at, :] - top).astype(BF16)

    def finish(i):
        lanes = pl.ds(pl.multiple_of(i * p.pair, p.pair), p.pair)
        r.vo[0:128, :] = r.vt[lanes, :]
        o = nn(r.vo[...], r.e[i])
        inv = 1.0 / o[128:136]
        r.inv[i] = inv
        low = pl.ds(pl.multiple_of(i * p.pair, p.pair), p.head)
        high = pl.ds(pl.multiple_of(i * p.pair + p.head, p.head), p.head)
        r.ot[low, :] = o[0 : p.head, 0 : p.rows] * inv[0:1, 0 : p.rows]
        r.ot[high, :] = o[p.head : p.pair, p.rows :] * inv[0:1, p.rows :]

    ready(0)
    top = None
    for c in range(8):
        top = scores(c, top)
    r.top[...] = top

    @pl.loop(0, p.pairs - 1)
    def _(i):
        ready(i + 1)
        top = jnp.max(r.top[...], axis=0, keepdims=True)
        later = None
        for c in range(8):
            soften(i, c, top)
            later = scores(c, later)
        r.top[...] = later
        finish(i)

    top = jnp.max(r.top[...], axis=0, keepdims=True)
    for c in range(8):
        soften(p.pairs - 1, c, top)
    finish(p.pairs - 1)


def transition(p, m, z, r, between):
    w = p.width
    rows = p.rows
    vec = lambda k: r.vec[k : k + 1, :]
    gain_a, bias_a, gain_b, bias_b, halt_vec = vec(1), vec(2), vec(3), vec(4), vec(5)
    w_out = slice(3 * w, 4 * w)

    lane = iota((128, rows), 0)
    packed = jnp.where(
        lane == 0,
        r.halting[pl.ds(m, 1), :],
        jnp.where(lane == 1, r.ponder[pl.ds(m, 1), :], r.cot_halt[pl.ds(m, 1), :]),
    ).T
    halting, ponder, cot_halt = packed[:, 0:1], packed[:, 1:2], packed[:, 2:3]

    r.otb[...] = r.ot[...].astype(BF16)
    state = r.states[m, z].astype(F32)
    y1 = state + jnp.concatenate(signal(p, r, z), axis=1) + tn(r.otb[...], r.wa[:, w_out])
    xh1, inv1 = norm(y1)
    n1 = xh1 * gain_a + bias_a
    r.xh1[...] = xh1
    r.u[...] = n1.astype(BF16)
    r.acc[...] = n1

    wide = w // 2
    count = p.hidden // wide

    def expand(c):
        r.pre[c % 2] = (
            nn(r.u[...], r.wa[:, 4 * w + c * wide : 4 * w + (c + 1) * wide])
            + r.bup[:, c * wide : (c + 1) * wide]
        )

    def bend(c):
        block = slice((c // 2) * rows, (c // 2 + 1) * rows)
        off = (c % 2) * wide
        pre = r.pre[c % 2]
        square = pre * pre
        t = jnp.tanh(pre * (GELU_C + (GELU_C * GELU_A) * square))
        half = 0.5 + 0.5 * t
        r.dkv[block, off : off + wide] = (pre * half).astype(BF16)
        slope = half + (0.5 * pre) * (1.0 - t * t) * (
            GELU_C + (3.0 * GELU_A * GELU_C) * square
        )
        r.dkv[block, w + off : w + off + wide] = slope.astype(BF16)

    def shrink(c):
        block = slice((c // 2) * rows, (c // 2 + 1) * rows)
        off = (c % 2) * wide
        r.acc[...] += nn(
            r.dkv[block, off : off + wide], r.wd[c * wide : (c + 1) * wide, :]
        )

    expand(0)
    for c in range(count):
        if c + 1 < count:
            expand(c + 1)
        bend(c)
        if c:
            shrink(c - 1)
    shrink(count - 1)

    between()
    y2 = r.acc[...] + vec(0)
    xh2, inv2 = norm(y2)
    s2 = xh2 * gain_b + bias_b
    ph = jax.nn.sigmoid(jnp.sum(s2 * halt_vec, axis=1, keepdims=True))
    run = jnp.where(halting < HALT_LIMIT, 1.0, 0.0)
    room = run * (1.0 - halting)
    weight = room * ph
    state = r.states[m, z].astype(F32)
    r.new_state[m] = (weight * s2 + (1.0 - weight) * state).astype(BF16)
    lane = iota((rows, 128), 1)
    packed = jnp.where(
        lane == 0, halting + weight, ponder + run * (1.0 - weight)
    ).T
    r.new_halting[pl.ds(m, 1), :] = packed[0:1, :]
    r.new_ponder[pl.ds(m, 1), :] = packed[1:2, :]

    cot = r.cot[m].astype(F32)
    dw = jnp.sum(cot * (s2 - state), axis=1, keepdims=True) + cot_halt
    dl = dw * room * ph * (1.0 - ph)
    ds2 = weight * cot + dl * halt_vec
    r.gvec[5:6, :] += col_sum(dl * s2)
    r.gvec[3:4, :] += col_sum(ds2 * xh2)
    r.gvec[4:5, :] += col_sum(ds2)
    dy2 = norm_back(ds2 * gain_b, xh2, inv2)
    r.gvec[0:1, :] += col_sum(dy2)
    r.dg[...] = dy2.astype(BF16)
    r.acc[...] = dy2
    r.gstate[m] = (1.0 - weight) * cot

    @pl.loop(0, p.hidden // w)
    def _(j):
        at = pl.ds(pl.multiple_of(j * w, w), w)
        at_up = pl.ds(pl.multiple_of(4 * w + j * w, w), w)
        block = pl.ds(pl.multiple_of(j * rows, rows), rows)
        dz = nt(r.dg[...], r.wd[at, :]) * r.dkv[block, w : 2 * w].astype(F32)
        r.gbup[:, at] += col_sum(dz)
        dzb = dz.astype(BF16)
        r.acc[...] += nt(dzb, r.wa[:, at_up])
        r.ga[:, at_up] += tn(r.u[...], dzb)
        r.gd[at, :] += tn(r.dkv[block, 0:w], r.dg[...])

    dn1 = r.acc[...]
    xh1 = r.xh1[...]
    r.gvec[1:2, :] += col_sum(dn1 * xh1)
    r.gvec[2:3, :] += col_sum(dn1)
    dy1 = norm_back(dn1 * gain_a, xh1, inv1)
    r.gstate[m] += dy1
    da = dy1.astype(BF16)
    r.ga[:, w_out] += nn(r.otb[...], da)
    r.dot[...] = nt(r.wa[:, w_out], da)


def attention_backward(p, r, inside):
    w = p.width

    @pl.loop(0, p.pairs)
    def _(i):
        inside(i)
        lanes = pl.ds(pl.multiple_of(i * p.pair, p.pair), p.pair)
        low = pl.ds(pl.multiple_of(i * p.pair, p.pair), p.head)
        high = pl.ds(pl.multiple_of(i * p.pair + p.head, p.head), p.head)
        inv = r.inv[i]
        do_a = (r.dot[low, :] * inv[0:1, 0 : p.rows]).astype(BF16)
        do_b = (r.dot[high, :] * inv[0:1, p.rows :]).astype(BF16)
        r.dofull[0 : p.head, 0 : p.rows] = do_a
        r.dofull[p.head : p.pair, p.rows :] = do_b
        inner = jnp.concatenate(
            [
                col_sum(do_a.astype(F32) * r.ot[low, :]),
                col_sum(do_b.astype(F32) * r.ot[high, :]),
            ],
            axis=1,
        )
        rough = (-inner).astype(BF16).astype(F32)
        row = iota((16, 2 * p.rows), 0)
        r.dofull[128:144, :] = jnp.where(
            row == 0, rough, jnp.where(row == 1, -inner - rough, 0.0)
        ).astype(BF16)
        r.vfull[:, 0:128] = r.v[:, lanes]
        fill_pair(p, r.qfull, r.qt, i)
        lanes_v = pl.ds(pl.multiple_of(w + i * p.pair, p.pair), p.pair)
        half = p.tree // 2
        for c in range(2):
            at = slice(c * half, (c + 1) * half)
            dp = nn(r.vfull[at, :], r.dofull[...])
            e = r.e[i, at, :]
            ds = (e.astype(F32) * dp).astype(BF16)
            r.ds[at, :] = ds
            r.dkv[at, lanes] = (nt(ds, r.qfull[0:128, :]) * LN2).astype(BF16)
            r.dkv[at, lanes_v] = nt(e, r.dofull[0:128, :]).astype(BF16)
        dq = nn(r.vt[lanes, :], r.ds[...]) * (p.head**-0.5)
        r.dqt[low, :] = dq[0 : p.head, 0 : p.rows].astype(BF16)
        r.dqt[high, :] = dq[p.head : p.pair, p.rows :].astype(BF16)


def back_to_input(p, m, z, r, back):
    w = p.width
    r.dq[...] = r.dqt[...].T
    r.gstate[m] += nt(r.dq[...], r.wa[:, 0:w])

    @pl.when(m >= 2)
    def _():
        back.left(m - 2)

    @pl.loop(0, p.n_z)
    def _(b):
        at = pl.ds(pl.multiple_of(b * p.rows, p.rows), p.rows)
        dh = nt(r.dkv[at, :], r.wa[:, w : 3 * w])
        r.dh[lax.rem(m, 2), b] = dh.astype(BF16)

        @pl.when(z == b)
        def _():
            r.gstate[m] += dh

    back.step(m, 0)


def input_gradients(p, z, r):
    w = p.width
    own = pl.ds(pl.multiple_of(z * p.rows, p.rows), p.rows)
    r.ga[:, 0:w] += tn(r.h[own, :], r.dq[...])
    for j in range(2):
        at = slice(j * w, (j + 1) * w)
        to = slice((1 + j) * w, (2 + j) * w)
        r.ga[:, to] += tn(r.h[...], r.dkv[0 : p.tree, at])


def remote(src, dst, send, recv, device):
    return pltpu.make_async_remote_copy(
        src_ref=src,
        dst_ref=dst,
        send_sem=send,
        recv_sem=recv,
        device_id=device,
        device_id_type=MESH,
    )


class Back:
    def __init__(self, p, dp, z, r):
        self.p, self.dp, self.z, self.r = p, dp, z, r
        self.last = p.n_z - 1

    def _copy(self, m, k, way, sender):
        r = self.r
        block = sender + way * (self.last - k)
        slot = block + 1 if way == 1 else block
        line = 0 if way == 1 else 1
        return remote(
            r.dh.at[lax.rem(m, 2), block],
            r.dh_in.at[m, slot],
            r.back_send.at[m, line, k],
            r.back_recv.at[m, line, k],
            (self.dp, sender + way),
        ), block, slot

    def _place(self, way):
        return self.z if way == 1 else self.last - self.z

    def step(self, m, k):
        r = self.r
        for way in (1, -1):
            place = self._place(way)
            if k == self.last:

                @pl.when(place > 0)
                def _():
                    copy, _, slot = self._copy(m, k - 1, way, self.z - way)
                    copy.wait_recv()
                    r.gstate[m] += r.dh_in[m, slot].astype(F32)

                continue

            @pl.when((place <= k) & (place < self.last))
            def _():
                if k:

                    @pl.when(place > 0)
                    def _():
                        copy, block, slot = self._copy(m, k - 1, way, self.z - way)
                        copy.wait_recv()
                        own = r.dh.at[lax.rem(m, 2), block]
                        own[...] = (
                            own[...].astype(F32) + r.dh_in[m, slot].astype(F32)
                        ).astype(BF16)

                self._copy(m, k, way, self.z)[0].start()

    def left(self, m):
        for way in (1, -1):
            place = self._place(way)
            for k in range(self.last):

                @pl.when((place <= k) & (place < self.last))
                def _():
                    self._copy(m, k, way, self.z)[0].wait_send()


class Copy:
    def __init__(self, flow, out, into=None, go=None, come=None):
        self.flow, self.out, self.into = flow, out, into or out
        self.go, self.come = go, come
        self.at = flow.used
        self.open = False
        flow.used += 1
        flow.copies.append(self)

    def _run(self, when, step):
        if when is None:
            step()
        else:
            pl.when(when())(step)

    def _make(self, ends):
        src, dst, device = ends()
        return remote(src, dst, self.flow.send.at[self.at], self.flow.recv.at[self.at], device)

    def start(self):
        self.open = True
        self._run(self.go, lambda: self._make(self.out).start())
        return self

    def arrived(self):
        self._run(self.come, lambda: self._make(self.into).wait_recv())

    def left(self):
        if self.open:
            self._run(self.go, lambda: self._make(self.out).wait_send())
            self.open = False


class Flow:
    def __init__(self, send, recv):
        self.send, self.recv, self.used, self.copies = send, recv, 0, []

    def finish(self):
        for copy in self.copies:
            copy.left()


class Line:
    def __init__(self, p, block, dp, z, flow):
        self.last = p.n_z - 1
        self.steps = []
        for step in range(p.n_z - 1):
            both = []
            for way in (1, -1):
                both.append(self._copy(p, block, dp, z, flow, step, way))
            self.steps.append(both)

    def _copy(self, p, block, dp, z, flow, step, way):
        place = z if way == 1 else self.last - z

        def out():
            at = block(z - way * step)
            return at, at, (dp, z + way)

        def into():
            at = block(z - way * (step + 1))
            return at, at, (dp, z - way)

        return Copy(
            flow,
            out,
            into,
            go=lambda: (place >= step) & (place < self.last),
            come=lambda: place >= step + 1,
        )

    def step(self, k):
        if k:
            for copy in self.steps[k - 1]:
                copy.arrived()
        if k < len(self.steps):
            for copy in self.steps[k]:
                copy.start()


def rows_of(dp, size):
    return pl.ds(pl.multiple_of(dp * size, size), size)


class Spread:
    def __init__(self, p, piece, dp, z, flow):
        ref, part, c0, c1 = piece
        size = part * p.n_z
        mid = (c0 + c1) // 2 if c1 - c0 >= 256 else c1
        self.split = mid < c1

        def made(block, turn, a, b):
            mine = ref.at[rows_of(block, size), a:b]
            theirs = ref.at[rows_of(flip(block, turn), size), a:b]
            to = (flip(dp, turn), z)
            return Copy(flow, lambda: (mine, mine, to), lambda: (theirs, theirs, to))

        dpx, dpy = flip(dp, 2), flip(dp, 4)
        dpxy = flip(dpx, 4)
        self.first = [made(dp, 2, c0, mid), made(dp, 4, c0, mid), made(dp, 1, c0, c1)]
        self.a3 = made(dpx, 4, c0, mid)
        if self.split:
            self.first += [made(dp, 4, mid, c1), made(dp, 2, mid, c1)]
            self.b3 = made(dpy, 2, mid, c1)
        self.cores = [made(block, 1, c0, c1) for block in (dpx, dpy, dpxy)]

    def start(self):
        for copy in self.first:
            copy.start()

    def middle(self):
        self.first[0].arrived()
        self.a3.start()
        if self.split:
            self.first[3].arrived()
            self.b3.start()
            self.first[4].arrived()
        self.cores[0].start()
        self.first[1].arrived()
        self.cores[1].start()

    def late(self):
        self.a3.arrived()
        if self.split:
            self.b3.arrived()
        self.cores[2].start()

    def end(self):
        self.first[2].arrived()
        for copy in self.cores:
            copy.arrived()


class Reduce:
    def __init__(self, p, g, part, c0, c1, bufs, dp, z, flow):
        self.p, self.g, self.part, self.c0, self.c1 = p, g, part, c0, c1
        self.dp, self.z = dp, z
        self.size = size = part * p.n_z
        self.cols = cols = c1 - c0
        self.mid = mid = cols // 2 if cols >= 256 else cols
        self.split = mid < cols
        self.s1, self.r1, self.r2, self.r3, self.s4, self.r4 = bufs
        s1, r1, r2, r3, s4, r4 = bufs
        x, y, core = (flip(dp, 2), z), (flip(dp, 4), z), (flip(dp, 1), z)
        dpx, dpy = flip(dp, 2), flip(dp, 4)
        self.order = (dp, dpx, dpy, flip(dpx, 4))

        def made(src, dst, to):
            return Copy(flow, lambda: (src, dst, to))

        self.core = made(s1.at[:, 0:cols], r1.at[:, 0:cols], core)
        self.a1 = made(s1.at[0 : 2 * size, 0:mid], r2.at[:, 0:mid], x)
        self.a2 = made(s1.at[0:size, 0:mid], r3.at[:, 0:mid], y)
        if self.split:
            self.b1 = made(s1.at[0 : 2 * size, mid:cols], r2.at[:, mid:cols], y)
            self.b2 = made(s1.at[0:size, mid:cols], r3.at[:, mid:cols], x)
        self.zs = []
        for i in range(1, p.n_z):
            peer = lax.rem(z + i, p.n_z)
            self.zs.append(made(s4.at[i - 1, :, 0:cols], r4.at[i - 1, :, 0:cols], (dp, peer)))

    def _rows(self, block, a, b):
        return self.g.at[rows_of(block, self.size), self.c0 + a : self.c0 + b]

    def _put(self, slot, block, a, b):
        size = self.size
        self.s1[slot * size : (slot + 1) * size, a:b] = self._rows(block, a, b)[...].astype(BF16)

    def _add(self, buf, slot, block, a, b):
        size = self.size
        self._rows(block, a, b)[...] += buf[slot * size : (slot + 1) * size, a:b].astype(F32)

    def core_start(self):
        for k, block in enumerate(self.order):
            self._put(k, flip(block, 1), 0, self.cols)
        self.core.start()

    def core_end(self):
        order, mid, cols = self.order, self.mid, self.cols
        self.core.arrived()
        self.core.left()
        for k, block in ((1, order[1]), (3, order[3])):
            self._add(self.r1, k, block, 0, mid)
        self._put(0, order[1], 0, mid)
        self._put(1, order[3], 0, mid)
        self.a1.start()
        if self.split:
            for k, block in ((2, order[2]), (3, order[3])):
                self._add(self.r1, k, block, mid, cols)
            self._put(0, order[2], mid, cols)
            self._put(1, order[3], mid, cols)
            self.b1.start()
            for k, block in ((0, order[0]), (1, order[1])):
                self._add(self.r1, k, block, mid, cols)
        for k, block in ((0, order[0]), (2, order[2])):
            self._add(self.r1, k, block, 0, mid)

    def plane_middle(self):
        order, mid, cols = self.order, self.mid, self.cols
        self.a1.arrived()
        self._add(self.r2, 1, order[2], 0, mid)
        self.a1.left()
        self._put(0, order[2], 0, mid)
        self.a2.start()
        self._add(self.r2, 0, order[0], 0, mid)
        if self.split:
            self.b1.arrived()
            self._add(self.r2, 1, order[1], mid, cols)
            self.b1.left()
            self._put(0, order[1], mid, cols)
            self.b2.start()
            self._add(self.r2, 0, order[0], mid, cols)

    def plane_end(self):
        self.a2.arrived()
        if self.split:
            self.b2.arrived()
        self._add(self.r3, 0, self.dp, 0, self.cols)
        p, part = self.p, self.part
        for i in range(1, p.n_z):
            peer = lax.rem(self.z + i, p.n_z)
            self.s4[i - 1, :, 0 : self.cols] = self.g[
                rows_of(self.dp * p.n_z + peer, part), self.c0 : self.c1
            ].astype(BF16)
            self.zs[i - 1].start()

    def total(self):
        p = self.p
        total = self.g[rows_of(self.dp * p.n_z + self.z, self.part), self.c0 : self.c1]
        for i in range(1, p.n_z):
            self.zs[i - 1].arrived()
            total = total + self.r4[i - 1, :, 0 : self.cols].astype(F32)
        return total


def spread_vectors(p, r):
    r.wsf[...] = r.ws[...].astype(F32)

    def spread(k, part, total):
        g = r.wsf[pl.ds(k, p.devices, stride=16), :].astype(BF16)
        lane, column = iota((128, total), 0), iota((128, total), 1)
        place = jnp.where((lane < part) & (lax.rem(column, part) == lane), 1.0, 0.0)
        full = nn(g, place.astype(BF16))
        mine = lax.div(iota((p.devices, total), 1), part) == iota((p.devices, total), 0)
        return col_sum(jnp.where(mine, full, 0.0))

    for k in range(VECTORS):
        r.vec[k : k + 1, :] = spread(k, p.part, p.width)
    r.bup[...] = spread(VECTORS, p.part_h, p.hidden)


def collect_vectors(p, r):
    r.gs[...] = jnp.zeros(r.gs.shape, F32)

    def collect(k, row, part, total):
        mine = lax.div(iota((p.devices, total), 1), part) == iota((p.devices, total), 0)
        full = jnp.where(mine, row, 0.0)
        high = full.astype(BF16)
        rest = (full - high.astype(F32)).astype(BF16)
        lane, column = iota((128, total), 0), iota((128, total), 1)
        place = jnp.where(
            (lane < part) & (lax.rem(column, part) == lane), 1.0, 0.0
        ).astype(BF16)
        r.gs[pl.ds(k, p.devices, stride=16), :] = nt(high, place) + nt(rest, place)

    for k in range(VECTORS):
        collect(k, r.gvec[k : k + 1, :], p.part, p.width)
    collect(VECTORS, r.gbup[...], p.part_h, p.hidden)


class Refs:
    pass


def buffers(r, tag):
    return [getattr(r, tag + str(k)) for k in range(6) if hasattr(r, tag + str(k))]


def targets(p, n, z, r):
    w = p.width
    at = rows_of(n, p.part)
    places = {}
    if p.fused:
        places["w_query"] = r.wa.at[at, 0:w]
        places["w_key"] = r.wa.at[at, w : 2 * w]
        places["w_value"] = r.wa.at[at, 2 * w : 3 * w]
        places["w_out"] = r.wa.at[at, 3 * w : 4 * w]
        places["w_up"] = r.wa.at[at, 4 * w :]
        places["w_down"] = r.wd.at[rows_of(n, p.part_h), :]
    places["state"] = r.states.at[:, z]
    return places


def place_vectors(p, n, r):
    r.small[...] = jnp.zeros((16, 128), F32)
    for k, name in enumerate(SMALL):
        r.small[k : k + 1, 0 : p.part] = getattr(r, name)[...].astype(F32)
    r.small[VECTORS : VECTORS + 1, 0 : p.part_h] = r.b_up[...].astype(F32)
    r.ws[rows_of(n, 16), :] = r.small[...].astype(BF16)


def clear(p, r):
    r.ga[...] = jnp.zeros(r.ga.shape, F32)
    r.gd[...] = jnp.zeros(r.gd.shape, F32)
    r.gvec[...] = jnp.zeros(r.gvec.shape, F32)
    r.gbup[...] = jnp.zeros(r.gbup.shape, F32)
    r.qfull[...] = jnp.zeros(r.qfull.shape, BF16)
    r.dofull[...] = jnp.zeros(r.dofull.shape, BF16)
    r.vo[128:144, :] = jnp.ones((16, p.tree), BF16)
    lane = iota((p.tree, 128), 1)
    r.vfull[:, 128:256] = jnp.where(lane < 2, 1.0, 0.0).astype(BF16)


def kernel(p, names, given, results, *refs):
    r = Refs()
    for name, ref in zip(names, refs):
        setattr(r, name, ref)
    dp = lax.axis_index("dp")
    z = lax.axis_index("fsdp")
    w = p.width
    places = targets(p, dp * p.n_z + z, z, r)
    loads = {}
    for k, name in enumerate(given):
        place = places.get(name, getattr(r, name, None))
        copy = pltpu.make_async_copy(getattr(r, "hbm_" + name), place, r.load_sem.at[k])
        loads[name] = copy
    stores = {}
    for k, name in enumerate(results):
        if name == "new_state":
            continue
        stores[name] = pltpu.make_async_copy(
            getattr(r, name), getattr(r, "hbm_" + name), r.store_sem.at[k]
        )
    flow = Flow(r.send_sem, r.recv_sem)

    barrier = pltpu.get_barrier_semaphore()
    peers = [(dp, lax.rem(z + i, p.n_z)) for i in range(1, p.n_z)]
    if p.fused:
        peers += [(flip(dp, bit), z) for bit in (1, 2, 4)]
    for peer in peers:
        pl.semaphore_signal(barrier, inc=1, device_id=peer, device_id_type=MESH)
    for copy in loads.values():
        copy.start()
    lines = [
        Line(p, lambda b, m=m: r.states.at[m, b], dp, z, flow) for m in range(p.micro)
    ]
    steps = p.n_z - 1
    back = Back(p, dp, z, r)
    if p.fused:
        parts = (
            (r.wa, p.part, 0, 3 * w),
            (r.ws, 16, 0, 128),
            (r.wa, p.part, 3 * w, p.cols),
            (r.wd, p.part_h, 0, w),
        )
        rods = []
        for ref, part, c0, c1 in parts:

            def block(b, ref=ref, part=part, c0=c0, c1=c1):
                return ref.at[rows_of(dp * p.n_z + b, part), c0:c1]

            rods.append(Line(p, block, dp, z, flow))
        spreads = [Spread(p, piece, dp, z, flow) for piece in parts]
        sums = [
            Reduce(p, r.ga, p.part, 3 * w, p.cols, buffers(r, "f"), dp, z, flow),
            Reduce(p, r.gd, p.part_h, 0, w, [r.k] + buffers(r, "d"), dp, z, flow),
            Reduce(p, r.gs, 16, 0, 128, buffers(r, "e"), dp, z, flow),
            Reduce(p, r.ga, p.part, 0, 3 * w, [r.q0] + buffers(r, "b"), dp, z, flow),
        ]
    for copy in loads.values():
        copy.wait()
    if p.fused:
        place_vectors(p, dp * p.n_z + z, r)
    pl.semaphore_wait(barrier, len(peers))

    if p.fused:
        for rod in rods:
            rod.step(0)
        make_signal(p, r)
        for k in range(1, steps):
            for rod in rods:
                rod.step(k)
            lines[0].step(k - 1)
            if k == 1:
                clear(p, r)
        for rod, spread in zip(rods, spreads):
            rod.step(steps)
            spread.start()
        lines[0].step(steps - 1)
        for spread in spreads:
            spread.middle()
        spreads[0].late()
        spreads[0].end()
        lines[0].step(steps)
        if p.micro > 1:
            lines[1].step(0)
    else:
        for k in range(steps + 1):
            for line in lines:
                line.step(k)
        make_signal(p, r)
        clear(p, r)

    @pl.loop(0, p.micro)
    def _(m):
        if p.fused:
            for k in range(1, p.micro):

                @pl.when(m == k)
                def _(k=k):
                    lines[k].step(steps)

        prepare_micro(p, m, z, r)
        if p.fused:

            @pl.when(m == 0)
            def _():
                for spread in spreads[1:]:
                    spread.late()

        attention_forward(p, r)

        @pl.when(m > 0)
        def _():
            for k in range(1, steps - 1):
                back.step(m - 1, k)

        if p.fused:

            @pl.when(m == 1)
            def _():
                for line in lines[2:]:
                    line.step(steps - 1)

            @pl.when(m == 0)
            def _():
                if p.micro > 1:
                    for k in range(1, steps - 1):
                        lines[1].step(k)
                for spread in spreads[1:]:
                    spread.end()
                spread_vectors(p, r)

        def between():
            if p.fused:

                @pl.when(m == 0)
                def _():
                    for line in lines[2:]:
                        line.step(0)

        transition(p, m, z, r, between)

        @pl.when(m > 0)
        def _():
            back.step(m - 1, steps - 1)

        out = pltpu.make_async_copy(
            r.new_state.at[m], r.hbm_new_state.at[m], r.state_sem.at[m]
        )
        out.start()
        if p.fused and p.micro > 1:

            @pl.when(m == 0)
            def _():
                lines[1].step(steps - 1)

        r.vt[...] = r.k[...].T
        if p.fused:

            @pl.when(m == p.micro - 1)
            def _():
                sums[0].core_start()
                sums[1].core_start()
                collect_vectors(p, r)
                sums[2].core_start()

        def inside(i):
            if p.fused:

                @pl.when((m == p.micro - 1) & (i == p.pairs // 2))
                def _():
                    for one in sums[:3]:
                        one.core_end()

        attention_backward(p, r, inside)
        if p.fused:

            @pl.when(m == 0)
            def _():
                for line in lines[2:]:
                    for k in range(1, steps - 1):
                        line.step(k)


        @pl.when(m > 0)
        def _():
            back.step(m - 1, steps)

        back_to_input(p, m, z, r, back)
        input_gradients(p, z, r)

    if p.fused:
        sums[3].core_start()
        for one in sums[:3]:
            one.plane_middle()
        sums[3].core_end()
        back.step(p.micro - 1, 1)
        for one in sums[:3]:
            one.plane_end()
        back.step(p.micro - 1, 2)
        sums[3].plane_middle()
        sums[3].plane_end()
        for k in range(3, steps + 1):
            back.step(p.micro - 1, k)
        total = sums[0].total()
        r.g_out[...] = total[:, 0:w]
        r.g_up[...] = total[:, w:]
        r.g_down[...] = sums[1].total()
        r.small[...] = sums[2].total()
        for k, name in enumerate(SMALL):
            getattr(r, "g_" + name)[...] = r.small[k : k + 1, 0 : p.part]
        r.g_b_up[...] = r.small[VECTORS : VECTORS + 1, 0 : p.part_h]
        total = sums[3].total()
        r.g_query[...] = total[:, 0:w]
        r.g_key[...] = total[:, w : 2 * w]
        r.g_value[...] = total[:, 2 * w : 3 * w]
    else:
        for k in range(1, steps + 1):
            back.step(p.micro - 1, k)
    for m in range(max(p.micro - 2, 0), p.micro):
        back.left(m)
    for copy in stores.values():
        copy.start()
    for m in range(p.micro):
        pltpu.make_async_copy(
            r.new_state.at[m], r.hbm_new_state.at[m], r.state_sem.at[m]
        ).wait()
    for copy in stores.values():
        copy.wait()
    flow.finish()


def run_kernel(p, inputs):
    w, t, rows = p.width, p.tree, p.rows
    outs = {
        "new_state": ((p.micro, rows, w), BF16),
        "new_halting": ((p.micro, rows), F32),
        "new_ponder": ((p.micro, rows), F32),
        "gstate": ((p.micro, rows, w), F32),
    }
    scratch = {}
    if p.fused:
        for name in ("query", "key", "value", "out"):
            outs["g_" + name] = ((p.part, w), F32)
        outs["g_up"] = ((p.part, p.hidden), F32)
        outs["g_down"] = ((p.part_h, w), F32)
        for name in SMALL:
            outs["g_" + name] = ((1, p.part), F32)
        outs["g_b_up"] = ((1, p.part_h), F32)
        scratch.update(
            wa=((w, p.cols), BF16),
            wd=((p.hidden, w), BF16),
            ws=((p.devices * 16, 128), BF16),
            wsf=((p.devices * 16, 128), F32),
            small=((16, 128), F32),
            vec=((8, w), F32),
            bup=((1, p.hidden), F32),
            ga=((w, p.cols), F32),
            gd=((p.hidden, w), F32),
            gs=((p.devices * 16, 128), F32),
            gvec=((8, w), F32),
            gbup=((1, p.hidden), F32),
        )
        kinds = (
            ("f", p.part, p.cols - 3 * w),
            ("b", p.part, 3 * w),
            ("d", p.part_h, w),
            ("e", 16, 128),
        )
        for tag, part, cols in kinds:
            size = part * p.n_z
            shapes = [(k * size, cols) for k in (4, 4, 2, 1)]
            shapes += [(p.n_z - 1, part, cols)] * 2
            for k, shape in enumerate(shapes):
                if k or tag in "fe":
                    scratch[tag + str(k)] = (shape, BF16)
        scratch["q0"] = ((4 * p.part * p.n_z, 3 * w), BF16)
    else:
        outs.update(
            ga=((w, p.cols), F32),
            gd=((p.hidden, w), F32),
            gvec=((8, w), F32),
            gbup=((1, p.hidden), F32),
        )
    scratch.update(
        states=((p.micro, p.n_z, rows, w), BF16),
        near=((rows, w), F32),
        far=((8, w), F32),
        h=((t, w), BF16),
        k=((t, w), BF16),
        v=((t, w), BF16),
        vt=((w, t), BF16),
        qt=((w, rows), BF16),
        kfull=((t, 256), BF16),
        qfull=((256, 2 * rows), BF16),
        vfull=((t, 256), BF16),
        dofull=((256, 2 * rows), BF16),
        vo=((144, t), BF16),
        e=((p.pairs, t, 2 * rows), BF16),
        s=((t, 2 * rows), F32),
        top=((8, 2 * rows), F32),
        pre=((2, rows, w // 2), F32),
        inv=((p.pairs, 8, 2 * rows), F32),
        ot=((w, rows), F32),
        otb=((w, rows), BF16),
        dot=((w, rows), F32),
        xh1=((rows, w), F32),
        u=((rows, w), BF16),
        acc=((rows, w), F32),
        dg=((rows, w), BF16),
        ds=((t, 2 * rows), BF16),
        dkv=((max(t, rows * (p.hidden // w)), 2 * w), BF16),
        dqt=((w, rows), BF16),
        dq=((rows, w), BF16),
        dh=((2, p.n_z, rows, w), BF16),
        dh_in=((p.micro, p.n_z + 1, rows, w), BF16),
    )
    direct = ("w_query", "w_key", "w_value", "w_out", "w_up", "w_down", "state")
    for name, value in inputs.items():
        if not (name == "state" or (p.fused and name in direct)):
            scratch[name] = (value.shape, value.dtype)
    scratch.update(outs)
    hbm = pl.BlockSpec(memory_space=pl.ANY)
    copies = 128
    names = (
        ["hbm_" + name for name in inputs]
        + ["hbm_" + name for name in outs]
        + list(scratch)
        + ["send_sem", "recv_sem", "back_send", "back_recv"]
        + ["load_sem", "store_sem", "state_sem"]
    )
    results = pl.pallas_call(
        functools.partial(kernel, p, names, list(inputs), list(outs)),
        out_shape=[jax.ShapeDtypeStruct(s, d) for s, d in outs.values()],
        in_specs=[hbm] * len(inputs),
        out_specs=[hbm] * len(outs),
        scratch_shapes=[pltpu.VMEM(s, d) for s, d in scratch.values()]
        + [pltpu.SemaphoreType.DMA((copies,))] * 2
        + [pltpu.SemaphoreType.DMA((p.micro, 2, p.n_z - 1))] * 2
        + [
            pltpu.SemaphoreType.DMA((len(inputs),)),
            pltpu.SemaphoreType.DMA((len(outs),)),
            pltpu.SemaphoreType.DMA((p.micro,)),
        ],
        compiler_params=pltpu.CompilerParams(
            collective_id=0, has_side_effects=True, vmem_limit_bytes=127 << 19
        ),
        name="layer",
    )(*inputs.values())
    return dict(zip(outs, results))


def hand_over(values):
    def body(*refs):
        count = len(values)
        held, sems = refs[2 * count : 3 * count], refs[3 * count :]
        taken = [
            pltpu.make_async_copy(refs[k], held[k], sems[0].at[k]) for k in range(count)
        ]
        given = [
            pltpu.make_async_copy(held[k], refs[count + k], sems[1].at[k])
            for k in range(count)
        ]
        for copy in taken:
            copy.start()
        for old, new in zip(taken, given):
            old.wait()
            new.start()
        for copy in given:
            copy.wait()

    hbm = pl.BlockSpec(memory_space=pl.ANY)
    moved = pl.pallas_call(
        body,
        out_shape=[jax.ShapeDtypeStruct(v.shape, v.dtype) for v in values.values()],
        in_specs=[hbm] * len(values),
        out_specs=[hbm] * len(values),
        scratch_shapes=[pltpu.VMEM(v.shape, v.dtype) for v in values.values()]
        + [pltpu.SemaphoreType.DMA((len(values),))] * 2,
        name="hand_over",
    )(*values.values())
    return dict(zip(values, moved))


WEIGHTS = (
    "w_query",
    "w_key",
    "w_value",
    "w_out",
    "w_up",
    "b_up",
    "w_down",
    "b_down",
    "gain_one",
    "bias_one",
    "gain_two",
    "bias_two",
    "w_halt",
)


def per_device(state, segment, parent, halting, ponder, cot_state, cot_halt, *weights):
    micro, rows, width = state.shape
    given = dict(zip(WEIGHTS, weights))
    n_dp, n_z = lax.axis_size("dp"), lax.axis_size("fsdp")
    part, hidden = given["w_query"].shape[0], given["w_up"].shape[1]
    fused = n_dp == 8 and part % 16 == 0 and part <= 128
    p = Plan(micro, rows, width, hidden, parent.shape[2], n_dp, n_z, fused)
    inputs = dict(
        state=state,
        seg=segment,
        parent=parent,
        halting=halting,
        ponder=ponder,
        cot=cot_state,
        cot_halt=cot_halt,
    )
    if fused:
        for name, value in given.items():
            inputs[name] = value if value.ndim == 2 else value.reshape(1, -1)
        out = hand_over(run_kernel(p, inputs))
        grads = []
        for name in WEIGHTS:
            value = out["g_" + name[2:]] if name.startswith("w_") and name != "w_halt" else out["g_" + name]
            grads.append(value.reshape(given[name].shape))
    else:
        axes = ("dp", "fsdp")
        full = {k: lax.all_gather(v, axes, axis=0, tiled=True) for k, v in given.items()}
        inputs["wa"] = jnp.concatenate([full[k] for k in WEIGHTS[:5]], axis=1)
        inputs["wd"] = full["w_down"]
        rows_f32 = [full[k].astype(F32) for k in WEIGHTS[7:]]
        rows_f32 += [jnp.zeros((width,), F32)] * 2
        inputs["vec"] = jnp.stack(rows_f32)
        inputs["bup"] = full["b_up"].astype(F32).reshape(1, -1)
        out = run_kernel(p, inputs)
        whole = [out["ga"][:, k * width : (k + 1) * width] for k in range(4)]
        whole += [out["ga"][:, 4 * width :], out["gbup"][0], out["gd"]]
        whole += [out["gvec"][k] for k in range(VECTORS)]
        grads = [
            lax.psum_scatter(g, axes, scatter_dimension=0, tiled=True) for g in whole
        ]
    return (out["new_state"], out["new_halting"], out["new_ponder"], out["gstate"], *grads)


def solution(mesh):
    tokens, flags = P(None, ("dp", "fsdp"), None), P(None, ("dp", "fsdp"))
    matrix, vector = P(("dp", "fsdp"), None), P(("dp", "fsdp"))
    weights = tuple(
        matrix if name in ("w_query", "w_key", "w_value", "w_out", "w_up", "w_down") else vector
        for name in WEIGHTS
    )
    return jax.shard_map(
        per_device,
        mesh=mesh,
        in_specs=(tokens, P(None, "dp"), P(None, "dp", None), flags, flags, tokens, flags)
        + weights,
        out_specs=(tokens, flags, flags, tokens) + weights,
        check_vma=False,
    )
```

```python
import functools
import math

import jax
import jax.numpy as jnp
from jax import lax
from jax.experimental import pallas as pl
from jax.experimental.pallas import tpu as pltpu
from jax.sharding import PartitionSpec as P

HEADS = 8
EPS = 1e-06
HALT_LIMIT = 0.99
GELU_C = math.sqrt(2.0 / math.pi)
GELU_A = 0.044715
LOG2E = 1.0 / math.log(2.0)
LN2 = math.log(2.0)
BIG = 2.0**100
F32 = jnp.float32
BF16 = jnp.bfloat16
MESH = pl.DeviceIdType.MESH
SMALL = ("b_down", "gain_one", "bias_one", "gain_two", "bias_two", "w_halt")
VECTORS = len(SMALL)


def nn(a, b):
    return lax.dot_general(a, b, (((1,), (0,)), ((), ())), preferred_element_type=F32)


def nt(a, b):
    return lax.dot_general(a, b, (((1,), (1,)), ((), ())), preferred_element_type=F32)


def tn(a, b):
    return lax.dot_general(a, b, (((0,), (0,)), ((), ())), preferred_element_type=F32)


def iota(shape, axis):
    return lax.broadcasted_iota(jnp.int32, shape, axis)


def split_at(values, size):
    if size & (size - 1) == 0:
        return values >> (size.bit_length() - 1), values & (size - 1)
    return lax.div(values, size), lax.rem(values, size)


def flip(index, bit):
    return index + bit - 2 * bit * lax.rem(lax.div(index, bit), 2)


def col_sum(values):
    return jnp.sum(values, axis=0, keepdims=True)


def norm(values):
    centered = values - jnp.mean(values, axis=-1, keepdims=True)
    inv = lax.rsqrt(jnp.mean(centered * centered, axis=-1, keepdims=True) + EPS)
    return centered * inv, inv


def norm_back(grad, normal, inv):
    return inv * (
        grad
        - jnp.mean(grad, axis=-1, keepdims=True)
        - normal * jnp.mean(grad * normal, axis=-1, keepdims=True)
    )


class Plan:
    def __init__(self, micro, rows, width, hidden, segs, n_dp, n_z, fused):
        self.micro, self.rows, self.width, self.hidden = micro, rows, width, hidden
        self.segs, self.n_dp, self.n_z, self.fused = segs, n_dp, n_z, fused
        self.tree = rows * n_z
        self.head = width // HEADS
        self.pair = 2 * self.head
        self.pairs = HEADS // 2
        self.cols = 4 * width + hidden
        self.devices = n_dp * n_z
        self.part = width // self.devices
        self.part_h = hidden // self.devices


def make_signal(p, r):
    half = p.width // 2
    freq = jnp.exp((-math.log(10000.0) / half) * iota((1, half), 1).astype(F32))
    far = (iota((8, 1), 0) * p.rows).astype(F32) * freq
    r.far[:, 0:half] = jnp.sin(far)
    r.far[:, half:] = jnp.cos(far)
    step = 32

    @pl.loop(0, p.rows // step)
    def _(i):
        near = (iota((step, 1), 0) + i * step).astype(F32) * freq
        at = pl.ds(pl.multiple_of(i * step, step), step)
        r.near[at, 0:half] = jnp.sin(near)
        r.near[at, half:] = jnp.cos(near)


def signal(p, r, b):
    half = p.width // 2
    far_sin, far_cos = r.far[pl.ds(b, 1), 0:half], r.far[pl.ds(b, 1), half:]
    near_sin, near_cos = r.near[:, 0:half], r.near[:, half:]
    return near_sin * far_cos + near_cos * far_sin, near_cos * far_cos - near_sin * far_sin


def blocked_table(p, parent_row):
    size = 128
    up = jnp.where(
        iota((16, p.segs), 0) == parent_row, 1.0, 0.0
    )
    up = jnp.concatenate([up, jnp.zeros((16, size - p.segs), F32)], axis=1)
    up = jnp.concatenate([up, jnp.zeros((size - 16, size), F32)], axis=0)
    row, column = iota((size, size), 0), iota((size, size), 1)
    reach = jnp.where(row == column, 1.0, up)
    for _ in range(4):
        reach = jnp.minimum(nn(reach.astype(BF16), reach.astype(BF16)), 1.0)
    inside = (row < p.segs) & (column < p.segs)
    return jnp.where(inside & (reach < 0.5), -BIG, 0.0)


def prepare_micro(p, m, z, r):
    table = blocked_table(p, r.parent[m])
    seg_row = r.seg[pl.ds(m, 1), :]
    hot = jnp.where(iota((128, p.tree), 0) == seg_row, 1.0, 0.0)
    r.kfull[:, 128:256] = hot.T.astype(BF16)
    own = pl.ds(pl.multiple_of(z * p.rows, p.rows), p.rows)
    hot = jnp.where(iota((128, p.rows), 0) == r.seg[pl.ds(m, 1), own], 1.0, 0.0)
    feature = nn(table.astype(BF16), hot.astype(BF16)).astype(BF16)
    r.qfull[128:256, 0 : p.rows] = feature
    r.qfull[128:256, p.rows : 2 * p.rows] = feature
    for b in range(p.n_z):
        at = slice(b * p.rows, (b + 1) * p.rows)
        for k, wave in enumerate(signal(p, r, b)):
            lanes = slice(k * (p.width // 2), (k + 1) * (p.width // 2))
            r.h[at, lanes] = (r.states[m, b, :, lanes].astype(F32) + wave).astype(BF16)

    w = p.width
    half = p.tree // 2
    for c in range(2):
        at = slice(c * half, (c + 1) * half)
        r.k[at, :] = nn(r.h[at, :], r.wa[:, w : 2 * w]).astype(BF16)
        r.v[at, :] = nn(r.h[at, :], r.wa[:, 2 * w : 3 * w]).astype(BF16)
    r.vt[...] = r.v[...].T
    q = nn(r.h[own, :], r.wa[:, 0:w]) * (LOG2E * p.head**-0.5)
    r.qt[...] = q.astype(BF16).T


def fill_pair(p, full, flat, i):
    low = pl.ds(pl.multiple_of(i * p.pair, p.pair), p.head)
    high = pl.ds(pl.multiple_of(i * p.pair + p.head, p.head), p.head)
    full[0 : p.head, 0 : p.rows] = flat[low, :].astype(BF16)
    full[p.head : p.pair, p.rows : 2 * p.rows] = flat[high, :].astype(BF16)


def attention_forward(p, r):
    step = p.tree // 8

    def ready(i):
        r.kfull[:, 0:128] = r.k[:, pl.ds(pl.multiple_of(i * p.pair, p.pair), p.pair)]
        fill_pair(p, r.qfull, r.qt, i)

    def scores(c, top):
        at = slice(c * step, (c + 1) * step)
        s = nn(r.kfull[at, :], r.qfull[...])
        r.s[at, :] = s
        own = jnp.max(s.reshape(step // 8, 8, 2 * p.rows), axis=0)
        return own if top is None else jnp.maximum(top, own)

    def soften(i, c, top):
        at = slice(c * step, (c + 1) * step)
        r.e[i, at, :] = jnp.exp2(r.s[at, :] - top).astype(BF16)

    def finish(i):
        lanes = pl.ds(pl.multiple_of(i * p.pair, p.pair), p.pair)
        r.vo[0:128, :] = r.vt[lanes, :]
        o = nn(r.vo[...], r.e[i])
        inv = 1.0 / o[128:136]
        r.inv[i] = inv
        low = pl.ds(pl.multiple_of(i * p.pair, p.pair), p.head)
        high = pl.ds(pl.multiple_of(i * p.pair + p.head, p.head), p.head)
        r.ot[low, :] = o[0 : p.head, 0 : p.rows] * inv[0:1, 0 : p.rows]
        r.ot[high, :] = o[p.head : p.pair, p.rows :] * inv[0:1, p.rows :]

    ready(0)
    top = None
    for c in range(8):
        top = scores(c, top)
    r.top[...] = top

    @pl.loop(0, p.pairs - 1)
    def _(i):
        ready(i + 1)
        top = jnp.max(r.top[...], axis=0, keepdims=True)
        later = None
        for c in range(8):
            soften(i, c, top)
            later = scores(c, later)
        r.top[...] = later
        finish(i)

    top = jnp.max(r.top[...], axis=0, keepdims=True)
    for c in range(8):
        soften(p.pairs - 1, c, top)
    finish(p.pairs - 1)


def transition(p, m, z, r, between, down_done, up_done):
    w = p.width
    rows = p.rows
    vec = lambda k: r.vec[k : k + 1, :]
    gain_a, bias_a, gain_b, bias_b, halt_vec = vec(1), vec(2), vec(3), vec(4), vec(5)
    w_out = slice(3 * w, 4 * w)

    lane = iota((128, rows), 0)
    packed = jnp.where(
        lane == 0,
        r.halting[pl.ds(m, 1), :],
        jnp.where(lane == 1, r.ponder[pl.ds(m, 1), :], r.cot_halt[pl.ds(m, 1), :]),
    ).T
    halting, ponder, cot_halt = packed[:, 0:1], packed[:, 1:2], packed[:, 2:3]

    r.otb[...] = r.ot[...].astype(BF16)
    state = r.states[m, z].astype(F32)
    y1 = state + jnp.concatenate(signal(p, r, z), axis=1) + tn(r.otb[...], r.wa[:, w_out])
    xh1, inv1 = norm(y1)
    n1 = xh1 * gain_a + bias_a
    r.xh1[...] = xh1
    r.u[...] = n1.astype(BF16)
    r.acc[...] = n1

    wide = w // 2
    count = p.hidden // wide

    def expand(c):
        r.pre[c % 2] = (
            nn(r.u[...], r.wa[:, 4 * w + c * wide : 4 * w + (c + 1) * wide])
            + r.bup[:, c * wide : (c + 1) * wide]
        )

    def bend(c):
        block = slice((c // 2) * rows, (c // 2 + 1) * rows)
        off = (c % 2) * wide
        pre = r.pre[c % 2]
        square = pre * pre
        t = jnp.tanh(pre * (GELU_C + (GELU_C * GELU_A) * square))
        half = 0.5 + 0.5 * t
        r.dkv[block, off : off + wide] = (pre * half).astype(BF16)
        slope = half + (0.5 * pre) * (1.0 - t * t) * (
            GELU_C + (3.0 * GELU_A * GELU_C) * square
        )
        r.dkv[block, w + off : w + off + wide] = slope.astype(BF16)

    def shrink(c):
        block = slice((c // 2) * rows, (c // 2 + 1) * rows)
        off = (c % 2) * wide
        r.acc[...] += nn(
            r.dkv[block, off : off + wide], r.wd[c * wide : (c + 1) * wide, :]
        )

    expand(0)
    for c in range(count):
        if c + 1 < count:
            expand(c + 1)
        bend(c)
        if c:
            shrink(c - 1)
    shrink(count - 1)

    between()
    y2 = r.acc[...] + vec(0)
    xh2, inv2 = norm(y2)
    s2 = xh2 * gain_b + bias_b
    ph = jax.nn.sigmoid(jnp.sum(s2 * halt_vec, axis=1, keepdims=True))
    run = jnp.where(halting < HALT_LIMIT, 1.0, 0.0)
    room = run * (1.0 - halting)
    weight = room * ph
    state = r.states[m, z].astype(F32)
    r.new_state[m] = (weight * s2 + (1.0 - weight) * state).astype(BF16)
    lane = iota((rows, 128), 1)
    packed = jnp.where(
        lane == 0, halting + weight, ponder + run * (1.0 - weight)
    ).T
    r.new_halting[pl.ds(m, 1), :] = packed[0:1, :]
    r.new_ponder[pl.ds(m, 1), :] = packed[1:2, :]

    cot = r.cot[m].astype(F32)
    dw = jnp.sum(cot * (s2 - state), axis=1, keepdims=True) + cot_halt
    dl = dw * room * ph * (1.0 - ph)
    ds2 = weight * cot + dl * halt_vec
    r.gvec[5:6, :] += col_sum(dl * s2)
    r.gvec[3:4, :] += col_sum(ds2 * xh2)
    r.gvec[4:5, :] += col_sum(ds2)
    dy2 = norm_back(ds2 * gain_b, xh2, inv2)
    r.gvec[0:1, :] += col_sum(dy2)
    r.dg[...] = dy2.astype(BF16)
    r.acc[...] = dy2
    r.gstate[m] = (1.0 - weight) * cot

    for j in range(p.hidden // w):
        at = slice(j * w, (j + 1) * w)
        block = slice(j * rows, (j + 1) * rows)
        r.gd[at, :] += tn(r.dkv[block, 0:w], r.dg[...])
        down_done(j)
    for j in range(p.hidden // w):
        at = slice(j * w, (j + 1) * w)
        at_up = slice((4 + j) * w, (5 + j) * w)
        block = slice(j * rows, (j + 1) * rows)
        dz = nt(r.dg[...], r.wd[at, :]) * r.dkv[block, w : 2 * w].astype(F32)
        r.gbup[:, at] += col_sum(dz)
        dzb = dz.astype(BF16)
        r.acc[...] += nt(dzb, r.wa[:, at_up])
        r.ga[:, at_up] += tn(r.u[...], dzb)
        up_done(j)

    dn1 = r.acc[...]
    xh1 = r.xh1[...]
    r.gvec[1:2, :] += col_sum(dn1 * xh1)
    r.gvec[2:3, :] += col_sum(dn1)
    dy1 = norm_back(dn1 * gain_a, xh1, inv1)
    r.gstate[m] += dy1
    da = dy1.astype(BF16)
    r.ga[:, w_out] += nn(r.otb[...], da)
    r.dot[...] = nt(r.wa[:, w_out], da)


def attention_backward(p, m, z, r, back, inside):
    w = p.width
    size = p.tree // 2

    @pl.when(m >= 2)
    def _():
        back.left(m - 2)

    def ready(i):
        low = slice(i * p.pair, i * p.pair + p.head)
        high = slice(i * p.pair + p.head, (i + 1) * p.pair)
        inv = r.inv[i]
        full, q = r.dofull.at[i % 2], r.qpair.at[i % 2]
        do_a = (r.dot[low, :] * inv[0:1, 0 : p.rows]).astype(BF16)
        do_b = (r.dot[high, :] * inv[0:1, p.rows :]).astype(BF16)
        full[0 : p.head, 0 : p.rows] = do_a
        full[p.head : p.pair, p.rows :] = do_b
        inner = jnp.concatenate(
            [
                col_sum(do_a.astype(F32) * r.ot[low, :]),
                col_sum(do_b.astype(F32) * r.ot[high, :]),
            ],
            axis=1,
        )
        rough = (-inner).astype(BF16).astype(F32)
        row = iota((16, 2 * p.rows), 0)
        full[128:144, :] = jnp.where(
            row == 0, rough, jnp.where(row == 1, -inner - rough, 0.0)
        ).astype(BF16)
        q[0 : p.head, 0 : p.rows] = r.qt[low, :]
        q[p.head : p.pair, p.rows :] = r.qt[high, :]

    ready(0)
    for i in range(p.pairs):
        inside(i)
        lanes = slice(i * p.pair, (i + 1) * p.pair)
        lanes_v = slice(w + i * p.pair, w + (i + 1) * p.pair)
        r.vfull[:, 0:128] = r.v[:, lanes]
        total = None
        for c in range(2):
            at = slice(c * size, (c + 1) * size)
            dp = nn(r.vfull[at, :], r.dofull[i % 2])
            if c == 0 and i + 1 < p.pairs:
                ready(i + 1)
            e = r.e[i, at, :]
            ds = (e.astype(F32) * dp).astype(BF16)
            r.ds[c] = ds
            r.dkv[at, lanes] = (nt(ds, r.qpair[i % 2]) * LN2).astype(BF16)
            r.dkv[at, lanes_v] = nt(e, r.dofull[i % 2, 0:128, :]).astype(BF16)
            part = nn(r.vt[lanes, at], r.ds[c])
            total = part if total is None else total + part
        dq = (total * (p.head**-0.5)).astype(BF16)
        r.dqt[i * p.pair : i * p.pair + p.head, :] = dq[0 : p.head, 0 : p.rows]
        r.dqt[i * p.pair + p.head : (i + 1) * p.pair, :] = dq[p.head : p.pair, p.rows :]

    for b in range(p.n_z):
        at = slice(b * p.rows, (b + 1) * p.rows)
        dh = nt(r.dkv[at, :], r.wa[:, w : 3 * w])
        r.dh[lax.rem(m, 2), b] = dh.astype(BF16)

        @pl.when(z == b)
        def _():
            r.gstate[m] += dh

    back.step(m, 0)
    r.dq[...] = r.dqt[...].T
    r.gstate[m] += nt(r.dq[...], r.wa[:, 0:w])


def input_gradients(p, z, r):
    w = p.width
    own = pl.ds(pl.multiple_of(z * p.rows, p.rows), p.rows)
    r.ga[:, 0:w] += tn(r.h[own, :], r.dq[...])
    for j in range(2):
        at = slice(j * w, (j + 1) * w)
        to = slice((1 + j) * w, (2 + j) * w)
        r.ga[:, to] += tn(r.h[...], r.dkv[0 : p.tree, at])


def remote(src, dst, send, recv, device):
    return pltpu.make_async_remote_copy(
        src_ref=src,
        dst_ref=dst,
        send_sem=send,
        recv_sem=recv,
        device_id=device,
        device_id_type=MESH,
    )


class Back:
    def __init__(self, p, dp, z, r):
        self.p, self.dp, self.z, self.r = p, dp, z, r
        self.last = p.n_z - 1

    def _copy(self, m, k, way, sender):
        r = self.r
        block = sender + way * (self.last - k)
        slot = block + 1 if way == 1 else block
        line = 0 if way == 1 else 1
        return remote(
            r.dh.at[lax.rem(m, 2), block],
            r.dh_in.at[m, slot],
            r.back_send.at[m, line, k],
            r.back_recv.at[m, line, k],
            (self.dp, sender + way),
        ), block, slot

    def _place(self, way):
        return self.z if way == 1 else self.last - self.z

    def step(self, m, k):
        r = self.r
        for way in (1, -1):
            place = self._place(way)
            if k == self.last:

                @pl.when(place > 0)
                def _():
                    copy, _, slot = self._copy(m, k - 1, way, self.z - way)
                    copy.wait_recv()
                    r.gstate[m] += r.dh_in[m, slot].astype(F32)

                continue

            @pl.when((place <= k) & (place < self.last))
            def _():
                if k:

                    @pl.when(place > 0)
                    def _():
                        copy, block, slot = self._copy(m, k - 1, way, self.z - way)
                        copy.wait_recv()
                        own = r.dh.at[lax.rem(m, 2), block]
                        own[...] = (
                            own[...].astype(F32) + r.dh_in[m, slot].astype(F32)
                        ).astype(BF16)

                self._copy(m, k, way, self.z)[0].start()

    def left(self, m):
        for way in (1, -1):
            place = self._place(way)
            for k in range(self.last):

                @pl.when((place <= k) & (place < self.last))
                def _():
                    self._copy(m, k, way, self.z)[0].wait_send()


class Copy:
    def __init__(self, flow, out, into=None, go=None, come=None):
        self.flow, self.out, self.into = flow, out, into or out
        self.go, self.come = go, come
        self.at = flow.used
        self.open = False
        flow.used += 1
        flow.copies.append(self)

    def _run(self, when, step):
        if when is None:
            step()
        else:
            pl.when(when())(step)

    def _make(self, ends):
        src, dst, device = ends()
        return remote(src, dst, self.flow.send.at[self.at], self.flow.recv.at[self.at], device)

    def start(self):
        self.open = True
        self._run(self.go, lambda: self._make(self.out).start())
        return self

    def arrived(self):
        self._run(self.come, lambda: self._make(self.into).wait_recv())

    def left(self):
        if self.open:
            self._run(self.go, lambda: self._make(self.out).wait_send())
            self.open = False


class Flow:
    def __init__(self, send, recv):
        self.send, self.recv, self.used, self.copies = send, recv, 0, []

    def finish(self):
        for copy in self.copies:
            copy.left()


class Line:
    def __init__(self, p, block, dp, z, flow):
        self.last = p.n_z - 1
        self.steps = []
        for step in range(p.n_z - 1):
            both = []
            for way in (1, -1):
                both.append(self._copy(p, block, dp, z, flow, step, way))
            self.steps.append(both)

    def _copy(self, p, block, dp, z, flow, step, way):
        place = z if way == 1 else self.last - z

        def out():
            at = block(z - way * step)
            return at, at, (dp, z + way)

        def into():
            at = block(z - way * (step + 1))
            return at, at, (dp, z - way)

        return Copy(
            flow,
            out,
            into,
            go=lambda: (place >= step) & (place < self.last),
            come=lambda: place >= step + 1,
        )

    def step(self, k):
        if k:
            for copy in self.steps[k - 1]:
                copy.arrived()
        if k < len(self.steps):
            for copy in self.steps[k]:
                copy.start()


def rows_of(dp, size):
    return pl.ds(pl.multiple_of(dp * size, size), size)


class Spread:
    def __init__(self, p, piece, dp, z, flow, far):
        ref, part, c0, c1 = piece
        size = part * p.n_z // 2
        side = lax.div(z, p.n_z // 2)
        side = 1 - side if far else side
        mid = (c0 + c1) // 2 if c1 - c0 >= 256 else c1
        self.split = mid < c1

        def made(block, turn, a, b):
            mine = ref.at[rows_of(2 * block + side, size), a:b]
            theirs = ref.at[rows_of(2 * flip(block, turn) + side, size), a:b]
            to = (flip(dp, turn), z)
            return Copy(flow, lambda: (mine, mine, to), lambda: (theirs, theirs, to))

        dpx, dpy = flip(dp, 2), flip(dp, 4)
        dpxy = flip(dpx, 4)
        self.first = [made(dp, 2, c0, mid), made(dp, 4, c0, mid), made(dp, 1, c0, c1)]
        self.a3 = made(dpx, 4, c0, mid)
        if self.split:
            self.first += [made(dp, 4, mid, c1), made(dp, 2, mid, c1)]
            self.b3 = made(dpy, 2, mid, c1)
        self.cores = [made(block, 1, c0, c1) for block in (dpx, dpy, dpxy)]

    def start(self):
        for copy in self.first:
            copy.start()

    def middle(self):
        self.first[0].arrived()
        self.a3.start()
        if self.split:
            self.first[3].arrived()
            self.b3.start()
            self.first[4].arrived()
        self.cores[0].start()
        self.first[1].arrived()
        self.cores[1].start()

    def late(self):
        self.a3.arrived()
        if self.split:
            self.b3.arrived()
        self.cores[2].start()

    def end(self):
        self.first[2].arrived()
        for copy in self.cores:
            copy.arrived()


class Reduce:
    def __init__(self, p, g, part, c0, c1, bufs, dp, z, flow, by_rows=False):
        self.p, self.g, self.part, self.c0, self.c1 = p, g, part, c0, c1
        self.dp, self.z, self.by_rows = dp, z, by_rows
        self.size = size = part * p.n_z
        self.cols = cols = c1 - c0
        self.mid = mid = cols // 2 if cols >= 256 else cols
        self.split = mid < cols
        self.s1, self.r1, self.r2, self.r3, self.s4, self.r4 = bufs
        s1, r1, r2, r3, s4, r4 = bufs
        x, y, core = (flip(dp, 2), z), (flip(dp, 4), z), (flip(dp, 1), z)
        dpx, dpy = flip(dp, 2), flip(dp, 4)
        self.order = (dp, dpx, dpy, flip(dpx, 4))

        def made(src, dst, to):
            return Copy(flow, lambda: (src, dst, to))

        if by_rows:
            self.chunks = [
                (slice(k * size, (k + 1) * size), slice(0, cols)) for k in range(4)
            ]
        else:
            wide = min(p.width, cols)
            self.chunks = [
                (slice(0, 4 * size), slice(k * wide, (k + 1) * wide))
                for k in range(cols // wide)
            ]
        self.core = [made(s1.at[at], r1.at[at], core) for at in self.chunks]
        self.a1 = made(s1.at[0 : 2 * size, 0:mid], r2.at[:, 0:mid], x)
        self.a2 = made(s1.at[0:size, 0:mid], r3.at[:, 0:mid], y)
        if self.split:
            self.b1 = made(s1.at[0 : 2 * size, mid:cols], r2.at[:, mid:cols], y)
            self.b2 = made(s1.at[0:size, mid:cols], r3.at[:, mid:cols], x)
        self.zs = []
        for i in range(1, p.n_z):
            peer = lax.rem(z + i, p.n_z)
            self.zs.append(made(s4.at[i - 1, :, 0:cols], r4.at[i - 1, :, 0:cols], (dp, peer)))

    def _sum(self, block, a, b, got=(), sub=None):
        first, count = (0, self.size) if sub is None else (sub * self.part, self.part)

        def at(start):
            return pl.ds(pl.multiple_of(start + first, self.part), count)

        total = self.g[at(block * self.size), self.c0 + a : self.c0 + b]
        for buf, slot in got:
            total = total + buf[at(slot * self.size), a:b].astype(F32)
        return total

    def _first(self, block):
        return self.r1, lax.div(block, 2)

    def _put(self, slot, a, b, total):
        self.s1[rows_of(slot, self.size), a:b] = total.astype(BF16)

    def core_start(self, k):
        _, lanes = self.chunks[k]
        a, b = lanes.start, lanes.stop
        theirs = 1 - lax.rem(self.dp, 2)
        for slot in (k,) if self.by_rows else range(4):
            self._put(slot, a, b, self._sum(2 * slot + theirs, a, b))
        self.core[k].start()

    def core_end(self):
        order, mid, cols = self.order, self.mid, self.cols
        for copy in self.core:
            copy.arrived()
        for copy in self.core:
            copy.left()
        for slot, k in ((0, 1), (1, 3)):
            self._put(slot, 0, mid, self._sum(order[k], 0, mid, [self._first(order[k])]))
        self.a1.start()
        if self.split:
            for slot, k in ((0, 2), (1, 3)):
                one = self._sum(order[k], mid, cols, [self._first(order[k])])
                self._put(slot, mid, cols, one)
            self.b1.start()

    def plane_middle(self):
        order, mid, cols = self.order, self.mid, self.cols
        self.a1.arrived()
        self.a1.left()
        got = [self._first(order[2]), (self.r2, 1)]
        self._put(0, 0, mid, self._sum(order[2], 0, mid, got))
        self.a2.start()
        if self.split:
            self.b1.arrived()
            self.b1.left()
            got = [self._first(order[1]), (self.r2, 1)]
            self._put(0, mid, cols, self._sum(order[1], mid, cols, got))
            self.b2.start()

    def _own(self, place):
        got = [self._first(self.dp), (self.r2, 0), (self.r3, 0)]
        return self._sum(self.dp, 0, self.cols, got, place)

    def plane_end(self):
        self.a2.arrived()
        if self.split:
            self.b2.arrived()
        for i in range(1, self.p.n_z):
            peer = lax.rem(self.z + i, self.p.n_z)
            self.s4[i - 1, :, 0 : self.cols] = self._own(peer).astype(BF16)
            self.zs[i - 1].start()

    def total(self):
        total = self._own(self.z)
        for i in range(1, self.p.n_z):
            self.zs[i - 1].arrived()
            total = total + self.r4[i - 1, :, 0 : self.cols].astype(F32)
        return total


def spread_vectors(p, r):
    r.wsf[...] = r.ws[...].astype(F32)

    def spread(k, part, total):
        g = r.wsf[pl.ds(k, p.devices, stride=16), :].astype(BF16)
        lane, column = iota((128, total), 0), iota((128, total), 1)
        place = jnp.where(split_at(column, part)[1] == lane, 1.0, 0.0)
        full = nn(g, place.astype(BF16))
        mine = split_at(iota((p.devices, total), 1), part)[0] == iota((p.devices, total), 0)
        return col_sum(jnp.where(mine, full, 0.0))

    for k in range(VECTORS):
        r.vec[k : k + 1, :] = spread(k, p.part, p.width)
    r.bup[...] = spread(VECTORS, p.part_h, p.hidden)


def collect_vectors(p, r):
    r.gs[...] = jnp.zeros(r.gs.shape, F32)

    def collect(k, row, part, total):
        mine = split_at(iota((p.devices, total), 1), part)[0] == iota((p.devices, total), 0)
        full = jnp.where(mine, row, 0.0)
        high = full.astype(BF16)
        rest = (full - high.astype(F32)).astype(BF16)
        lane, column = iota((128, total), 0), iota((128, total), 1)
        place = jnp.where(split_at(column, part)[1] == lane, 1.0, 0.0).astype(BF16)
        r.gs[pl.ds(k, p.devices, stride=16), :] = nt(high, place) + nt(rest, place)

    for k in range(VECTORS):
        collect(k, r.gvec[k : k + 1, :], p.part, p.width)
    collect(VECTORS, r.gbup[...], p.part_h, p.hidden)


class Refs:
    pass


def buffers(r, tag):
    return [getattr(r, tag + str(k)) for k in range(6) if hasattr(r, tag + str(k))]


def targets(p, n, z, r):
    w = p.width
    at = rows_of(n, p.part)
    places = {}
    if p.fused:
        places["w_query"] = r.wa.at[at, 0:w]
        places["w_key"] = r.wa.at[at, w : 2 * w]
        places["w_value"] = r.wa.at[at, 2 * w : 3 * w]
        places["w_out"] = r.wa.at[at, 3 * w : 4 * w]
        places["w_up"] = r.wa.at[at, 4 * w :]
        places["w_down"] = r.wd.at[rows_of(n, p.part_h), :]
    places["state"] = r.states.at[:, z]
    return places


def place_vectors(p, n, r):
    r.small[...] = jnp.zeros((16, 128), F32)
    for k, name in enumerate(SMALL):
        r.small[k : k + 1, 0 : p.part] = getattr(r, name)[...].astype(F32)
    r.small[VECTORS : VECTORS + 1, 0 : p.part_h] = r.b_up[...].astype(F32)
    r.ws[rows_of(n, 16), :] = r.small[...].astype(BF16)


def clear(p, r):
    r.ga[...] = jnp.zeros(r.ga.shape, F32)
    r.gd[...] = jnp.zeros(r.gd.shape, F32)
    r.gvec[...] = jnp.zeros(r.gvec.shape, F32)
    r.gbup[...] = jnp.zeros(r.gbup.shape, F32)
    r.qfull[...] = jnp.zeros(r.qfull.shape, BF16)
    r.dofull[...] = jnp.zeros(r.dofull.shape, BF16)
    r.qpair[...] = jnp.zeros(r.qpair.shape, BF16)
    r.vo[128:144, :] = jnp.ones((16, p.tree), BF16)
    lane = iota((p.tree, 128), 1)
    r.vfull[:, 128:256] = jnp.where(lane < 2, 1.0, 0.0).astype(BF16)


def kernel(p, names, given, results, *refs):
    r = Refs()
    for name, ref in zip(names, refs):
        setattr(r, name, ref)
    dp = lax.axis_index("dp")
    z = lax.axis_index("fsdp")
    w = p.width
    places = targets(p, dp * p.n_z + z, z, r)
    loads = {}
    for k, name in enumerate(given):
        place = places.get(name, getattr(r, name, None))
        copy = pltpu.make_async_copy(getattr(r, "hbm_" + name), place, r.load_sem.at[k])
        loads[name] = copy
    stores = {}
    for k, name in enumerate(results):
        if name == "new_state":
            continue
        stores[name] = pltpu.make_async_copy(
            getattr(r, name), getattr(r, "hbm_" + name), r.store_sem.at[k]
        )
    flow = Flow(r.send_sem, r.recv_sem)

    barrier = pltpu.get_barrier_semaphore()
    peers = [(dp, lax.rem(z + i, p.n_z)) for i in range(1, p.n_z)]
    if p.fused:
        peers += [(flip(dp, bit), z) for bit in (1, 2, 4)]
    for peer in peers:
        pl.semaphore_signal(barrier, inc=1, device_id=peer, device_id_type=MESH)
    for copy in loads.values():
        copy.start()
    lines = [
        Line(p, lambda b, m=m: r.states.at[m, b], dp, z, flow) for m in range(p.micro)
    ]
    steps = p.n_z - 1
    back = Back(p, dp, z, r)
    if p.fused:
        parts = (
            (r.wa, p.part, 0, 3 * w),
            (r.ws, 16, 0, 128),
            (r.wa, p.part, 3 * w, p.cols),
            (r.wd, p.part_h, 0, w),
        )
        rods = []
        for ref, part, c0, c1 in parts:

            def block(b, ref=ref, part=part, c0=c0, c1=c1):
                return ref.at[rows_of(dp * p.n_z + b, part), c0:c1]

            rods.append(Line(p, block, dp, z, flow))
        spreads, fars = (
            [Spread(p, piece, dp, z, flow, far) for piece in parts] for far in (False, True)
        )
        sums = [
            Reduce(p, r.ga, p.part, 3 * w, p.cols, buffers(r, "f"), dp, z, flow),
            Reduce(p, r.gd, p.part_h, 0, w, buffers(r, "d"), dp, z, flow, by_rows=True),
            Reduce(p, r.gs, 16, 0, 128, buffers(r, "e"), dp, z, flow),
            Reduce(p, r.ga, p.part, 0, 3 * w, [r.q0] + buffers(r, "b"), dp, z, flow),
        ]
    for copy in loads.values():
        copy.wait()
    if p.fused:
        place_vectors(p, dp * p.n_z + z, r)
    pl.semaphore_wait(barrier, len(peers))

    if p.fused:
        for rod in rods:
            rod.step(0)
        make_signal(p, r)
        for rod, spread in zip(rods, spreads):
            rod.step(1)
            spread.start()
        clear(p, r)
        for rod in rods:
            rod.step(2)
        lines[0].step(0)
        for rod, spread, far in zip(rods, spreads, fars):
            rod.step(3)
            spread.middle()
            far.start()
        lines[0].step(1)
        for spread in spreads:
            spread.late()
        fars[0].middle()
        lines[0].step(2)
        if p.micro > 1:
            lines[1].step(0)
        fars[0].late()
        for far in fars[1:]:
            far.middle()
        spreads[0].end()
        fars[0].end()
        lines[0].step(3)
    else:
        for k in range(steps + 1):
            for line in lines:
                line.step(k)
        make_signal(p, r)
        clear(p, r)

    @pl.loop(0, p.micro)
    def _(m):
        if p.fused:
            for k in range(1, p.micro):

                @pl.when(m == k)
                def _(k=k):
                    lines[k].step(steps)

        prepare_micro(p, m, z, r)
        if p.fused:

            @pl.when(m == 0)
            def _():
                for far in fars[1:]:
                    far.late()

        attention_forward(p, r)

        @pl.when(m > 1)
        def _():
            back.step(m - 2, steps)

        if p.fused:

            @pl.when(m == 1)
            def _():
                for line in lines[2:]:
                    for k in range(1, steps - 1):
                        line.step(k)

            @pl.when(m == 0)
            def _():
                if p.micro > 1:
                    for k in range(1, steps - 1):
                        lines[1].step(k)
                for spread in spreads[1:] + fars[1:]:
                    spread.end()
                spread_vectors(p, r)

        def between():
            @pl.when(m > 0)
            def _():
                for k in range(1, steps - 1):
                    back.step(m - 1, k)

        def down_done(j):
            if p.fused:

                @pl.when(m == p.micro - 1)
                def _():
                    sums[1].core_start(j)

        def up_done(j):
            if p.fused:

                @pl.when(m == p.micro - 1)
                def _():
                    sums[0].core_start(1 + j)
                    if j == p.hidden // w - 1:
                        sums[1].core_end()

        transition(p, m, z, r, between, down_done, up_done)

        out = pltpu.make_async_copy(
            r.new_state.at[m], r.hbm_new_state.at[m], r.state_sem.at[m]
        )
        out.start()
        if p.fused and p.micro > 1:

            @pl.when(m == 0)
            def _():
                lines[1].step(steps - 1)
                for line in lines[2:]:
                    line.step(0)

            @pl.when(m == 1)
            def _():
                for line in lines[2:]:
                    line.step(steps - 1)

        r.vt[...] = r.k[...].T
        if p.fused:

            @pl.when(m == p.micro - 1)
            def _():
                sums[0].core_start(0)
                collect_vectors(p, r)
                sums[2].core_start(0)

        def inside(i):
            if i == p.pairs // 2:

                @pl.when(m > 0)
                def _():
                    back.step(m - 1, steps - 1)

            if p.fused and i == 1:

                @pl.when(m == p.micro - 1)
                def _():
                    sums[0].core_end()

            if p.fused and i == p.pairs - 1:

                @pl.when(m == p.micro - 1)
                def _():
                    sums[2].core_end()

        attention_backward(p, m, z, r, back, inside)
        input_gradients(p, z, r)

    if p.fused:
        last = p.micro - 1
        for k in range(3):
            sums[3].core_start(k)
        sums[1].plane_middle()
        if last > 0:
            back.step(last - 1, steps)
        sums[3].core_end()
        sums[2].plane_middle()
        sums[0].plane_middle()
        back.step(last, 1)
        sums[1].plane_end()
        sums[2].plane_end()
        sums[3].plane_middle()
        back.step(last, 2)
        sums[0].plane_end()
        sums[3].plane_end()
        back.step(last, 3)
        r.g_down[...] = sums[1].total()
        total = sums[0].total()
        r.g_out[...] = total[:, 0:w]
        r.g_up[...] = total[:, w:]
        r.small[...] = sums[2].total()
        for k, name in enumerate(SMALL):
            getattr(r, "g_" + name)[...] = r.small[k : k + 1, 0 : p.part]
        r.g_b_up[...] = r.small[VECTORS : VECTORS + 1, 0 : p.part_h]
        total = sums[3].total()
        r.g_query[...] = total[:, 0:w]
        r.g_key[...] = total[:, w : 2 * w]
        r.g_value[...] = total[:, 2 * w : 3 * w]
    else:
        if p.micro > 1:
            back.step(p.micro - 2, steps)
        for k in range(1, steps + 1):
            back.step(p.micro - 1, k)
    for m in range(max(p.micro - 2, 0), p.micro):
        back.left(m)
    for copy in stores.values():
        copy.start()
    for m in range(p.micro):
        pltpu.make_async_copy(
            r.new_state.at[m], r.hbm_new_state.at[m], r.state_sem.at[m]
        ).wait()
    for copy in stores.values():
        copy.wait()
    flow.finish()
    if flow.used != copy_count(p):
        raise ValueError("copies: %d" % flow.used)


def copy_count(p):
    line = 2 * (p.n_z - 1)
    if not p.fused:
        return p.micro * line
    spreads = 2 * (3 * 10 + 7)
    exchanges = 3 * (4 + p.n_z - 1) + 2 + p.n_z - 1
    chunks = (p.cols // p.width - 3) + 4 + 1 + 3
    return (p.micro + 4) * line + spreads + exchanges + chunks


def run_kernel(p, inputs):
    w, t, rows = p.width, p.tree, p.rows
    outs = {
        "new_state": ((p.micro, rows, w), BF16),
        "new_halting": ((p.micro, rows), F32),
        "new_ponder": ((p.micro, rows), F32),
        "gstate": ((p.micro, rows, w), F32),
    }
    scratch = {}
    if p.fused:
        for name in ("query", "key", "value", "out"):
            outs["g_" + name] = ((p.part, w), F32)
        outs["g_up"] = ((p.part, p.hidden), F32)
        outs["g_down"] = ((p.part_h, w), F32)
        for name in SMALL:
            outs["g_" + name] = ((1, p.part), F32)
        outs["g_b_up"] = ((1, p.part_h), F32)
        scratch.update(
            wa=((w, p.cols), BF16),
            wd=((p.hidden, w), BF16),
            ws=((p.devices * 16, 128), BF16),
            wsf=((p.devices * 16, 128), F32),
            small=((16, 128), F32),
            vec=((8, w), F32),
            bup=((1, p.hidden), F32),
            ga=((w, p.cols), F32),
            gd=((p.hidden, w), F32),
            gs=((p.devices * 16, 128), F32),
            gvec=((8, w), F32),
            gbup=((1, p.hidden), F32),
        )
        kinds = (
            ("f", p.part, p.cols - 3 * w),
            ("b", p.part, 3 * w),
            ("d", p.part_h, w),
            ("e", 16, 128),
        )
        for tag, part, cols in kinds:
            size = part * p.n_z
            shapes = [(k * size, cols) for k in (4, 4, 2, 1)]
            shapes += [(p.n_z - 1, part, cols)] * 2
            for k, shape in enumerate(shapes):
                if k or tag in "fed":
                    scratch[tag + str(k)] = (shape, BF16)
        scratch["q0"] = ((4 * p.part * p.n_z, 3 * w), BF16)
    else:
        outs.update(
            ga=((w, p.cols), F32),
            gd=((p.hidden, w), F32),
            gvec=((8, w), F32),
            gbup=((1, p.hidden), F32),
        )
    scratch.update(
        states=((p.micro, p.n_z, rows, w), BF16),
        near=((rows, w), F32),
        far=((8, w), F32),
        h=((t, w), BF16),
        k=((t, w), BF16),
        v=((t, w), BF16),
        vt=((w, t), BF16),
        qt=((w, rows), BF16),
        kfull=((t, 256), BF16),
        qfull=((256, 2 * rows), BF16),
        vfull=((t, 256), BF16),
        dofull=((2, 256, 2 * rows), BF16),
        vo=((144, t), BF16),
        e=((p.pairs, t, 2 * rows), BF16),
        s=((t, 2 * rows), F32),
        top=((8, 2 * rows), F32),
        pre=((2, rows, w // 2), F32),
        inv=((p.pairs, 8, 2 * rows), F32),
        ot=((w, rows), F32),
        otb=((w, rows), BF16),
        dot=((w, rows), F32),
        xh1=((rows, w), F32),
        u=((rows, w), BF16),
        acc=((rows, w), F32),
        dg=((rows, w), BF16),
        ds=((2, t // 2, 2 * rows), BF16),
        dkv=((max(t, rows * (p.hidden // w)), 2 * w), BF16),
        dqt=((w, rows), BF16),
        qpair=((2, 128, 2 * rows), BF16),
        dq=((rows, w), BF16),
        dh=((2, p.n_z, rows, w), BF16),
        dh_in=((p.micro, p.n_z + 1, rows, w), BF16),
    )
    direct = ("w_query", "w_key", "w_value", "w_out", "w_up", "w_down", "state")
    for name, value in inputs.items():
        if not (name == "state" or (p.fused and name in direct)):
            scratch[name] = (value.shape, value.dtype)
    scratch.update(outs)
    hbm = pl.BlockSpec(memory_space=pl.ANY)
    copies = copy_count(p)
    names = (
        ["hbm_" + name for name in inputs]
        + ["hbm_" + name for name in outs]
        + list(scratch)
        + ["send_sem", "recv_sem", "back_send", "back_recv"]
        + ["load_sem", "store_sem", "state_sem"]
    )
    results = pl.pallas_call(
        functools.partial(kernel, p, names, list(inputs), list(outs)),
        out_shape=[jax.ShapeDtypeStruct(s, d) for s, d in outs.values()],
        in_specs=[hbm] * len(inputs),
        out_specs=[hbm] * len(outs),
        scratch_shapes=[pltpu.VMEM(s, d) for s, d in scratch.values()]
        + [pltpu.SemaphoreType.DMA((copies,))] * 2
        + [pltpu.SemaphoreType.DMA((p.micro, 2, p.n_z - 1))] * 2
        + [
            pltpu.SemaphoreType.DMA((len(inputs),)),
            pltpu.SemaphoreType.DMA((len(outs),)),
            pltpu.SemaphoreType.DMA((p.micro,)),
        ],
        compiler_params=pltpu.CompilerParams(
            collective_id=0, has_side_effects=True, vmem_limit_bytes=127 << 19
        ),
        name="layer",
    )(*inputs.values())
    return dict(zip(outs, results))


def hand_over(values):
    def body(*refs):
        count = len(values)
        held, sems = refs[2 * count : 3 * count], refs[3 * count :]
        taken = [
            pltpu.make_async_copy(refs[k], held[k], sems[0].at[k]) for k in range(count)
        ]
        given = [
            pltpu.make_async_copy(held[k], refs[count + k], sems[1].at[k])
            for k in range(count)
        ]
        for copy in taken:
            copy.start()
        for old, new in zip(taken, given):
            old.wait()
            new.start()
        for copy in given:
            copy.wait()

    hbm = pl.BlockSpec(memory_space=pl.ANY)
    moved = pl.pallas_call(
        body,
        out_shape=[jax.ShapeDtypeStruct(v.shape, v.dtype) for v in values.values()],
        in_specs=[hbm] * len(values),
        out_specs=[hbm] * len(values),
        scratch_shapes=[pltpu.VMEM(v.shape, v.dtype) for v in values.values()]
        + [pltpu.SemaphoreType.DMA((len(values),))] * 2,
        name="hand_over",
    )(*values.values())
    return dict(zip(values, moved))


WEIGHTS = (
    "w_query",
    "w_key",
    "w_value",
    "w_out",
    "w_up",
    "b_up",
    "w_down",
    "b_down",
    "gain_one",
    "bias_one",
    "gain_two",
    "bias_two",
    "w_halt",
)


def per_device(state, segment, parent, halting, ponder, cot_state, cot_halt, *weights):
    micro, rows, width = state.shape
    given = dict(zip(WEIGHTS, weights))
    n_dp, n_z = lax.axis_size("dp"), lax.axis_size("fsdp")
    part, hidden = given["w_query"].shape[0], given["w_up"].shape[1]
    fused = n_dp == 8 and n_z == 4 and part % 16 == 0 and part <= 128
    p = Plan(micro, rows, width, hidden, parent.shape[2], n_dp, n_z, fused)
    inputs = dict(
        state=state,
        seg=segment,
        parent=parent,
        halting=halting,
        ponder=ponder,
        cot=cot_state,
        cot_halt=cot_halt,
    )
    if fused:
        for name, value in given.items():
            inputs[name] = value if value.ndim == 2 else value.reshape(1, -1)
        out = hand_over(run_kernel(p, inputs))
        grads = []
        for name in WEIGHTS:
            value = out["g_" + name[2:]] if name.startswith("w_") and name != "w_halt" else out["g_" + name]
            grads.append(value.reshape(given[name].shape))
    else:
        axes = ("dp", "fsdp")
        full = {k: lax.all_gather(v, axes, axis=0, tiled=True) for k, v in given.items()}
        inputs["wa"] = jnp.concatenate([full[k] for k in WEIGHTS[:5]], axis=1)
        inputs["wd"] = full["w_down"]
        rows_f32 = [full[k].astype(F32) for k in WEIGHTS[7:]]
        rows_f32 += [jnp.zeros((width,), F32)] * 2
        inputs["vec"] = jnp.stack(rows_f32)
        inputs["bup"] = full["b_up"].astype(F32).reshape(1, -1)
        out = run_kernel(p, inputs)
        whole = [out["ga"][:, k * width : (k + 1) * width] for k in range(4)]
        whole += [out["ga"][:, 4 * width :], out["gbup"][0], out["gd"]]
        whole += [out["gvec"][k] for k in range(VECTORS)]
        grads = [
            lax.psum_scatter(g, axes, scatter_dimension=0, tiled=True) for g in whole
        ]
    return (out["new_state"], out["new_halting"], out["new_ponder"], out["gstate"], *grads)


def solution(mesh):
    tokens, flags = P(None, ("dp", "fsdp"), None), P(None, ("dp", "fsdp"))
    matrix, vector = P(("dp", "fsdp"), None), P(("dp", "fsdp"))
    weights = tuple(
        matrix if name in ("w_query", "w_key", "w_value", "w_out", "w_up", "w_down") else vector
        for name in WEIGHTS
    )
    return jax.shard_map(
        per_device,
        mesh=mesh,
        in_specs=(tokens, P(None, "dp"), P(None, "dp", None), flags, flags, tokens, flags)
        + weights,
        out_specs=(tokens, flags, flags, tokens) + weights,
        check_vma=False,
    )
```

```python
import functools
import math

import jax
import jax.numpy as jnp
from jax import lax
from jax.experimental import pallas as pl
from jax.experimental.pallas import tpu as pltpu
from jax.sharding import PartitionSpec as P

HEADS = 8
EPS = 1e-06
HALT_LIMIT = 0.99
GELU_C = math.sqrt(2.0 / math.pi)
GELU_A = 0.044715
LOG2E = 1.0 / math.log(2.0)
LN2 = math.log(2.0)
BIG = 2.0**100
F32 = jnp.float32
BF16 = jnp.bfloat16
MESH = pl.DeviceIdType.MESH
SMALL = ("b_down", "gain_one", "bias_one", "gain_two", "bias_two", "w_halt")
VECTORS = len(SMALL)


def nn(a, b):
    return lax.dot_general(a, b, (((1,), (0,)), ((), ())), preferred_element_type=F32)


def nt(a, b):
    return lax.dot_general(a, b, (((1,), (1,)), ((), ())), preferred_element_type=F32)


def tn(a, b):
    return lax.dot_general(a, b, (((0,), (0,)), ((), ())), preferred_element_type=F32)


def iota(shape, axis):
    return lax.broadcasted_iota(jnp.int32, shape, axis)


def split_at(values, size):
    if size & (size - 1) == 0:
        return values >> (size.bit_length() - 1), values & (size - 1)
    return lax.div(values, size), lax.rem(values, size)


def flip(index, bit):
    return index + bit - 2 * bit * lax.rem(lax.div(index, bit), 2)


def col_sum(values):
    return jnp.sum(values, axis=0, keepdims=True)


def norm(values):
    centered = values - jnp.mean(values, axis=-1, keepdims=True)
    inv = lax.rsqrt(jnp.mean(centered * centered, axis=-1, keepdims=True) + EPS)
    return centered * inv, inv


def norm_back(grad, normal, inv):
    return inv * (
        grad
        - jnp.mean(grad, axis=-1, keepdims=True)
        - normal * jnp.mean(grad * normal, axis=-1, keepdims=True)
    )


class Plan:
    def __init__(self, micro, rows, width, hidden, segs, n_dp, n_z, fused):
        self.micro, self.rows, self.width, self.hidden = micro, rows, width, hidden
        self.segs, self.n_dp, self.n_z, self.fused = segs, n_dp, n_z, fused
        self.tree = rows * n_z
        self.head = width // HEADS
        self.pair = 2 * self.head
        self.pairs = HEADS // 2
        self.cols = 4 * width + hidden
        self.devices = n_dp * n_z
        self.part = width // self.devices
        self.part_h = hidden // self.devices


def make_signal(p, r):
    half = p.width // 2
    freq = jnp.exp((-math.log(10000.0) / half) * iota((1, half), 1).astype(F32))
    far = (iota((8, 1), 0) * p.rows).astype(F32) * freq
    r.far[:, 0:half] = jnp.sin(far)
    r.far[:, half:] = jnp.cos(far)
    step = 32

    @pl.loop(0, p.rows // step)
    def _(i):
        near = (iota((step, 1), 0) + i * step).astype(F32) * freq
        at = pl.ds(pl.multiple_of(i * step, step), step)
        r.near[at, 0:half] = jnp.sin(near)
        r.near[at, half:] = jnp.cos(near)


def signal(p, r, b):
    half = p.width // 2
    far_sin, far_cos = r.far[pl.ds(b, 1), 0:half], r.far[pl.ds(b, 1), half:]
    near_sin, near_cos = r.near[:, 0:half], r.near[:, half:]
    return near_sin * far_cos + near_cos * far_sin, near_cos * far_cos - near_sin * far_sin


def blocked_table(p, parent_row):
    size = 128
    up = jnp.where(
        iota((16, p.segs), 0) == parent_row, 1.0, 0.0
    )
    up = jnp.concatenate([up, jnp.zeros((16, size - p.segs), F32)], axis=1)
    up = jnp.concatenate([up, jnp.zeros((size - 16, size), F32)], axis=0)
    row, column = iota((size, size), 0), iota((size, size), 1)
    reach = jnp.where(row == column, 1.0, up)
    for _ in range(4):
        reach = jnp.minimum(nn(reach.astype(BF16), reach.astype(BF16)), 1.0)
    inside = (row < p.segs) & (column < p.segs)
    return jnp.where(inside & (reach < 0.5), -BIG, 0.0)


def prepare_micro(p, m, z, r):
    table = blocked_table(p, r.parent[m])
    seg_row = r.seg[pl.ds(m, 1), :]
    hot = jnp.where(iota((128, p.tree), 0) == seg_row, 1.0, 0.0)
    r.kfull[:, 128:256] = hot.T.astype(BF16)
    own = pl.ds(pl.multiple_of(z * p.rows, p.rows), p.rows)
    hot = jnp.where(iota((128, p.rows), 0) == r.seg[pl.ds(m, 1), own], 1.0, 0.0)
    feature = nn(table.astype(BF16), hot.astype(BF16)).astype(BF16)
    r.qfull[128:256, 0 : p.rows] = feature
    r.qfull[128:256, p.rows : 2 * p.rows] = feature
    for b in range(p.n_z):
        at = slice(b * p.rows, (b + 1) * p.rows)
        for k, wave in enumerate(signal(p, r, b)):
            lanes = slice(k * (p.width // 2), (k + 1) * (p.width // 2))
            r.h[at, lanes] = (r.states[m, b, :, lanes].astype(F32) + wave).astype(BF16)

    w = p.width
    half = p.tree // 2
    for c in range(2):
        at = slice(c * half, (c + 1) * half)
        r.k[at, :] = nn(r.h[at, :], r.wa[:, w : 2 * w]).astype(BF16)
        r.v[at, :] = nn(r.h[at, :], r.wa[:, 2 * w : 3 * w]).astype(BF16)
    r.vt[...] = r.v[...].T
    q = nn(r.h[own, :], r.wa[:, 0:w]) * (LOG2E * p.head**-0.5)
    r.qt[...] = q.astype(BF16).T


def fill_pair(p, full, flat, i):
    low = pl.ds(pl.multiple_of(i * p.pair, p.pair), p.head)
    high = pl.ds(pl.multiple_of(i * p.pair + p.head, p.head), p.head)
    full[0 : p.head, 0 : p.rows] = flat[low, :].astype(BF16)
    full[p.head : p.pair, p.rows : 2 * p.rows] = flat[high, :].astype(BF16)


def attention_forward(p, r):
    step = p.tree // 8

    def ready(i):
        r.kfull[:, 0:128] = r.k[:, pl.ds(pl.multiple_of(i * p.pair, p.pair), p.pair)]
        fill_pair(p, r.qfull, r.qt, i)

    def scores(c, top):
        at = slice(c * step, (c + 1) * step)
        s = nn(r.kfull[at, :], r.qfull[...])
        r.s[at, :] = s
        own = jnp.max(s.reshape(step // 8, 8, 2 * p.rows), axis=0)
        return own if top is None else jnp.maximum(top, own)

    def soften(i, c, top):
        at = slice(c * step, (c + 1) * step)
        r.e[i, at, :] = jnp.exp2(r.s[at, :] - top).astype(BF16)

    def finish(i):
        lanes = pl.ds(pl.multiple_of(i * p.pair, p.pair), p.pair)
        r.vo[0:128, :] = r.vt[lanes, :]
        o = nn(r.vo[...], r.e[i])
        inv = 1.0 / o[128:136]
        r.inv[i] = inv
        low = pl.ds(pl.multiple_of(i * p.pair, p.pair), p.head)
        high = pl.ds(pl.multiple_of(i * p.pair + p.head, p.head), p.head)
        r.ot[low, :] = o[0 : p.head, 0 : p.rows] * inv[0:1, 0 : p.rows]
        r.ot[high, :] = o[p.head : p.pair, p.rows :] * inv[0:1, p.rows :]

    ready(0)
    top = None
    for c in range(8):
        top = scores(c, top)
    r.top[...] = top

    @pl.loop(0, p.pairs - 1)
    def _(i):
        ready(i + 1)
        top = jnp.max(r.top[...], axis=0, keepdims=True)
        later = None
        for c in range(8):
            soften(i, c, top)
            later = scores(c, later)
        r.top[...] = later
        finish(i)

    top = jnp.max(r.top[...], axis=0, keepdims=True)
    for c in range(8):
        soften(p.pairs - 1, c, top)
    finish(p.pairs - 1)


def transition(p, m, z, r, between, down_done, up_done):
    w = p.width
    rows = p.rows
    vec = lambda k: r.vec[k : k + 1, :]
    gain_a, bias_a, gain_b, bias_b, halt_vec = vec(1), vec(2), vec(3), vec(4), vec(5)
    w_out = slice(3 * w, 4 * w)

    lane = iota((128, rows), 0)
    packed = jnp.where(
        lane == 0,
        r.halting[pl.ds(m, 1), :],
        jnp.where(lane == 1, r.ponder[pl.ds(m, 1), :], r.cot_halt[pl.ds(m, 1), :]),
    ).T
    halting, ponder, cot_halt = packed[:, 0:1], packed[:, 1:2], packed[:, 2:3]

    r.otb[...] = r.ot[...].astype(BF16)
    state = r.states[m, z].astype(F32)
    y1 = state + jnp.concatenate(signal(p, r, z), axis=1) + tn(r.otb[...], r.wa[:, w_out])
    xh1, inv1 = norm(y1)
    n1 = xh1 * gain_a + bias_a
    r.xh1[...] = xh1
    r.u[...] = n1.astype(BF16)
    r.acc[...] = n1

    wide = w // 2
    count = p.hidden // wide

    def expand(c):
        r.pre[c % 2] = (
            nn(r.u[...], r.wa[:, 4 * w + c * wide : 4 * w + (c + 1) * wide])
            + r.bup[:, c * wide : (c + 1) * wide]
        )

    def bend(c):
        block = slice((c // 2) * rows, (c // 2 + 1) * rows)
        off = (c % 2) * wide
        pre = r.pre[c % 2]
        square = pre * pre
        t = jnp.tanh(pre * (GELU_C + (GELU_C * GELU_A) * square))
        half = 0.5 + 0.5 * t
        r.dkv[block, off : off + wide] = (pre * half).astype(BF16)
        slope = half + (0.5 * pre) * (1.0 - t * t) * (
            GELU_C + (3.0 * GELU_A * GELU_C) * square
        )
        r.dkv[block, w + off : w + off + wide] = slope.astype(BF16)

    def shrink(c):
        block = slice((c // 2) * rows, (c // 2 + 1) * rows)
        off = (c % 2) * wide
        r.acc[...] += nn(
            r.dkv[block, off : off + wide], r.wd[c * wide : (c + 1) * wide, :]
        )

    expand(0)
    for c in range(count):
        if c + 1 < count:
            expand(c + 1)
        bend(c)
        if c:
            shrink(c - 1)
    shrink(count - 1)

    between()
    y2 = r.acc[...] + vec(0)
    xh2, inv2 = norm(y2)
    s2 = xh2 * gain_b + bias_b
    ph = jax.nn.sigmoid(jnp.sum(s2 * halt_vec, axis=1, keepdims=True))
    run = jnp.where(halting < HALT_LIMIT, 1.0, 0.0)
    room = run * (1.0 - halting)
    weight = room * ph
    state = r.states[m, z].astype(F32)
    r.new_state[m] = (weight * s2 + (1.0 - weight) * state).astype(BF16)
    lane = iota((rows, 128), 1)
    packed = jnp.where(
        lane == 0, halting + weight, ponder + run * (1.0 - weight)
    ).T
    r.new_halting[pl.ds(m, 1), :] = packed[0:1, :]
    r.new_ponder[pl.ds(m, 1), :] = packed[1:2, :]

    cot = r.cot[m].astype(F32)
    dw = jnp.sum(cot * (s2 - state), axis=1, keepdims=True) + cot_halt
    dl = dw * room * ph * (1.0 - ph)
    ds2 = weight * cot + dl * halt_vec
    r.gvec[5:6, :] += col_sum(dl * s2)
    r.gvec[3:4, :] += col_sum(ds2 * xh2)
    r.gvec[4:5, :] += col_sum(ds2)
    dy2 = norm_back(ds2 * gain_b, xh2, inv2)
    r.gvec[0:1, :] += col_sum(dy2)
    r.dg[...] = dy2.astype(BF16)
    r.acc[...] = dy2
    r.gstate[m] = (1.0 - weight) * cot

    for j in range(p.hidden // w):
        at = slice(j * w, (j + 1) * w)
        block = slice(j * rows, (j + 1) * rows)
        r.gd[at, :] += tn(r.dkv[block, 0:w], r.dg[...])
        down_done(j)
    for j in range(p.hidden // w):
        at = slice(j * w, (j + 1) * w)
        at_up = slice((4 + j) * w, (5 + j) * w)
        block = slice(j * rows, (j + 1) * rows)
        dz = nt(r.dg[...], r.wd[at, :]) * r.dkv[block, w : 2 * w].astype(F32)
        r.gbup[:, at] += col_sum(dz)
        dzb = dz.astype(BF16)
        r.acc[...] += nt(dzb, r.wa[:, at_up])
        r.ga[:, at_up] += tn(r.u[...], dzb)
        up_done(j)

    dn1 = r.acc[...]
    xh1 = r.xh1[...]
    r.gvec[1:2, :] += col_sum(dn1 * xh1)
    r.gvec[2:3, :] += col_sum(dn1)
    dy1 = norm_back(dn1 * gain_a, xh1, inv1)
    r.gstate[m] += dy1
    da = dy1.astype(BF16)
    r.ga[:, w_out] += nn(r.otb[...], da)
    r.dot[...] = nt(r.wa[:, w_out], da)


def attention_backward(p, m, z, r, back, inside):
    w = p.width
    size = p.tree // 2

    @pl.when(m >= 2)
    def _():
        back.left(m - 2)

    def ready(i):
        low = slice(i * p.pair, i * p.pair + p.head)
        high = slice(i * p.pair + p.head, (i + 1) * p.pair)
        inv = r.inv[i]
        full, q = r.dofull.at[i], r.qpair.at[i]
        do_a = (r.dot[low, :] * inv[0:1, 0 : p.rows]).astype(BF16)
        do_b = (r.dot[high, :] * inv[0:1, p.rows :]).astype(BF16)
        full[0 : p.head, 0 : p.rows] = do_a
        full[p.head : p.pair, p.rows :] = do_b
        inner = jnp.concatenate(
            [
                col_sum(do_a.astype(F32) * r.ot[low, :]),
                col_sum(do_b.astype(F32) * r.ot[high, :]),
            ],
            axis=1,
        )
        rough = (-inner).astype(BF16).astype(F32)
        row = iota((16, 2 * p.rows), 0)
        full[128:144, :] = jnp.where(
            row == 0, rough, jnp.where(row == 1, -inner - rough, 0.0)
        ).astype(BF16)
        q[0 : p.head, 0 : p.rows] = r.qt[low, :]
        q[p.head : p.pair, p.rows :] = r.qt[high, :]

    side = lax.div(z, p.n_z // 2)
    ready(0)
    for c in range(2):
        half = side if c else 1 - side
        at = pl.ds(pl.multiple_of(half * size, size), size)
        for i in range(p.pairs):
            inside(c * p.pairs + i)
            lanes = slice(i * p.pair, (i + 1) * p.pair)
            lanes_v = slice(w + i * p.pair, w + (i + 1) * p.pair)
            r.vfull[at, 0:128] = r.v[at, lanes]
            dp = nn(r.vfull[at, :], r.dofull[i])
            if c == 0 and i + 1 < p.pairs:
                ready(i + 1)
            e = r.e[i, at, :]
            ds = (e.astype(F32) * dp).astype(BF16)
            r.ds[...] = ds
            r.dkv[at, lanes] = (nt(ds, r.qpair[i]) * LN2).astype(BF16)
            r.dkv[at, lanes_v] = nt(e, r.dofull[i, 0:128, :]).astype(BF16)
            dq = nn(r.vt[lanes, at], r.ds[...]) * (p.head**-0.5)
            low = slice(i * p.pair, i * p.pair + p.head)
            high = slice(i * p.pair + p.head, (i + 1) * p.pair)
            if c == 0:
                r.dqt[low, :] = dq[0 : p.head, 0 : p.rows].astype(BF16)
                r.dqt[high, :] = dq[p.head : p.pair, p.rows :].astype(BF16)
            else:
                one = r.dqt[low, :].astype(F32) + dq[0 : p.head, 0 : p.rows]
                two = r.dqt[high, :].astype(F32) + dq[p.head : p.pair, p.rows :]
                r.dqt[low, :] = one.astype(BF16)
                r.dqt[high, :] = two.astype(BF16)
        for k in range(p.n_z // 2):
            b = half * (p.n_z // 2) + k
            mine = pl.ds(pl.multiple_of(b * p.rows, p.rows), p.rows)
            dh = nt(r.dkv[mine, :], r.wa[:, w : 3 * w])
            r.dh[lax.rem(m, 2), b] = dh.astype(BF16)
            if c:

                @pl.when(z == b)
                def _():
                    r.gstate[m] += dh

        if c == 0:
            back.step(m, 0)

    r.dq[...] = r.dqt[...].T
    r.gstate[m] += nt(r.dq[...], r.wa[:, 0:w])


def input_gradients(p, z, r):
    w = p.width
    own = pl.ds(pl.multiple_of(z * p.rows, p.rows), p.rows)
    r.ga[:, 0:w] += tn(r.h[own, :], r.dq[...])
    for j in range(2):
        at = slice(j * w, (j + 1) * w)
        to = slice((1 + j) * w, (2 + j) * w)
        r.ga[:, to] += tn(r.h[...], r.dkv[0 : p.tree, at])


def remote(src, dst, send, recv, device):
    return pltpu.make_async_remote_copy(
        src_ref=src,
        dst_ref=dst,
        send_sem=send,
        recv_sem=recv,
        device_id=device,
        device_id_type=MESH,
    )


class Back:
    def __init__(self, p, dp, z, r):
        self.p, self.dp, self.z, self.r = p, dp, z, r
        self.last = p.n_z - 1

    def _copy(self, m, k, way, sender):
        r = self.r
        block = sender + way * (self.last - k)
        slot = block + 1 if way == 1 else block
        line = 0 if way == 1 else 1
        return remote(
            r.dh.at[lax.rem(m, 2), block],
            r.dh_in.at[m, slot],
            r.back_send.at[m, line, k],
            r.back_recv.at[m, line, k],
            (self.dp, sender + way),
        ), block, slot

    def _place(self, way):
        return self.z if way == 1 else self.last - self.z

    def step(self, m, k):
        r = self.r
        for way in (1, -1):
            place = self._place(way)
            if k == self.last:

                @pl.when(place > 0)
                def _():
                    copy, _, slot = self._copy(m, k - 1, way, self.z - way)
                    copy.wait_recv()
                    r.gstate[m] += r.dh_in[m, slot].astype(F32)

                continue

            @pl.when((place <= k) & (place < self.last))
            def _():
                if k:

                    @pl.when(place > 0)
                    def _():
                        copy, block, slot = self._copy(m, k - 1, way, self.z - way)
                        copy.wait_recv()
                        own = r.dh.at[lax.rem(m, 2), block]
                        own[...] = (
                            own[...].astype(F32) + r.dh_in[m, slot].astype(F32)
                        ).astype(BF16)

                self._copy(m, k, way, self.z)[0].start()

    def left(self, m):
        for way in (1, -1):
            place = self._place(way)
            for k in range(self.last):

                @pl.when((place <= k) & (place < self.last))
                def _():
                    self._copy(m, k, way, self.z)[0].wait_send()


class Copy:
    def __init__(self, flow, out, into=None, go=None, come=None):
        self.flow, self.out, self.into = flow, out, into or out
        self.go, self.come = go, come
        self.at = flow.used
        self.open = False
        flow.used += 1
        flow.copies.append(self)

    def _run(self, when, step):
        if when is None:
            step()
        else:
            pl.when(when())(step)

    def _make(self, ends):
        src, dst, device = ends()
        return remote(src, dst, self.flow.send.at[self.at], self.flow.recv.at[self.at], device)

    def start(self):
        self.open = True
        self._run(self.go, lambda: self._make(self.out).start())
        return self

    def arrived(self):
        self._run(self.come, lambda: self._make(self.into).wait_recv())

    def left(self):
        if self.open:
            self._run(self.go, lambda: self._make(self.out).wait_send())
            self.open = False


class Flow:
    def __init__(self, send, recv):
        self.send, self.recv, self.used, self.copies = send, recv, 0, []

    def finish(self):
        for copy in self.copies:
            copy.left()


class Line:
    def __init__(self, p, block, dp, z, flow):
        self.last = p.n_z - 1
        self.steps = []
        for step in range(p.n_z - 1):
            both = []
            for way in (1, -1):
                both.append(self._copy(p, block, dp, z, flow, step, way))
            self.steps.append(both)

    def _copy(self, p, block, dp, z, flow, step, way):
        place = z if way == 1 else self.last - z

        def out():
            at = block(z - way * step)
            return at, at, (dp, z + way)

        def into():
            at = block(z - way * (step + 1))
            return at, at, (dp, z - way)

        return Copy(
            flow,
            out,
            into,
            go=lambda: (place >= step) & (place < self.last),
            come=lambda: place >= step + 1,
        )

    def step(self, k):
        if k:
            for copy in self.steps[k - 1]:
                copy.arrived()
        if k < len(self.steps):
            for copy in self.steps[k]:
                copy.start()


def rows_of(dp, size):
    return pl.ds(pl.multiple_of(dp * size, size), size)


class Spread:
    def __init__(self, p, piece, dp, z, flow, far):
        ref, part, c0, c1 = piece
        size = part * p.n_z // 2
        side = lax.div(z, p.n_z // 2)
        side = 1 - side if far else side
        mid = (c0 + c1) // 2 if c1 - c0 >= 256 else c1
        self.split = mid < c1

        def made(block, turn, a, b):
            mine = ref.at[rows_of(2 * block + side, size), a:b]
            theirs = ref.at[rows_of(2 * flip(block, turn) + side, size), a:b]
            to = (flip(dp, turn), z)
            return Copy(flow, lambda: (mine, mine, to), lambda: (theirs, theirs, to))

        dpx, dpy = flip(dp, 2), flip(dp, 4)
        dpxy = flip(dpx, 4)
        self.first = [made(dp, 2, c0, mid), made(dp, 4, c0, mid), made(dp, 1, c0, c1)]
        self.a3 = made(dpx, 4, c0, mid)
        if self.split:
            self.first += [made(dp, 4, mid, c1), made(dp, 2, mid, c1)]
            self.b3 = made(dpy, 2, mid, c1)
        self.cores = [made(block, 1, c0, c1) for block in (dpx, dpy, dpxy)]

    def start(self):
        for copy in self.first:
            copy.start()

    def middle(self):
        self.first[0].arrived()
        self.a3.start()
        if self.split:
            self.first[3].arrived()
            self.b3.start()
            self.first[4].arrived()
        self.cores[0].start()
        self.first[1].arrived()
        self.cores[1].start()

    def late(self):
        self.a3.arrived()
        if self.split:
            self.b3.arrived()
        self.cores[2].start()

    def end(self):
        self.first[2].arrived()
        for copy in self.cores:
            copy.arrived()


class Reduce:
    def __init__(self, p, g, part, c0, c1, bufs, dp, z, flow, by_rows=False):
        self.p, self.g, self.part, self.c0, self.c1 = p, g, part, c0, c1
        self.dp, self.z, self.by_rows = dp, z, by_rows
        self.size = size = part * p.n_z
        self.cols = cols = c1 - c0
        self.mid = mid = cols // 2 if cols >= 256 else cols
        self.split = mid < cols
        self.s1, self.r1, self.r2, self.r3, self.s4, self.r4 = bufs
        s1, r1, r2, r3, s4, r4 = bufs
        x, y, core = (flip(dp, 2), z), (flip(dp, 4), z), (flip(dp, 1), z)
        dpx, dpy = flip(dp, 2), flip(dp, 4)
        self.order = (dp, dpx, dpy, flip(dpx, 4))

        def made(src, dst, to):
            return Copy(flow, lambda: (src, dst, to))

        if by_rows:
            self.chunks = [
                (slice(k * size, (k + 1) * size), slice(0, cols)) for k in range(4)
            ]
        else:
            wide = min(p.width, cols)
            self.chunks = [
                (slice(0, 4 * size), slice(k * wide, (k + 1) * wide))
                for k in range(cols // wide)
            ]
        self.core = [made(s1.at[at], r1.at[at], core) for at in self.chunks]
        self.a1 = made(s1.at[0 : 2 * size, 0:mid], r2.at[:, 0:mid], x)
        self.a2 = made(s1.at[0:size, 0:mid], r3.at[:, 0:mid], y)
        if self.split:
            self.b1 = made(s1.at[0 : 2 * size, mid:cols], r2.at[:, mid:cols], y)
            self.b2 = made(s1.at[0:size, mid:cols], r3.at[:, mid:cols], x)
        self.zs = []
        for i in range(1, p.n_z):
            peer = lax.rem(z + i, p.n_z)
            self.zs.append(made(s4.at[i - 1, :, 0:cols], r4.at[i - 1, :, 0:cols], (dp, peer)))

    def _sum(self, block, a, b, got=(), sub=None):
        first, count = (0, self.size) if sub is None else (sub * self.part, self.part)

        def at(start):
            return pl.ds(pl.multiple_of(start + first, self.part), count)

        total = self.g[at(block * self.size), self.c0 + a : self.c0 + b]
        for buf, slot in got:
            total = total + buf[at(slot * self.size), a:b].astype(F32)
        return total

    def _first(self, block):
        return self.r1, lax.div(block, 2)

    def _put(self, slot, a, b, total):
        self.s1[rows_of(slot, self.size), a:b] = total.astype(BF16)

    def core_start(self, k):
        _, lanes = self.chunks[k]
        a, b = lanes.start, lanes.stop
        theirs = 1 - lax.rem(self.dp, 2)
        for slot in (k,) if self.by_rows else range(4):
            self._put(slot, a, b, self._sum(2 * slot + theirs, a, b))
        self.core[k].start()

    def core_end(self):
        order, mid, cols = self.order, self.mid, self.cols
        for copy in self.core:
            copy.arrived()
        for copy in self.core:
            copy.left()
        for slot, k in ((0, 1), (1, 3)):
            self._put(slot, 0, mid, self._sum(order[k], 0, mid, [self._first(order[k])]))
        self.a1.start()
        if self.split:
            for slot, k in ((0, 2), (1, 3)):
                one = self._sum(order[k], mid, cols, [self._first(order[k])])
                self._put(slot, mid, cols, one)
            self.b1.start()

    def plane_middle(self):
        order, mid, cols = self.order, self.mid, self.cols
        self.a1.arrived()
        self.a1.left()
        got = [self._first(order[2]), (self.r2, 1)]
        self._put(0, 0, mid, self._sum(order[2], 0, mid, got))
        self.a2.start()
        if self.split:
            self.b1.arrived()
            self.b1.left()
            got = [self._first(order[1]), (self.r2, 1)]
            self._put(0, mid, cols, self._sum(order[1], mid, cols, got))
            self.b2.start()

    def _own(self, place):
        got = [self._first(self.dp), (self.r2, 0), (self.r3, 0)]
        return self._sum(self.dp, 0, self.cols, got, place)

    def plane_end(self):
        self.a2.arrived()
        if self.split:
            self.b2.arrived()
        for i in range(1, self.p.n_z):
            peer = lax.rem(self.z + i, self.p.n_z)
            self.s4[i - 1, :, 0 : self.cols] = self._own(peer).astype(BF16)
            self.zs[i - 1].start()

    def total(self):
        total = self._own(self.z)
        for i in range(1, self.p.n_z):
            self.zs[i - 1].arrived()
            total = total + self.r4[i - 1, :, 0 : self.cols].astype(F32)
        return total


def spread_vectors(p, r):
    r.gs[...] = r.ws[...].astype(F32)

    def spread(k, part, total):
        g = r.gs[pl.ds(k, p.devices, stride=16), :].astype(BF16)
        lane, column = iota((128, total), 0), iota((128, total), 1)
        place = jnp.where(split_at(column, part)[1] == lane, 1.0, 0.0)
        full = nn(g, place.astype(BF16))
        mine = split_at(iota((p.devices, total), 1), part)[0] == iota((p.devices, total), 0)
        return col_sum(jnp.where(mine, full, 0.0))

    for k in range(VECTORS):
        r.vec[k : k + 1, :] = spread(k, p.part, p.width)
    r.bup[...] = spread(VECTORS, p.part_h, p.hidden)


def collect_vectors(p, r):
    r.gs[...] = jnp.zeros(r.gs.shape, F32)

    def collect(k, row, part, total):
        mine = split_at(iota((p.devices, total), 1), part)[0] == iota((p.devices, total), 0)
        full = jnp.where(mine, row, 0.0)
        high = full.astype(BF16)
        rest = (full - high.astype(F32)).astype(BF16)
        lane, column = iota((128, total), 0), iota((128, total), 1)
        place = jnp.where(split_at(column, part)[1] == lane, 1.0, 0.0).astype(BF16)
        r.gs[pl.ds(k, p.devices, stride=16), :] = nt(high, place) + nt(rest, place)

    for k in range(VECTORS):
        collect(k, r.gvec[k : k + 1, :], p.part, p.width)
    collect(VECTORS, r.gbup[...], p.part_h, p.hidden)


class Refs:
    pass


def buffers(r, tag):
    return [getattr(r, tag + str(k)) for k in range(6) if hasattr(r, tag + str(k))]


def targets(p, n, z, r):
    w = p.width
    at = rows_of(n, p.part)
    places = {}
    if p.fused:
        places["w_query"] = r.wa.at[at, 0:w]
        places["w_key"] = r.wa.at[at, w : 2 * w]
        places["w_value"] = r.wa.at[at, 2 * w : 3 * w]
        places["w_out"] = r.wa.at[at, 3 * w : 4 * w]
        places["w_up"] = r.wa.at[at, 4 * w :]
        places["w_down"] = r.wd.at[rows_of(n, p.part_h), :]
    places["state"] = r.states.at[:, z]
    return places


def place_vectors(p, n, r):
    r.small[...] = jnp.zeros((16, 128), F32)
    for k, name in enumerate(SMALL):
        r.small[k : k + 1, 0 : p.part] = getattr(r, name)[...].astype(F32)
    r.small[VECTORS : VECTORS + 1, 0 : p.part_h] = r.b_up[...].astype(F32)
    r.ws[rows_of(n, 16), :] = r.small[...].astype(BF16)


def clear(p, r):
    r.ga[...] = jnp.zeros(r.ga.shape, F32)
    r.gd[...] = jnp.zeros(r.gd.shape, F32)
    r.gvec[...] = jnp.zeros(r.gvec.shape, F32)
    r.gbup[...] = jnp.zeros(r.gbup.shape, F32)
    r.qfull[...] = jnp.zeros(r.qfull.shape, BF16)
    r.dofull[...] = jnp.zeros(r.dofull.shape, BF16)
    r.qpair[...] = jnp.zeros(r.qpair.shape, BF16)
    r.vo[128:144, :] = jnp.ones((16, p.tree), BF16)
    lane = iota((p.tree, 128), 1)
    r.vfull[:, 128:256] = jnp.where(lane < 2, 1.0, 0.0).astype(BF16)


def kernel(p, names, given, results, *refs):
    r = Refs()
    for name, ref in zip(names, refs):
        setattr(r, name, ref)
    dp = lax.axis_index("dp")
    z = lax.axis_index("fsdp")
    w = p.width
    places = targets(p, dp * p.n_z + z, z, r)
    loads = {}
    for k, name in enumerate(given):
        place = places.get(name, getattr(r, name, None))
        copy = pltpu.make_async_copy(getattr(r, "hbm_" + name), place, r.load_sem.at[k])
        loads[name] = copy
    stores = {}
    for k, name in enumerate(results):
        if name == "new_state":
            continue
        stores[name] = pltpu.make_async_copy(
            getattr(r, name), getattr(r, "hbm_" + name), r.store_sem.at[k]
        )
    flow = Flow(r.send_sem, r.recv_sem)

    barrier = pltpu.get_barrier_semaphore()
    peers = [(dp, lax.rem(z + i, p.n_z)) for i in range(1, p.n_z)]
    if p.fused:
        peers += [(flip(dp, bit), z) for bit in (1, 2, 4)]
    for peer in peers:
        pl.semaphore_signal(barrier, inc=1, device_id=peer, device_id_type=MESH)
    for copy in loads.values():
        copy.start()
    lines = [
        Line(p, lambda b, m=m: r.states.at[m, b], dp, z, flow) for m in range(p.micro)
    ]
    steps = p.n_z - 1
    back = Back(p, dp, z, r)
    if p.fused:
        parts = (
            (r.wa, p.part, 0, 3 * w),
            (r.ws, 16, 0, 128),
            (r.wa, p.part, 3 * w, p.cols),
            (r.wd, p.part_h, 0, w),
        )
        rods = []
        for ref, part, c0, c1 in parts:

            def block(b, ref=ref, part=part, c0=c0, c1=c1):
                return ref.at[rows_of(dp * p.n_z + b, part), c0:c1]

            rods.append(Line(p, block, dp, z, flow))
        spreads, fars = (
            [Spread(p, piece, dp, z, flow, far) for piece in parts] for far in (False, True)
        )
        sums = [
            Reduce(p, r.ga, p.part, 3 * w, p.cols, buffers(r, "f"), dp, z, flow),
            Reduce(p, r.gd, p.part_h, 0, w, buffers(r, "d"), dp, z, flow, by_rows=True),
            Reduce(p, r.gs, 16, 0, 128, buffers(r, "e"), dp, z, flow),
            Reduce(p, r.ga, p.part, 0, 3 * w, [r.q0] + buffers(r, "b"), dp, z, flow),
        ]
    for copy in loads.values():
        copy.wait()
    if p.fused:
        place_vectors(p, dp * p.n_z + z, r)
    pl.semaphore_wait(barrier, len(peers))

    if p.fused:
        for rod in rods:
            rod.step(0)
        make_signal(p, r)
        for rod, spread in zip(rods, spreads):
            rod.step(1)
            spread.start()
        clear(p, r)
        for rod in rods:
            rod.step(2)
        lines[0].step(0)
        for rod, spread, far in zip(rods, spreads, fars):
            rod.step(3)
            spread.middle()
            far.start()
        lines[0].step(1)
        for spread in spreads:
            spread.late()
        fars[0].middle()
        lines[0].step(2)
        if p.micro > 1:
            lines[1].step(0)
        fars[0].late()
        for far in fars[1:]:
            far.middle()
        spreads[0].end()
        fars[0].end()
        lines[0].step(3)
    else:
        for k in range(steps + 1):
            for line in lines:
                line.step(k)
        make_signal(p, r)
        clear(p, r)

    @pl.loop(0, p.micro)
    def _(m):
        if p.fused:
            for k in range(1, p.micro):

                @pl.when(m == k)
                def _(k=k):
                    lines[k].step(steps)

        prepare_micro(p, m, z, r)
        if p.fused:

            @pl.when(m == 0)
            def _():
                for far in fars[1:]:
                    far.late()

        attention_forward(p, r)

        @pl.when(m > 1)
        def _():
            back.step(m - 2, steps)

        if p.fused:

            @pl.when(m == 1)
            def _():
                for line in lines[2:]:
                    for k in range(1, steps - 1):
                        line.step(k)

            @pl.when(m == 0)
            def _():
                if p.micro > 1:
                    for k in range(1, steps - 1):
                        lines[1].step(k)
                for spread in spreads[1:] + fars[1:]:
                    spread.end()
                spread_vectors(p, r)

        def between():
            @pl.when(m > 0)
            def _():
                for k in range(1, steps - 1):
                    back.step(m - 1, k)

        def down_done(j):
            if p.fused:

                @pl.when(m == p.micro - 1)
                def _():
                    sums[1].core_start(j)

        def up_done(j):
            if p.fused:

                @pl.when(m == p.micro - 1)
                def _():
                    sums[0].core_start(1 + j)
                    if j == p.hidden // w - 1:
                        sums[1].core_end()

        transition(p, m, z, r, between, down_done, up_done)

        out = pltpu.make_async_copy(
            r.new_state.at[m], r.hbm_new_state.at[m], r.state_sem.at[m]
        )
        out.start()
        if p.fused and p.micro > 1:

            @pl.when(m == 0)
            def _():
                lines[1].step(steps - 1)
                for line in lines[2:]:
                    line.step(0)

            @pl.when(m == 1)
            def _():
                for line in lines[2:]:
                    line.step(steps - 1)

        r.vt[...] = r.k[...].T
        if p.fused:

            @pl.when(m == p.micro - 1)
            def _():
                sums[0].core_start(0)
                collect_vectors(p, r)
                sums[2].core_start(0)

        def inside(i):
            if i == p.pairs + 1:

                @pl.when(m > 0)
                def _():
                    back.step(m - 1, steps - 1)

            if p.fused and i == 2:

                @pl.when(m == p.micro - 1)
                def _():
                    sums[0].core_end()

            if p.fused and i == p.pairs + 2:

                @pl.when(m == p.micro - 1)
                def _():
                    sums[2].core_end()

        attention_backward(p, m, z, r, back, inside)
        input_gradients(p, z, r)

    if p.fused:
        last = p.micro - 1
        for k in range(3):
            sums[3].core_start(k)
        back.step(last, 1)
        sums[1].plane_middle()
        sums[3].core_end()
        sums[2].plane_middle()
        sums[0].plane_middle()
        sums[1].plane_end()
        back.step(last, 2)
        sums[3].plane_middle()
        sums[2].plane_end()
        sums[0].plane_end()
        sums[3].plane_end()
        back.step(last, 3)
        back.step(last - 1, steps)
        r.g_down[...] = sums[1].total()
        total = sums[0].total()
        r.g_out[...] = total[:, 0:w]
        r.g_up[...] = total[:, w:]
        r.small[...] = sums[2].total()
        for k, name in enumerate(SMALL):
            getattr(r, "g_" + name)[...] = r.small[k : k + 1, 0 : p.part]
        r.g_b_up[...] = r.small[VECTORS : VECTORS + 1, 0 : p.part_h]
        total = sums[3].total()
        r.g_query[...] = total[:, 0:w]
        r.g_key[...] = total[:, w : 2 * w]
        r.g_value[...] = total[:, 2 * w : 3 * w]
    else:
        if p.micro > 1:
            back.step(p.micro - 2, steps)
        for k in range(1, steps + 1):
            back.step(p.micro - 1, k)
    for m in range(max(p.micro - 2, 0), p.micro):
        back.left(m)
    for copy in stores.values():
        copy.start()
    for m in range(p.micro):
        pltpu.make_async_copy(
            r.new_state.at[m], r.hbm_new_state.at[m], r.state_sem.at[m]
        ).wait()
    for copy in stores.values():
        copy.wait()
    flow.finish()
    if flow.used != copy_count(p):
        raise ValueError("copies: %d" % flow.used)


def copy_count(p):
    line = 2 * (p.n_z - 1)
    if not p.fused:
        return p.micro * line
    spreads = 2 * (3 * 10 + 7)
    exchanges = 3 * (4 + p.n_z - 1) + 2 + p.n_z - 1
    chunks = (p.cols // p.width - 3) + 4 + 1 + 3
    return (p.micro + 4) * line + spreads + exchanges + chunks


def run_kernel(p, inputs):
    w, t, rows = p.width, p.tree, p.rows
    outs = {
        "new_state": ((p.micro, rows, w), BF16),
        "new_halting": ((p.micro, rows), F32),
        "new_ponder": ((p.micro, rows), F32),
        "gstate": ((p.micro, rows, w), F32),
    }
    scratch = {}
    if p.fused:
        for name in ("query", "key", "value", "out"):
            outs["g_" + name] = ((p.part, w), F32)
        outs["g_up"] = ((p.part, p.hidden), F32)
        outs["g_down"] = ((p.part_h, w), F32)
        for name in SMALL:
            outs["g_" + name] = ((1, p.part), F32)
        outs["g_b_up"] = ((1, p.part_h), F32)
        scratch.update(
            wa=((w, p.cols), BF16),
            wd=((p.hidden, w), BF16),
            ws=((p.devices * 16, 128), BF16),
            small=((16, 128), F32),
            vec=((8, w), F32),
            bup=((1, p.hidden), F32),
            ga=((w, p.cols), F32),
            gd=((p.hidden, w), F32),
            gs=((p.devices * 16, 128), F32),
            gvec=((8, w), F32),
            gbup=((1, p.hidden), F32),
        )
        kinds = (
            ("f", p.part, p.cols - 3 * w),
            ("b", p.part, 3 * w),
            ("d", p.part_h, w),
            ("e", 16, 128),
        )
        for tag, part, cols in kinds:
            size = part * p.n_z
            shapes = [(k * size, cols) for k in (4, 4, 2, 1)]
            shapes += [(p.n_z - 1, part, cols)] * 2
            for k, shape in enumerate(shapes):
                if k or tag in "fed":
                    scratch[tag + str(k)] = (shape, BF16)
        scratch["q0"] = ((4 * p.part * p.n_z, 3 * w), BF16)
    else:
        outs.update(
            ga=((w, p.cols), F32),
            gd=((p.hidden, w), F32),
            gvec=((8, w), F32),
            gbup=((1, p.hidden), F32),
        )
    scratch.update(
        states=((p.micro, p.n_z, rows, w), BF16),
        near=((rows, w), F32),
        far=((8, w), F32),
        h=((t, w), BF16),
        k=((t, w), BF16),
        v=((t, w), BF16),
        vt=((w, t), BF16),
        qt=((w, rows), BF16),
        kfull=((t, 256), BF16),
        qfull=((256, 2 * rows), BF16),
        vfull=((t, 256), BF16),
        dofull=((p.pairs, 256, 2 * rows), BF16),
        vo=((144, t), BF16),
        e=((p.pairs, t, 2 * rows), BF16),
        s=((t, 2 * rows), F32),
        top=((8, 2 * rows), F32),
        pre=((2, rows, w // 2), F32),
        inv=((p.pairs, 8, 2 * rows), F32),
        ot=((w, rows), F32),
        otb=((w, rows), BF16),
        dot=((w, rows), F32),
        xh1=((rows, w), F32),
        u=((rows, w), BF16),
        acc=((rows, w), F32),
        dg=((rows, w), BF16),
        ds=((t // 2, 2 * rows), BF16),
        dkv=((max(t, rows * (p.hidden // w)), 2 * w), BF16),
        dqt=((w, rows), BF16),
        qpair=((p.pairs, 128, 2 * rows), BF16),
        dq=((rows, w), BF16),
        dh=((2, p.n_z, rows, w), BF16),
        dh_in=((p.micro, p.n_z + 1, rows, w), BF16),
    )
    direct = ("w_query", "w_key", "w_value", "w_out", "w_up", "w_down", "state")
    for name, value in inputs.items():
        if not (name == "state" or (p.fused and name in direct)):
            scratch[name] = (value.shape, value.dtype)
    scratch.update(outs)
    hbm = pl.BlockSpec(memory_space=pl.ANY)
    copies = copy_count(p)
    names = (
        ["hbm_" + name for name in inputs]
        + ["hbm_" + name for name in outs]
        + list(scratch)
        + ["send_sem", "recv_sem", "back_send", "back_recv"]
        + ["load_sem", "store_sem", "state_sem"]
    )
    results = pl.pallas_call(
        functools.partial(kernel, p, names, list(inputs), list(outs)),
        out_shape=[jax.ShapeDtypeStruct(s, d) for s, d in outs.values()],
        in_specs=[hbm] * len(inputs),
        out_specs=[hbm] * len(outs),
        scratch_shapes=[pltpu.VMEM(s, d) for s, d in scratch.values()]
        + [pltpu.SemaphoreType.DMA((copies,))] * 2
        + [pltpu.SemaphoreType.DMA((p.micro, 2, p.n_z - 1))] * 2
        + [
            pltpu.SemaphoreType.DMA((len(inputs),)),
            pltpu.SemaphoreType.DMA((len(outs),)),
            pltpu.SemaphoreType.DMA((p.micro,)),
        ],
        compiler_params=pltpu.CompilerParams(
            collective_id=0, has_side_effects=True, vmem_limit_bytes=127 << 19
        ),
        name="layer",
    )(*inputs.values())
    return dict(zip(outs, results))


def hand_over(values):
    def body(*refs):
        count = len(values)
        held, sems = refs[2 * count : 3 * count], refs[3 * count :]
        taken = [
            pltpu.make_async_copy(refs[k], held[k], sems[0].at[k]) for k in range(count)
        ]
        given = [
            pltpu.make_async_copy(held[k], refs[count + k], sems[1].at[k])
            for k in range(count)
        ]
        for copy in taken:
            copy.start()
        for old, new in zip(taken, given):
            old.wait()
            new.start()
        for copy in given:
            copy.wait()

    hbm = pl.BlockSpec(memory_space=pl.ANY)
    moved = pl.pallas_call(
        body,
        out_shape=[jax.ShapeDtypeStruct(v.shape, v.dtype) for v in values.values()],
        in_specs=[hbm] * len(values),
        out_specs=[hbm] * len(values),
        scratch_shapes=[pltpu.VMEM(v.shape, v.dtype) for v in values.values()]
        + [pltpu.SemaphoreType.DMA((len(values),))] * 2,
        name="hand_over",
    )(*values.values())
    return dict(zip(values, moved))


WEIGHTS = (
    "w_query",
    "w_key",
    "w_value",
    "w_out",
    "w_up",
    "b_up",
    "w_down",
    "b_down",
    "gain_one",
    "bias_one",
    "gain_two",
    "bias_two",
    "w_halt",
)


def per_device(state, segment, parent, halting, ponder, cot_state, cot_halt, *weights):
    micro, rows, width = state.shape
    given = dict(zip(WEIGHTS, weights))
    n_dp, n_z = lax.axis_size("dp"), lax.axis_size("fsdp")
    part, hidden = given["w_query"].shape[0], given["w_up"].shape[1]
    fused = n_dp == 8 and n_z == 4 and part % 16 == 0 and part <= 128
    p = Plan(micro, rows, width, hidden, parent.shape[2], n_dp, n_z, fused)
    inputs = dict(
        state=state,
        seg=segment,
        parent=parent,
        halting=halting,
        ponder=ponder,
        cot=cot_state,
        cot_halt=cot_halt,
    )
    if fused:
        for name, value in given.items():
            inputs[name] = value if value.ndim == 2 else value.reshape(1, -1)
        out = hand_over(run_kernel(p, inputs))
        grads = []
        for name in WEIGHTS:
            value = out["g_" + name[2:]] if name.startswith("w_") and name != "w_halt" else out["g_" + name]
            grads.append(value.reshape(given[name].shape))
    else:
        axes = ("dp", "fsdp")
        full = {k: lax.all_gather(v, axes, axis=0, tiled=True) for k, v in given.items()}
        inputs["wa"] = jnp.concatenate([full[k] for k in WEIGHTS[:5]], axis=1)
        inputs["wd"] = full["w_down"]
        rows_f32 = [full[k].astype(F32) for k in WEIGHTS[7:]]
        rows_f32 += [jnp.zeros((width,), F32)] * 2
        inputs["vec"] = jnp.stack(rows_f32)
        inputs["bup"] = full["b_up"].astype(F32).reshape(1, -1)
        out = run_kernel(p, inputs)
        whole = [out["ga"][:, k * width : (k + 1) * width] for k in range(4)]
        whole += [out["ga"][:, 4 * width :], out["gbup"][0], out["gd"]]
        whole += [out["gvec"][k] for k in range(VECTORS)]
        grads = [
            lax.psum_scatter(g, axes, scatter_dimension=0, tiled=True) for g in whole
        ]
    return (out["new_state"], out["new_halting"], out["new_ponder"], out["gstate"], *grads)


def solution(mesh):
    tokens, flags = P(None, ("dp", "fsdp"), None), P(None, ("dp", "fsdp"))
    matrix, vector = P(("dp", "fsdp"), None), P(("dp", "fsdp"))
    weights = tuple(
        matrix if name in ("w_query", "w_key", "w_value", "w_out", "w_up", "w_down") else vector
        for name in WEIGHTS
    )
    return jax.shard_map(
        per_device,
        mesh=mesh,
        in_specs=(tokens, P(None, "dp"), P(None, "dp", None), flags, flags, tokens, flags)
        + weights,
        out_specs=(tokens, flags, flags, tokens) + weights,
        check_vma=False,
    )
```

```python
import functools
import math

import jax
import jax.numpy as jnp
from jax import lax
from jax.experimental import pallas as pl
from jax.experimental.pallas import tpu as pltpu
from jax.sharding import PartitionSpec as P

HEADS = 8
EPS = 1e-06
HALT_LIMIT = 0.99
GELU_C = math.sqrt(2.0 / math.pi)
GELU_A = 0.044715
LOG2E = 1.0 / math.log(2.0)
LN2 = math.log(2.0)
BIG = 2.0**100
F32 = jnp.float32
BF16 = jnp.bfloat16
MESH = pl.DeviceIdType.MESH
SMALL = ("b_down", "gain_one", "bias_one", "gain_two", "bias_two", "w_halt")
VECTORS = len(SMALL)


def nn(a, b):
    return lax.dot_general(a, b, (((1,), (0,)), ((), ())), preferred_element_type=F32)


def nt(a, b):
    return lax.dot_general(a, b, (((1,), (1,)), ((), ())), preferred_element_type=F32)


def tn(a, b):
    return lax.dot_general(a, b, (((0,), (0,)), ((), ())), preferred_element_type=F32)


def iota(shape, axis):
    return lax.broadcasted_iota(jnp.int32, shape, axis)


def split_at(values, size):
    if size & (size - 1) == 0:
        return values >> (size.bit_length() - 1), values & (size - 1)
    return lax.div(values, size), lax.rem(values, size)


def flip(index, bit):
    return index + bit - 2 * bit * lax.rem(lax.div(index, bit), 2)


def col_sum(values):
    return jnp.sum(values, axis=0, keepdims=True)


def norm(values):
    centered = values - jnp.mean(values, axis=-1, keepdims=True)
    inv = lax.rsqrt(jnp.mean(centered * centered, axis=-1, keepdims=True) + EPS)
    return centered * inv, inv


def norm_back(grad, normal, inv):
    return inv * (
        grad
        - jnp.mean(grad, axis=-1, keepdims=True)
        - normal * jnp.mean(grad * normal, axis=-1, keepdims=True)
    )


class Plan:
    def __init__(self, micro, rows, width, hidden, segs, n_dp, n_z, fused):
        self.micro, self.rows, self.width, self.hidden = micro, rows, width, hidden
        self.segs, self.n_dp, self.n_z, self.fused = segs, n_dp, n_z, fused
        self.tree = rows * n_z
        self.head = width // HEADS
        self.pair = 2 * self.head
        self.pairs = HEADS // 2
        self.cols = 4 * width + hidden
        self.devices = n_dp * n_z
        self.part = width // self.devices
        self.part_h = hidden // self.devices


def make_signal(p, r):
    half = p.width // 2
    freq = jnp.exp((-math.log(10000.0) / half) * iota((1, half), 1).astype(F32))
    far = (iota((8, 1), 0) * p.rows).astype(F32) * freq
    r.far[:, 0:half] = jnp.sin(far)
    r.far[:, half:] = jnp.cos(far)
    step = 32

    @pl.loop(0, p.rows // step)
    def _(i):
        near = (iota((step, 1), 0) + i * step).astype(F32) * freq
        at = pl.ds(pl.multiple_of(i * step, step), step)
        r.near[at, 0:half] = jnp.sin(near)
        r.near[at, half:] = jnp.cos(near)


def signal(p, r, b):
    half = p.width // 2
    far_sin, far_cos = r.far[pl.ds(b, 1), 0:half], r.far[pl.ds(b, 1), half:]
    near_sin, near_cos = r.near[:, 0:half], r.near[:, half:]
    return near_sin * far_cos + near_cos * far_sin, near_cos * far_cos - near_sin * far_sin


def blocked_table(p, parent_row):
    size = 128
    up = jnp.where(
        iota((16, p.segs), 0) == parent_row, 1.0, 0.0
    )
    up = jnp.concatenate([up, jnp.zeros((16, size - p.segs), F32)], axis=1)
    up = jnp.concatenate([up, jnp.zeros((size - 16, size), F32)], axis=0)
    row, column = iota((size, size), 0), iota((size, size), 1)
    reach = jnp.where(row == column, 1.0, up)
    for _ in range(4):
        reach = jnp.minimum(nn(reach.astype(BF16), reach.astype(BF16)), 1.0)
    inside = (row < p.segs) & (column < p.segs)
    return jnp.where(inside & (reach < 0.5), -BIG, 0.0)


def prepare_micro(p, m, z, r):
    table = blocked_table(p, r.parent[m])
    seg_row = r.seg[pl.ds(m, 1), :]
    hot = jnp.where(iota((128, p.tree), 0) == seg_row, 1.0, 0.0)
    r.kfull[:, 128:256] = hot.T.astype(BF16)
    own = pl.ds(pl.multiple_of(z * p.rows, p.rows), p.rows)
    hot = jnp.where(iota((128, p.rows), 0) == r.seg[pl.ds(m, 1), own], 1.0, 0.0)
    feature = nn(table.astype(BF16), hot.astype(BF16)).astype(BF16)
    r.qfull[128:256, 0 : p.rows] = feature
    r.qfull[128:256, p.rows : 2 * p.rows] = feature
    for b in range(p.n_z):
        at = slice(b * p.rows, (b + 1) * p.rows)
        for k, wave in enumerate(signal(p, r, b)):
            lanes = slice(k * (p.width // 2), (k + 1) * (p.width // 2))
            r.h[at, lanes] = (r.states[m, b, :, lanes].astype(F32) + wave).astype(BF16)

    w = p.width
    half = p.tree // 2
    for c in range(2):
        at = slice(c * half, (c + 1) * half)
        r.k[at, :] = nn(r.h[at, :], r.wa[:, w : 2 * w]).astype(BF16)
        r.v[at, :] = nn(r.h[at, :], r.wa[:, 2 * w : 3 * w]).astype(BF16)
    r.vt[...] = r.v[...].T
    q = nn(r.h[own, :], r.wa[:, 0:w]) * (LOG2E * p.head**-0.5)
    r.qt[...] = q.astype(BF16).T


def fill_pair(p, full, flat, i):
    low = pl.ds(pl.multiple_of(i * p.pair, p.pair), p.head)
    high = pl.ds(pl.multiple_of(i * p.pair + p.head, p.head), p.head)
    full[0 : p.head, 0 : p.rows] = flat[low, :].astype(BF16)
    full[p.head : p.pair, p.rows : 2 * p.rows] = flat[high, :].astype(BF16)


def attention_forward(p, r):
    step = p.tree // 8

    def ready(i):
        r.kfull[:, 0:128] = r.k[:, pl.ds(pl.multiple_of(i * p.pair, p.pair), p.pair)]
        fill_pair(p, r.qfull, r.qt, i)

    def scores(c, top):
        at = slice(c * step, (c + 1) * step)
        s = nn(r.kfull[at, :], r.qfull[...])
        r.s[at, :] = s
        own = jnp.max(s.reshape(step // 8, 8, 2 * p.rows), axis=0)
        return own if top is None else jnp.maximum(top, own)

    def soften(i, c, top):
        at = slice(c * step, (c + 1) * step)
        r.e[i, at, :] = jnp.exp2(r.s[at, :] - top).astype(BF16)

    def finish(i):
        lanes = pl.ds(pl.multiple_of(i * p.pair, p.pair), p.pair)
        r.vo[0:128, :] = r.vt[lanes, :]
        o = nn(r.vo[...], r.e[i])
        inv = 1.0 / o[128:136]
        r.inv[i] = inv
        low = pl.ds(pl.multiple_of(i * p.pair, p.pair), p.head)
        high = pl.ds(pl.multiple_of(i * p.pair + p.head, p.head), p.head)
        r.ot[low, :] = o[0 : p.head, 0 : p.rows] * inv[0:1, 0 : p.rows]
        r.ot[high, :] = o[p.head : p.pair, p.rows :] * inv[0:1, p.rows :]

    ready(0)
    top = None
    for c in range(8):
        top = scores(c, top)
    r.top[...] = top

    @pl.loop(0, p.pairs - 1)
    def _(i):
        ready(i + 1)
        top = jnp.max(r.top[...], axis=0, keepdims=True)
        later = None
        for c in range(8):
            soften(i, c, top)
            later = scores(c, later)
        r.top[...] = later
        finish(i)

    top = jnp.max(r.top[...], axis=0, keepdims=True)
    for c in range(8):
        soften(p.pairs - 1, c, top)
    finish(p.pairs - 1)


def transition(p, m, z, r, between, down_done, up_done):
    w = p.width
    rows = p.rows
    vec = lambda k: r.vec[k : k + 1, :]
    gain_a, bias_a, gain_b, bias_b, halt_vec = vec(1), vec(2), vec(3), vec(4), vec(5)
    w_out = slice(3 * w, 4 * w)

    lane = iota((128, rows), 0)
    packed = jnp.where(
        lane == 0,
        r.halting[pl.ds(m, 1), :],
        jnp.where(lane == 1, r.ponder[pl.ds(m, 1), :], r.cot_halt[pl.ds(m, 1), :]),
    ).T
    halting, ponder, cot_halt = packed[:, 0:1], packed[:, 1:2], packed[:, 2:3]

    r.otb[...] = r.ot[...].astype(BF16)
    state = r.states[m, z].astype(F32)
    y1 = state + jnp.concatenate(signal(p, r, z), axis=1) + tn(r.otb[...], r.wa[:, w_out])
    xh1, inv1 = norm(y1)
    n1 = xh1 * gain_a + bias_a
    r.xh1[...] = xh1
    r.u[...] = n1.astype(BF16)
    r.acc[...] = n1

    wide = w // 2
    count = p.hidden // wide

    def expand(c):
        r.pre[c % 2] = (
            nn(r.u[...], r.wa[:, 4 * w + c * wide : 4 * w + (c + 1) * wide])
            + r.bup[:, c * wide : (c + 1) * wide]
        )

    def bend(c):
        block = slice((c // 2) * rows, (c // 2 + 1) * rows)
        off = (c % 2) * wide
        pre = r.pre[c % 2]
        square = pre * pre
        t = jnp.tanh(pre * (GELU_C + (GELU_C * GELU_A) * square))
        half = 0.5 + 0.5 * t
        r.dkv[block, off : off + wide] = (pre * half).astype(BF16)
        slope = half + (0.5 * pre) * (1.0 - t * t) * (
            GELU_C + (3.0 * GELU_A * GELU_C) * square
        )
        r.dkv[block, w + off : w + off + wide] = slope.astype(BF16)

    def shrink(c):
        block = slice((c // 2) * rows, (c // 2 + 1) * rows)
        off = (c % 2) * wide
        r.acc[...] += nn(
            r.dkv[block, off : off + wide], r.wd[c * wide : (c + 1) * wide, :]
        )

    expand(0)
    for c in range(count):
        if c + 1 < count:
            expand(c + 1)
        bend(c)
        if c:
            shrink(c - 1)
    shrink(count - 1)

    between()
    y2 = r.acc[...] + vec(0)
    xh2, inv2 = norm(y2)
    s2 = xh2 * gain_b + bias_b
    ph = jax.nn.sigmoid(jnp.sum(s2 * halt_vec, axis=1, keepdims=True))
    run = jnp.where(halting < HALT_LIMIT, 1.0, 0.0)
    room = run * (1.0 - halting)
    weight = room * ph
    state = r.states[m, z].astype(F32)
    r.new_state[m] = (weight * s2 + (1.0 - weight) * state).astype(BF16)
    lane = iota((rows, 128), 1)
    packed = jnp.where(
        lane == 0, halting + weight, ponder + run * (1.0 - weight)
    ).T
    r.new_halting[pl.ds(m, 1), :] = packed[0:1, :]
    r.new_ponder[pl.ds(m, 1), :] = packed[1:2, :]

    cot = r.cot[m].astype(F32)
    dw = jnp.sum(cot * (s2 - state), axis=1, keepdims=True) + cot_halt
    dl = dw * room * ph * (1.0 - ph)
    ds2 = weight * cot + dl * halt_vec
    r.gvec[5:6, :] += col_sum(dl * s2)
    r.gvec[3:4, :] += col_sum(ds2 * xh2)
    r.gvec[4:5, :] += col_sum(ds2)
    dy2 = norm_back(ds2 * gain_b, xh2, inv2)
    r.gvec[0:1, :] += col_sum(dy2)
    r.dg[...] = dy2.astype(BF16)
    r.acc[...] = dy2
    r.gstate[m] = (1.0 - weight) * cot

    for j in range(p.hidden // w):
        at = slice(j * w, (j + 1) * w)
        block = slice(j * rows, (j + 1) * rows)
        r.gd[at, :] += tn(r.dkv[block, 0:w], r.dg[...])
        down_done(j)
    for j in range(p.hidden // w):
        at = slice(j * w, (j + 1) * w)
        at_up = slice((4 + j) * w, (5 + j) * w)
        block = slice(j * rows, (j + 1) * rows)
        dz = nt(r.dg[...], r.wd[at, :]) * r.dkv[block, w : 2 * w].astype(F32)
        r.gbup[:, at] += col_sum(dz)
        dzb = dz.astype(BF16)
        r.acc[...] += nt(dzb, r.wa[:, at_up])
        r.ga[:, at_up] += tn(r.u[...], dzb)
        up_done(j)

    dn1 = r.acc[...]
    xh1 = r.xh1[...]
    r.gvec[1:2, :] += col_sum(dn1 * xh1)
    r.gvec[2:3, :] += col_sum(dn1)
    dy1 = norm_back(dn1 * gain_a, xh1, inv1)
    r.gstate[m] += dy1
    da = dy1.astype(BF16)
    r.ga[:, w_out] += nn(r.otb[...], da)
    r.dot[...] = nt(r.wa[:, w_out], da)


def attention_backward(p, m, z, r, back, inside):
    w = p.width
    size = p.tree // 2

    @pl.when(m >= 2)
    def _():
        back.left(m - 2)

    def ready(i):
        low = slice(i * p.pair, i * p.pair + p.head)
        high = slice(i * p.pair + p.head, (i + 1) * p.pair)
        inv = r.inv[i]
        full, q = r.dofull.at[i], r.qpair.at[i]
        do_a = (r.dot[low, :] * inv[0:1, 0 : p.rows]).astype(BF16)
        do_b = (r.dot[high, :] * inv[0:1, p.rows :]).astype(BF16)
        full[0 : p.head, 0 : p.rows] = do_a
        full[p.head : p.pair, p.rows :] = do_b
        inner = jnp.concatenate(
            [
                col_sum(do_a.astype(F32) * r.ot[low, :]),
                col_sum(do_b.astype(F32) * r.ot[high, :]),
            ],
            axis=1,
        )
        rough = (-inner).astype(BF16).astype(F32)
        row = iota((16, 2 * p.rows), 0)
        full[128:144, :] = jnp.where(
            row == 0, rough, jnp.where(row == 1, -inner - rough, 0.0)
        ).astype(BF16)
        q[0 : p.head, 0 : p.rows] = r.qt[low, :]
        q[p.head : p.pair, p.rows :] = r.qt[high, :]

    side = lax.div(z, p.n_z // 2)
    ready(0)
    for c in range(2):
        half = side if c else 1 - side
        at = pl.ds(pl.multiple_of(half * size, size), size)
        for i in range(p.pairs):
            inside(c * p.pairs + i)
            lanes = slice(i * p.pair, (i + 1) * p.pair)
            lanes_v = slice(w + i * p.pair, w + (i + 1) * p.pair)
            r.vfull[at, 0:128] = r.v[at, lanes]
            dp = nn(r.vfull[at, :], r.dofull[i])
            if c == 0 and i + 1 < p.pairs:
                ready(i + 1)
            e = r.e[i, at, :]
            ds = (e.astype(F32) * dp).astype(BF16)
            r.ds[...] = ds
            r.dkv[at, lanes] = (nt(ds, r.qpair[i]) * LN2).astype(BF16)
            r.dkv[at, lanes_v] = nt(e, r.dofull[i, 0:128, :]).astype(BF16)
            dq = nn(r.vt[lanes, at], r.ds[...]) * (p.head**-0.5)
            low = slice(i * p.pair, i * p.pair + p.head)
            high = slice(i * p.pair + p.head, (i + 1) * p.pair)
            if c == 0:
                r.dqt[low, :] = dq[0 : p.head, 0 : p.rows].astype(BF16)
                r.dqt[high, :] = dq[p.head : p.pair, p.rows :].astype(BF16)
            else:
                one = r.dqt[low, :].astype(F32) + dq[0 : p.head, 0 : p.rows]
                two = r.dqt[high, :].astype(F32) + dq[p.head : p.pair, p.rows :]
                r.dqt[low, :] = one.astype(BF16)
                r.dqt[high, :] = two.astype(BF16)
        for k in range(p.n_z // 2):
            b = half * (p.n_z // 2) + k
            mine = pl.ds(pl.multiple_of(b * p.rows, p.rows), p.rows)
            dh = nt(r.dkv[mine, :], r.wa[:, w : 3 * w])
            r.dh[lax.rem(m, 2), b] = dh.astype(BF16)
            if c:

                @pl.when(z == b)
                def _():
                    r.gstate[m] += dh

        if c == 0:
            back.step(m, 0)

    r.dq[...] = r.dqt[...].T
    r.gstate[m] += nt(r.dq[...], r.wa[:, 0:w])


def input_gradients(p, z, r):
    w = p.width
    own = pl.ds(pl.multiple_of(z * p.rows, p.rows), p.rows)
    r.ga[:, 0:w] += tn(r.h[own, :], r.dq[...])
    for j in range(2):
        at = slice(j * w, (j + 1) * w)
        to = slice((1 + j) * w, (2 + j) * w)
        r.ga[:, to] += tn(r.h[...], r.dkv[0 : p.tree, at])


def remote(src, dst, send, recv, device):
    return pltpu.make_async_remote_copy(
        src_ref=src,
        dst_ref=dst,
        send_sem=send,
        recv_sem=recv,
        device_id=device,
        device_id_type=MESH,
    )


class Back:
    def __init__(self, p, dp, z, r):
        self.p, self.dp, self.z, self.r = p, dp, z, r
        self.last = p.n_z - 1

    def _copy(self, m, k, way, sender):
        r = self.r
        block = sender + way * (self.last - k)
        slot = block + 1 if way == 1 else block
        line = 0 if way == 1 else 1
        return remote(
            r.dh.at[lax.rem(m, 2), block],
            r.dh_in.at[m, slot],
            r.back_send.at[m, line, k],
            r.back_recv.at[m, line, k],
            (self.dp, sender + way),
        ), block, slot

    def _place(self, way):
        return self.z if way == 1 else self.last - self.z

    def step(self, m, k):
        r = self.r
        for way in (1, -1):
            place = self._place(way)
            if k == self.last:

                @pl.when(place > 0)
                def _():
                    copy, _, slot = self._copy(m, k - 1, way, self.z - way)
                    copy.wait_recv()
                    r.gstate[m] += r.dh_in[m, slot].astype(F32)

                continue

            @pl.when((place <= k) & (place < self.last))
            def _():
                if k:

                    @pl.when(place > 0)
                    def _():
                        copy, block, slot = self._copy(m, k - 1, way, self.z - way)
                        copy.wait_recv()
                        own = r.dh.at[lax.rem(m, 2), block]
                        own[...] = (
                            own[...].astype(F32) + r.dh_in[m, slot].astype(F32)
                        ).astype(BF16)

                self._copy(m, k, way, self.z)[0].start()

    def left(self, m):
        for way in (1, -1):
            place = self._place(way)
            for k in range(self.last):

                @pl.when((place <= k) & (place < self.last))
                def _():
                    self._copy(m, k, way, self.z)[0].wait_send()


class Copy:
    def __init__(self, flow, out, into=None, go=None, come=None):
        self.flow, self.out, self.into = flow, out, into or out
        self.go, self.come = go, come
        self.at = flow.used
        self.open = False
        flow.used += 1
        flow.copies.append(self)

    def _run(self, when, step):
        if when is None:
            step()
        else:
            pl.when(when())(step)

    def _make(self, ends):
        src, dst, device = ends()
        return remote(src, dst, self.flow.send.at[self.at], self.flow.recv.at[self.at], device)

    def start(self):
        self.open = True
        self._run(self.go, lambda: self._make(self.out).start())
        return self

    def arrived(self):
        self._run(self.come, lambda: self._make(self.into).wait_recv())

    def left(self):
        if self.open:
            self._run(self.go, lambda: self._make(self.out).wait_send())
            self.open = False


class Flow:
    def __init__(self, send, recv):
        self.send, self.recv, self.used, self.copies = send, recv, 0, []

    def finish(self):
        for copy in self.copies:
            copy.left()


class Line:
    def __init__(self, p, block, dp, z, flow):
        self.last = p.n_z - 1
        self.steps = []
        for step in range(p.n_z - 1):
            both = []
            for way in (1, -1):
                both.append(self._copy(p, block, dp, z, flow, step, way))
            self.steps.append(both)

    def _copy(self, p, block, dp, z, flow, step, way):
        place = z if way == 1 else self.last - z

        def out():
            at = block(z - way * step)
            return at, at, (dp, z + way)

        def into():
            at = block(z - way * (step + 1))
            return at, at, (dp, z - way)

        return Copy(
            flow,
            out,
            into,
            go=lambda: (place >= step) & (place < self.last),
            come=lambda: place >= step + 1,
        )

    def step(self, k):
        if k:
            for copy in self.steps[k - 1]:
                copy.arrived()
        if k < len(self.steps):
            for copy in self.steps[k]:
                copy.start()


def rows_of(dp, size):
    return pl.ds(pl.multiple_of(dp * size, size), size)


class Spread:
    def __init__(self, p, piece, dp, z, flow, far):
        ref, part, c0, c1 = piece
        size = part * p.n_z // 2
        side = lax.div(z, p.n_z // 2)
        side = 1 - side if far else side
        mid = (c0 + c1) // 2 if c1 - c0 >= 256 else c1
        self.split = mid < c1

        def made(block, turn, a, b):
            mine = ref.at[rows_of(2 * block + side, size), a:b]
            theirs = ref.at[rows_of(2 * flip(block, turn) + side, size), a:b]
            to = (flip(dp, turn), z)
            return Copy(flow, lambda: (mine, mine, to), lambda: (theirs, theirs, to))

        dpx, dpy = flip(dp, 2), flip(dp, 4)
        dpxy = flip(dpx, 4)
        self.first = [made(dp, 2, c0, mid), made(dp, 4, c0, mid), made(dp, 1, c0, c1)]
        self.a3 = made(dpx, 4, c0, mid)
        if self.split:
            self.first += [made(dp, 4, mid, c1), made(dp, 2, mid, c1)]
            self.b3 = made(dpy, 2, mid, c1)
        self.cores = [made(block, 1, c0, c1) for block in (dpx, dpy, dpxy)]

    def start(self):
        for copy in self.first:
            copy.start()

    def middle(self):
        self.first[0].arrived()
        self.a3.start()
        if self.split:
            self.first[3].arrived()
            self.b3.start()
            self.first[4].arrived()
        self.cores[0].start()
        self.first[1].arrived()
        self.cores[1].start()

    def late(self):
        self.a3.arrived()
        if self.split:
            self.b3.arrived()
        self.cores[2].start()

    def end(self):
        self.first[2].arrived()
        for copy in self.cores:
            copy.arrived()


class Reduce:
    def __init__(self, p, g, part, c0, c1, bufs, dp, z, flow, by_rows=False):
        self.p, self.g, self.part, self.c0, self.c1 = p, g, part, c0, c1
        self.dp, self.z, self.by_rows = dp, z, by_rows
        self.size = size = part * p.n_z
        self.cols = cols = c1 - c0
        self.mid = mid = cols // 2 if cols >= 256 else cols
        self.split = mid < cols
        self.s1, self.r1, self.r2, self.r3, self.s4, self.r4 = bufs
        s1, r1, r2, r3, s4, r4 = bufs
        x, y, core = (flip(dp, 2), z), (flip(dp, 4), z), (flip(dp, 1), z)
        dpx, dpy = flip(dp, 2), flip(dp, 4)
        self.order = (dp, dpx, dpy, flip(dpx, 4))

        def made(src, dst, to):
            return Copy(flow, lambda: (src, dst, to))

        if by_rows:
            self.chunks = [
                (slice(k * size, (k + 1) * size), slice(0, cols)) for k in range(4)
            ]
        else:
            wide = min(p.width, cols)
            self.chunks = [
                (slice(0, 4 * size), slice(k * wide, (k + 1) * wide))
                for k in range(cols // wide)
            ]
        self.core = [made(s1.at[at], r1.at[at], core) for at in self.chunks]
        self.a1 = made(s1.at[0 : 2 * size, 0:mid], r2.at[:, 0:mid], x)
        self.a2 = made(s1.at[0:size, 0:mid], r3.at[:, 0:mid], y)
        if self.split:
            self.b1 = made(s1.at[0 : 2 * size, mid:cols], r2.at[:, mid:cols], y)
            self.b2 = made(s1.at[0:size, mid:cols], r3.at[:, mid:cols], x)
        self.zs = []
        for i in range(1, p.n_z):
            peer = lax.rem(z + i, p.n_z)
            self.zs.append(made(s4.at[i - 1, :, 0:cols], r4.at[i - 1, :, 0:cols], (dp, peer)))

    def _sum(self, block, a, b, got=(), sub=None):
        first, count = (0, self.size) if sub is None else (sub * self.part, self.part)

        def at(start):
            return pl.ds(pl.multiple_of(start + first, self.part), count)

        total = self.g[at(block * self.size), self.c0 + a : self.c0 + b]
        for buf, slot in got:
            total = total + buf[at(slot * self.size), a:b].astype(F32)
        return total

    def _first(self, block):
        return self.r1, lax.div(block, 2)

    def _put(self, slot, a, b, total):
        self.s1[rows_of(slot, self.size), a:b] = total.astype(BF16)

    def core_start(self, k):
        _, lanes = self.chunks[k]
        a, b = lanes.start, lanes.stop
        theirs = 1 - lax.rem(self.dp, 2)
        for slot in (k,) if self.by_rows else range(4):
            self._put(slot, a, b, self._sum(2 * slot + theirs, a, b))
        self.core[k].start()

    def core_end(self):
        order, mid, cols = self.order, self.mid, self.cols
        for copy in self.core:
            copy.arrived()
        for copy in self.core:
            copy.left()
        for slot, k in ((0, 1), (1, 3)):
            self._put(slot, 0, mid, self._sum(order[k], 0, mid, [self._first(order[k])]))
        self.a1.start()
        if self.split:
            for slot, k in ((0, 2), (1, 3)):
                one = self._sum(order[k], mid, cols, [self._first(order[k])])
                self._put(slot, mid, cols, one)
            self.b1.start()

    def plane_middle(self):
        order, mid, cols = self.order, self.mid, self.cols
        self.a1.arrived()
        self.a1.left()
        got = [self._first(order[2]), (self.r2, 1)]
        self._put(0, 0, mid, self._sum(order[2], 0, mid, got))
        self.a2.start()
        if self.split:
            self.b1.arrived()
            self.b1.left()
            got = [self._first(order[1]), (self.r2, 1)]
            self._put(0, mid, cols, self._sum(order[1], mid, cols, got))
            self.b2.start()

    def _own(self, place):
        got = [self._first(self.dp), (self.r2, 0), (self.r3, 0)]
        return self._sum(self.dp, 0, self.cols, got, place)

    def plane_end(self):
        self.a2.arrived()
        if self.split:
            self.b2.arrived()
        for i in range(1, self.p.n_z):
            peer = lax.rem(self.z + i, self.p.n_z)
            self.s4[i - 1, :, 0 : self.cols] = self._own(peer).astype(BF16)
            self.zs[i - 1].start()

    def total(self):
        total = self._own(self.z)
        for i in range(1, self.p.n_z):
            self.zs[i - 1].arrived()
            total = total + self.r4[i - 1, :, 0 : self.cols].astype(F32)
        return total


def spread_vectors(p, r):
    r.gs[...] = r.ws[...].astype(F32)

    def spread(k, part, total):
        g = r.gs[pl.ds(k, p.devices, stride=16), :].astype(BF16)
        lane, column = iota((128, total), 0), iota((128, total), 1)
        place = jnp.where(split_at(column, part)[1] == lane, 1.0, 0.0)
        full = nn(g, place.astype(BF16))
        mine = split_at(iota((p.devices, total), 1), part)[0] == iota((p.devices, total), 0)
        return col_sum(jnp.where(mine, full, 0.0))

    for k in range(VECTORS):
        r.vec[k : k + 1, :] = spread(k, p.part, p.width)
    r.bup[...] = spread(VECTORS, p.part_h, p.hidden)


def collect_vectors(p, r):
    r.gs[...] = jnp.zeros(r.gs.shape, F32)

    def collect(k, row, part, total):
        mine = split_at(iota((p.devices, total), 1), part)[0] == iota((p.devices, total), 0)
        full = jnp.where(mine, row, 0.0)
        high = full.astype(BF16)
        rest = (full - high.astype(F32)).astype(BF16)
        lane, column = iota((128, total), 0), iota((128, total), 1)
        place = jnp.where(split_at(column, part)[1] == lane, 1.0, 0.0).astype(BF16)
        r.gs[pl.ds(k, p.devices, stride=16), :] = nt(high, place) + nt(rest, place)

    for k in range(VECTORS):
        collect(k, r.gvec[k : k + 1, :], p.part, p.width)
    collect(VECTORS, r.gbup[...], p.part_h, p.hidden)


class Refs:
    pass


def buffers(r, tag):
    return [getattr(r, tag + str(k)) for k in range(6) if hasattr(r, tag + str(k))]


def targets(p, n, z, r):
    w = p.width
    at = rows_of(n, p.part)
    places = {}
    if p.fused:
        places["w_query"] = r.wa.at[at, 0:w]
        places["w_key"] = r.wa.at[at, w : 2 * w]
        places["w_value"] = r.wa.at[at, 2 * w : 3 * w]
        places["w_out"] = r.wa.at[at, 3 * w : 4 * w]
        places["w_up"] = r.wa.at[at, 4 * w :]
        places["w_down"] = r.wd.at[rows_of(n, p.part_h), :]
    places["state"] = r.states.at[:, z]
    return places


def place_vectors(p, n, r):
    r.small[...] = jnp.zeros((16, 128), F32)
    for k, name in enumerate(SMALL):
        r.small[k : k + 1, 0 : p.part] = getattr(r, name)[...].astype(F32)
    r.small[VECTORS : VECTORS + 1, 0 : p.part_h] = r.b_up[...].astype(F32)
    r.ws[rows_of(n, 16), :] = r.small[...].astype(BF16)


def clear(p, r):
    r.ga[...] = jnp.zeros(r.ga.shape, F32)
    r.gd[...] = jnp.zeros(r.gd.shape, F32)
    r.gvec[...] = jnp.zeros(r.gvec.shape, F32)
    r.gbup[...] = jnp.zeros(r.gbup.shape, F32)
    r.qfull[...] = jnp.zeros(r.qfull.shape, BF16)
    r.dofull[...] = jnp.zeros(r.dofull.shape, BF16)
    r.qpair[...] = jnp.zeros(r.qpair.shape, BF16)
    r.vo[128:144, :] = jnp.ones((16, p.tree), BF16)
    lane = iota((p.tree, 128), 1)
    r.vfull[:, 128:256] = jnp.where(lane < 2, 1.0, 0.0).astype(BF16)


def kernel(p, names, given, results, *refs):
    r = Refs()
    for name, ref in zip(names, refs):
        setattr(r, name, ref)
    dp = lax.axis_index("dp")
    z = lax.axis_index("fsdp")
    w = p.width
    places = targets(p, dp * p.n_z + z, z, r)
    loads = {}
    for k, name in enumerate(given):
        place = places.get(name, getattr(r, name, None))
        copy = pltpu.make_async_copy(getattr(r, "hbm_" + name), place, r.load_sem.at[k])
        loads[name] = copy
    stores = {}
    for k, name in enumerate(results):
        if name == "new_state":
            continue
        stores[name] = pltpu.make_async_copy(
            getattr(r, name), getattr(r, "hbm_" + name), r.store_sem.at[k]
        )
    flow = Flow(r.send_sem, r.recv_sem)

    barrier = pltpu.get_barrier_semaphore()
    peers = [(dp, lax.rem(z + i, p.n_z)) for i in range(1, p.n_z)]
    if p.fused:
        peers += [(flip(dp, bit), z) for bit in (1, 2, 4)]
    for peer in peers:
        pl.semaphore_signal(barrier, inc=1, device_id=peer, device_id_type=MESH)
    for copy in loads.values():
        copy.start()
    lines = [
        Line(p, lambda b, m=m: r.states.at[m, b], dp, z, flow) for m in range(p.micro)
    ]
    steps = p.n_z - 1
    back = Back(p, dp, z, r)
    if p.fused:
        parts = (
            (r.wa, p.part, 0, 3 * w),
            (r.ws, 16, 0, 128),
            (r.wa, p.part, 3 * w, p.cols),
            (r.wd, p.part_h, 0, w),
        )
        rods = []
        for ref, part, c0, c1 in parts:

            def block(b, ref=ref, part=part, c0=c0, c1=c1):
                return ref.at[rows_of(dp * p.n_z + b, part), c0:c1]

            rods.append(Line(p, block, dp, z, flow))
        spreads, fars = (
            [Spread(p, piece, dp, z, flow, far) for piece in parts] for far in (False, True)
        )
        sums = [
            Reduce(p, r.ga, p.part, 3 * w, p.cols, buffers(r, "f"), dp, z, flow),
            Reduce(p, r.gd, p.part_h, 0, w, buffers(r, "d"), dp, z, flow, by_rows=True),
            Reduce(p, r.gs, 16, 0, 128, buffers(r, "e"), dp, z, flow),
            Reduce(p, r.ga, p.part, 0, 3 * w, [r.q0] + buffers(r, "b"), dp, z, flow),
        ]
    for copy in loads.values():
        copy.wait()
    if p.fused:
        place_vectors(p, dp * p.n_z + z, r)
    pl.semaphore_wait(barrier, len(peers))

    if p.fused:
        for rod in rods:
            rod.step(0)
        make_signal(p, r)
        for rod, spread in zip(rods, spreads):
            rod.step(1)
            spread.start()
        clear(p, r)
        for rod in rods:
            rod.step(2)
        lines[0].step(0)
        for rod, spread, far in zip(rods, spreads, fars):
            rod.step(3)
            spread.middle()
            far.start()
        lines[0].step(1)
        for spread in spreads:
            spread.late()
        fars[0].middle()
        lines[0].step(2)
        if p.micro > 1:
            lines[1].step(0)
        fars[0].late()
        for far in fars[1:]:
            far.middle()
        spreads[0].end()
        fars[0].end()
        lines[0].step(3)
    else:
        for k in range(steps + 1):
            for line in lines:
                line.step(k)
        make_signal(p, r)
        clear(p, r)

    @pl.loop(0, p.micro)
    def _(m):
        if p.fused:
            for k in range(1, p.micro):

                @pl.when(m == k)
                def _(k=k):
                    lines[k].step(steps)

        prepare_micro(p, m, z, r)
        if p.fused:

            @pl.when(m == 0)
            def _():
                for far in fars[1:]:
                    far.late()

        attention_forward(p, r)

        @pl.when(m > 1)
        def _():
            back.step(m - 2, steps)

        if p.fused:

            @pl.when(m == 1)
            def _():
                for line in lines[2:]:
                    for k in range(1, steps - 1):
                        line.step(k)

            @pl.when(m == 0)
            def _():
                if p.micro > 1:
                    for k in range(1, steps - 1):
                        lines[1].step(k)
                for spread in spreads[1:] + fars[1:]:
                    spread.end()
                spread_vectors(p, r)

        def between():
            @pl.when(m > 0)
            def _():
                for k in range(1, steps - 1):
                    back.step(m - 1, k)

        def down_done(j):
            if p.fused:

                @pl.when(m == p.micro - 1)
                def _():
                    sums[1].core_start(j)

        def up_done(j):
            if p.fused:

                @pl.when(m == p.micro - 1)
                def _():
                    sums[0].core_start(1 + j)
                    if j == p.hidden // w - 1:
                        sums[1].core_end()

        transition(p, m, z, r, between, down_done, up_done)

        out = pltpu.make_async_copy(
            r.new_state.at[m], r.hbm_new_state.at[m], r.state_sem.at[m]
        )
        out.start()
        if p.fused and p.micro > 1:

            @pl.when(m == 0)
            def _():
                lines[1].step(steps - 1)
                for line in lines[2:]:
                    line.step(0)

            @pl.when(m == 1)
            def _():
                for line in lines[2:]:
                    line.step(steps - 1)

        r.vt[...] = r.k[...].T
        if p.fused:

            @pl.when(m == p.micro - 1)
            def _():
                sums[0].core_start(0)
                collect_vectors(p, r)
                sums[2].core_start(0)

        def inside(i):
            if i == p.pairs + 1:

                @pl.when(m > 0)
                def _():
                    back.step(m - 1, steps - 1)

            if p.fused and i == 2:

                @pl.when(m == p.micro - 1)
                def _():
                    sums[0].core_end()

            if p.fused and i == p.pairs + 2:

                @pl.when(m == p.micro - 1)
                def _():
                    sums[2].core_end()

        attention_backward(p, m, z, r, back, inside)
        input_gradients(p, z, r)

    if p.fused:
        last = p.micro - 1
        for k in range(3):
            sums[3].core_start(k)
        back.step(last, 1)
        sums[1].plane_middle()
        sums[3].core_end()
        sums[2].plane_middle()
        sums[0].plane_middle()
        sums[1].plane_end()
        sums[3].plane_middle()
        back.step(last, 2)
        sums[2].plane_end()
        sums[0].plane_end()
        sums[3].plane_end()
        back.step(last, 3)
        back.step(last - 1, steps)
        r.g_down[...] = sums[1].total()
        total = sums[0].total()
        r.g_out[...] = total[:, 0:w]
        r.g_up[...] = total[:, w:]
        r.small[...] = sums[2].total()
        for k, name in enumerate(SMALL):
            getattr(r, "g_" + name)[...] = r.small[k : k + 1, 0 : p.part]
        r.g_b_up[...] = r.small[VECTORS : VECTORS + 1, 0 : p.part_h]
        total = sums[3].total()
        r.g_query[...] = total[:, 0:w]
        r.g_key[...] = total[:, w : 2 * w]
        r.g_value[...] = total[:, 2 * w : 3 * w]
    else:
        if p.micro > 1:
            back.step(p.micro - 2, steps)
        for k in range(1, steps + 1):
            back.step(p.micro - 1, k)
    for m in range(max(p.micro - 2, 0), p.micro):
        back.left(m)
    for copy in stores.values():
        copy.start()
    for m in range(p.micro):
        pltpu.make_async_copy(
            r.new_state.at[m], r.hbm_new_state.at[m], r.state_sem.at[m]
        ).wait()
    for copy in stores.values():
        copy.wait()
    flow.finish()
    if flow.used != copy_count(p):
        raise ValueError("copies: %d" % flow.used)


def copy_count(p):
    line = 2 * (p.n_z - 1)
    if not p.fused:
        return p.micro * line
    spreads = 2 * (3 * 10 + 7)
    exchanges = 3 * (4 + p.n_z - 1) + 2 + p.n_z - 1
    chunks = (p.cols // p.width - 3) + 4 + 1 + 3
    return (p.micro + 4) * line + spreads + exchanges + chunks


def run_kernel(p, inputs):
    w, t, rows = p.width, p.tree, p.rows
    outs = {
        "new_state": ((p.micro, rows, w), BF16),
        "new_halting": ((p.micro, rows), F32),
        "new_ponder": ((p.micro, rows), F32),
        "gstate": ((p.micro, rows, w), F32),
    }
    scratch = {}
    if p.fused:
        for name in ("query", "key", "value", "out"):
            outs["g_" + name] = ((p.part, w), F32)
        outs["g_up"] = ((p.part, p.hidden), F32)
        outs["g_down"] = ((p.part_h, w), F32)
        for name in SMALL:
            outs["g_" + name] = ((1, p.part), F32)
        outs["g_b_up"] = ((1, p.part_h), F32)
        scratch.update(
            wa=((w, p.cols), BF16),
            wd=((p.hidden, w), BF16),
            ws=((p.devices * 16, 128), BF16),
            small=((16, 128), F32),
            vec=((8, w), F32),
            bup=((1, p.hidden), F32),
            ga=((w, p.cols), F32),
            gd=((p.hidden, w), F32),
            gs=((p.devices * 16, 128), F32),
            gvec=((8, w), F32),
            gbup=((1, p.hidden), F32),
        )
        kinds = (
            ("f", p.part, p.cols - 3 * w),
            ("b", p.part, 3 * w),
            ("d", p.part_h, w),
            ("e", 16, 128),
        )
        for tag, part, cols in kinds:
            size = part * p.n_z
            shapes = [(k * size, cols) for k in (4, 4, 2, 1)]
            shapes += [(p.n_z - 1, part, cols)] * 2
            for k, shape in enumerate(shapes):
                if k or tag in "fed":
                    scratch[tag + str(k)] = (shape, BF16)
        scratch["q0"] = ((4 * p.part * p.n_z, 3 * w), BF16)
    else:
        outs.update(
            ga=((w, p.cols), F32),
            gd=((p.hidden, w), F32),
            gvec=((8, w), F32),
            gbup=((1, p.hidden), F32),
        )
    scratch.update(
        states=((p.micro, p.n_z, rows, w), BF16),
        near=((rows, w), F32),
        far=((8, w), F32),
        h=((t, w), BF16),
        k=((t, w), BF16),
        v=((t, w), BF16),
        vt=((w, t), BF16),
        qt=((w, rows), BF16),
        kfull=((t, 256), BF16),
        qfull=((256, 2 * rows), BF16),
        vfull=((t, 256), BF16),
        dofull=((p.pairs, 256, 2 * rows), BF16),
        vo=((144, t), BF16),
        e=((p.pairs, t, 2 * rows), BF16),
        s=((t, 2 * rows), F32),
        top=((8, 2 * rows), F32),
        pre=((2, rows, w // 2), F32),
        inv=((p.pairs, 8, 2 * rows), F32),
        ot=((w, rows), F32),
        otb=((w, rows), BF16),
        dot=((w, rows), F32),
        xh1=((rows, w), F32),
        u=((rows, w), BF16),
        acc=((rows, w), F32),
        dg=((rows, w), BF16),
        ds=((t // 2, 2 * rows), BF16),
        dkv=((max(t, rows * (p.hidden // w)), 2 * w), BF16),
        dqt=((w, rows), BF16),
        qpair=((p.pairs, 128, 2 * rows), BF16),
        dq=((rows, w), BF16),
        dh=((2, p.n_z, rows, w), BF16),
        dh_in=((p.micro, p.n_z + 1, rows, w), BF16),
    )
    direct = ("w_query", "w_key", "w_value", "w_out", "w_up", "w_down", "state")
    for name, value in inputs.items():
        if not (name == "state" or (p.fused and name in direct)):
            scratch[name] = (value.shape, value.dtype)
    scratch.update(outs)
    hbm = pl.BlockSpec(memory_space=pl.ANY)
    copies = copy_count(p)
    names = (
        ["hbm_" + name for name in inputs]
        + ["hbm_" + name for name in outs]
        + list(scratch)
        + ["send_sem", "recv_sem", "back_send", "back_recv"]
        + ["load_sem", "store_sem", "state_sem"]
    )
    results = pl.pallas_call(
        functools.partial(kernel, p, names, list(inputs), list(outs)),
        out_shape=[jax.ShapeDtypeStruct(s, d) for s, d in outs.values()],
        in_specs=[hbm] * len(inputs),
        out_specs=[hbm] * len(outs),
        scratch_shapes=[pltpu.VMEM(s, d) for s, d in scratch.values()]
        + [pltpu.SemaphoreType.DMA((copies,))] * 2
        + [pltpu.SemaphoreType.DMA((p.micro, 2, p.n_z - 1))] * 2
        + [
            pltpu.SemaphoreType.DMA((len(inputs),)),
            pltpu.SemaphoreType.DMA((len(outs),)),
            pltpu.SemaphoreType.DMA((p.micro,)),
        ],
        compiler_params=pltpu.CompilerParams(
            collective_id=0, has_side_effects=True, vmem_limit_bytes=127 << 19
        ),
        name="layer",
    )(*inputs.values())
    return dict(zip(outs, results))


def hand_over(values):
    def body(*refs):
        count = len(values)
        held, sems = refs[2 * count : 3 * count], refs[3 * count :]
        taken = [
            pltpu.make_async_copy(refs[k], held[k], sems[0].at[k]) for k in range(count)
        ]
        given = [
            pltpu.make_async_copy(held[k], refs[count + k], sems[1].at[k])
            for k in range(count)
        ]
        for copy in taken:
            copy.start()
        for old, new in zip(taken, given):
            old.wait()
            new.start()
        for copy in given:
            copy.wait()

    hbm = pl.BlockSpec(memory_space=pl.ANY)
    moved = pl.pallas_call(
        body,
        out_shape=[jax.ShapeDtypeStruct(v.shape, v.dtype) for v in values.values()],
        in_specs=[hbm] * len(values),
        out_specs=[hbm] * len(values),
        scratch_shapes=[pltpu.VMEM(v.shape, v.dtype) for v in values.values()]
        + [pltpu.SemaphoreType.DMA((len(values),))] * 2,
        name="hand_over",
    )(*values.values())
    return dict(zip(values, moved))


WEIGHTS = (
    "w_query",
    "w_key",
    "w_value",
    "w_out",
    "w_up",
    "b_up",
    "w_down",
    "b_down",
    "gain_one",
    "bias_one",
    "gain_two",
    "bias_two",
    "w_halt",
)


def per_device(state, segment, parent, halting, ponder, cot_state, cot_halt, *weights):
    micro, rows, width = state.shape
    given = dict(zip(WEIGHTS, weights))
    n_dp, n_z = lax.axis_size("dp"), lax.axis_size("fsdp")
    part, hidden = given["w_query"].shape[0], given["w_up"].shape[1]
    fused = n_dp == 8 and n_z == 4 and part % 16 == 0 and part <= 128
    p = Plan(micro, rows, width, hidden, parent.shape[2], n_dp, n_z, fused)
    inputs = dict(
        state=state,
        seg=segment,
        parent=parent,
        halting=halting,
        ponder=ponder,
        cot=cot_state,
        cot_halt=cot_halt,
    )
    if fused:
        for name, value in given.items():
            inputs[name] = value if value.ndim == 2 else value.reshape(1, -1)
        out = hand_over(run_kernel(p, inputs))
        grads = []
        for name in WEIGHTS:
            value = out["g_" + name[2:]] if name.startswith("w_") and name != "w_halt" else out["g_" + name]
            grads.append(value.reshape(given[name].shape))
    else:
        axes = ("dp", "fsdp")
        full = {k: lax.all_gather(v, axes, axis=0, tiled=True) for k, v in given.items()}
        inputs["wa"] = jnp.concatenate([full[k] for k in WEIGHTS[:5]], axis=1)
        inputs["wd"] = full["w_down"]
        rows_f32 = [full[k].astype(F32) for k in WEIGHTS[7:]]
        rows_f32 += [jnp.zeros((width,), F32)] * 2
        inputs["vec"] = jnp.stack(rows_f32)
        inputs["bup"] = full["b_up"].astype(F32).reshape(1, -1)
        out = run_kernel(p, inputs)
        whole = [out["ga"][:, k * width : (k + 1) * width] for k in range(4)]
        whole += [out["ga"][:, 4 * width :], out["gbup"][0], out["gd"]]
        whole += [out["gvec"][k] for k in range(VECTORS)]
        grads = [
            lax.psum_scatter(g, axes, scatter_dimension=0, tiled=True) for g in whole
        ]
    return (out["new_state"], out["new_halting"], out["new_ponder"], out["gstate"], *grads)


def solution(mesh):
    tokens, flags = P(None, ("dp", "fsdp"), None), P(None, ("dp", "fsdp"))
    matrix, vector = P(("dp", "fsdp"), None), P(("dp", "fsdp"))
    weights = tuple(
        matrix if name in ("w_query", "w_key", "w_value", "w_out", "w_up", "w_down") else vector
        for name in WEIGHTS
    )
    return jax.shard_map(
        per_device,
        mesh=mesh,
        in_specs=(tokens, P(None, "dp"), P(None, "dp", None), flags, flags, tokens, flags)
        + weights,
        out_specs=(tokens, flags, flags, tokens) + weights,
        check_vma=False,
    )
```
